32 devices in a mesh: dp: 16 (over z, x, core), head: 2 (over y).
Axes of the slice: x: 2, y: 2, z: 4, core: 2. Of those that a mesh axis runs over, the one named last changes fastest.
Arguments:
- tokens: bfloat16 [16384, 768], P('dp'), may hold values from -6 to 6
- boxes: int32 [4, 16384], P(None, 'dp'), may hold values from 0 to 611
- resolution: int32 [32], P('dp'), may hold values from 0 to 3
- w_query: bfloat16 [768, 768], P(None, 'head'), may hold values from -0.21875 to 0.21875
- bias_query: bfloat16 [768], P('head'), may hold values from -3 to 3
- w_key: bfloat16 [768, 768], P(None, 'head'), may hold values from -0.21875 to 0.21875
- w_value: bfloat16 [768, 768], P(None, 'head'), may hold values from -0.21875 to 0.21875
- bias_value: bfloat16 [768], P('head'), may hold values from -3 to 3
- w_box: bfloat16 [768, 768], P(None, 'head'), may hold values from -0.21875 to 0.21875
- w_out: bfloat16 [768, 768], P('head'), may hold values from -1.25 to 1.25
- bias_out: bfloat16 [768], replicated, may hold values from -3 to 3
- norm1_gain: bfloat16 [768], replicated, may hold values from 0.25 to 1.75
- norm1_bias: bfloat16 [768], replicated, may hold values from -2 to 2
- w_in: bfloat16 [768, 3072], P(None, 'head'), may hold values from -0.21875 to 0.21875
- bias_in: bfloat16 [3072], P('head'), may hold values from -3 to 3
- w_back: bfloat16 [3072, 768], P('head'), may hold values from -0.109375 to 0.109375
- bias_back: bfloat16 [768], replicated, may hold values from -3 to 3
- norm2_gain: bfloat16 [768], replicated, may hold values from 0.25 to 1.75
- norm2_bias: bfloat16 [768], replicated, may hold values from -2 to 2
- grad_out: bfloat16 [16384, 768], P('dp'), may hold values from -18 to 18
Outputs:
- output: bfloat16 [16384, 768], P('dp')
- grad_input: float32 [16384, 768], P('dp')
- grad_w_query: float32 [768, 768], P('dp', 'head')
- grad_bias_query: float32 [768], P('head')
- grad_w_key: float32 [768, 768], P('dp', 'head')
- grad_w_value: float32 [768, 768], P('dp', 'head')
- grad_bias_value: float32 [768], P('head')
- grad_w_box: float32 [768, 768], P('dp', 'head')
- grad_w_out: float32 [768, 768], P('head', 'dp')
- grad_bias_out: float32 [768], replicated
- grad_norm1_gain: float32 [768], replicated
- grad_norm1_bias: float32 [768], replicated
- grad_w_in: float32 [768, 3072], P('dp', 'head')
- grad_bias_in: float32 [3072], P('head')
- grad_w_back: float32 [3072, 768], P('head', 'dp')
- grad_bias_back: float32 [768], replicated
- grad_norm2_gain: float32 [768], replicated
- grad_norm2_bias: float32 [768], replicated
The draws below stay inside these ranges and needn't reach their ends.
All inputs are finite; a program needn't handle non-finite values.
Results may differ from the reference program's by a relative error of at most 0.02.
Values may be sent and summed in bfloat16 or wider, within the bound.
No kernel may reach another device: no remote copies, remote signals or barrier semaphores. Data moves between devices by JAX's collectives and lax.ppermute only.
A program may use at most 192 MiB of HBM per device.

```python
import math
import jax
import jax.numpy as jnp
from jax import lax

D = 768
HEADS = 12
HEAD = 64
FF = 3072
E = 768
PAGE = 512
PAGES = 32
TOKENS = 16384


def draw_grad_out(key, part):
    scale_key, value_key = jax.random.split(key)
    scales = jnp.exp(jax.random.uniform(scale_key, (PAGES, 1, 1), jnp.float32, math.log(0.3), math.log(3.0)))
    values = jnp.clip(jax.random.normal(value_key, (PAGES, PAGE, D), jnp.float32), -6.0, 6.0)
    return (values * scales).reshape(TOKENS, D).astype(jnp.bfloat16)


def place_ends(values, rng, least, top_value):
    longest = values.shape.index(max(values.shape))
    spots = []
    for shift in (0, 1):
        where = [jax.random.randint(jax.random.fold_in(rng, axis), (), 0, length) for axis, length in enumerate(values.shape)]
        where[longest] = (where[longest] + shift) % values.shape[longest]
        spots.append(tuple(where))
    return values.at[spots[0]].set(least).at[spots[1]].set(top_value)


def levels(key, shape, shards, low, top_value):
    loudness = 1.0
    for dim, blocks in shards:
        draws = jax.random.uniform(jax.random.fold_in(jax.random.fold_in(key, 6), dim), (blocks,), jnp.float32, low / len(shards), top_value / len(shards))
        loudness = loudness * jnp.repeat(jnp.exp(draws), shape[dim] // blocks).reshape((-1,) + (1,) * (len(shape) - 1 - dim))
    return loudness


def noise(rng, extent, spread, bound, cuts=(), kind=jnp.bfloat16):
    drawn = spread * jax.random.normal(rng, extent, jnp.float32)
    if cuts:
        drawn = drawn * levels(rng, extent, cuts, -0.22, 0.18)
    return jnp.clip(drawn, -bound, bound).astype(kind)


def setup_inputs(seed: int = 0) -> dict:
    arg_keys = jax.random.split(jax.random.key(seed), 21)
    return {
        "tokens": noise(arg_keys[0], (TOKENS, D), 1.0, 6.0, ((0, 16),)),
        "boxes": place_ends(jax.random.randint(arg_keys[1], (4, TOKENS), 0, 612), jax.random.fold_in(arg_keys[1], 1), 0, 611).astype(jnp.int32),
        "resolution": place_ends(jax.random.randint(arg_keys[2], (PAGES,), 0, 4), jax.random.fold_in(arg_keys[2], 1), 0, 3).astype(jnp.int32),
        "w_query": noise(arg_keys[3], (D, D), D ** -0.5, 0.21875, ((1, 2),)),
        "bias_query": noise(arg_keys[4], (D,), 0.5, 3.0, ((0, 2),)),
        "w_key": noise(arg_keys[5], (D, D), D ** -0.5, 0.21875, ((1, 2),)),
        "w_value": noise(arg_keys[6], (D, D), D ** -0.5, 0.21875, ((1, 2),)),
        "bias_value": noise(arg_keys[7], (D,), 0.5, 3.0, ((0, 2),)),
        "w_box": noise(arg_keys[8], (E, D), D ** -0.5, 0.21875, ((1, 2),)),
        "w_out": noise(arg_keys[9], (D, D), (D // 32) ** -0.5, 1.25, ((0, 2),)),
        "bias_out": noise(arg_keys[10], (D,), 0.5, 3.0),
        "norm1_gain": jnp.clip(1.0 + 0.15 * jax.random.normal(arg_keys[11], (D,), jnp.float32), 0.25, 1.75).astype(jnp.bfloat16),
        "norm1_bias": noise(arg_keys[12], (D,), 0.3, 2.0),
        "w_in": noise(arg_keys[13], (D, FF), D ** -0.5, 0.21875, ((1, 2),)),
        "bias_in": noise(arg_keys[14], (FF,), 0.5, 3.0, ((0, 2),)),
        "w_back": noise(arg_keys[15], (FF, D), FF ** -0.5, 0.109375, ((0, 2),)),
        "bias_back": noise(arg_keys[16], (D,), 0.5, 3.0),
        "norm2_gain": jnp.clip(1.0 + 0.15 * jax.random.normal(arg_keys[17], (D,), jnp.float32), 0.25, 1.75).astype(jnp.bfloat16),
        "norm2_bias": noise(arg_keys[18], (D,), 0.3, 2.0),
        "grad_out": draw_grad_out(jax.random.fold_in(arg_keys[20], 71), 0),
    }


@jax.custom_vjp
def lower_precision(v):
    return lax.optimization_barrier(v.astype(jnp.bfloat16)).astype(jnp.float32)

@jax.custom_vjp
def low_back(v):
    return v

def low_keep(v):
    return (lower_precision(v), None)

def low_pass(kept, grad):
    return (grad,)

def back_keep(v):
    return (v, None)

def back_low(kept, grad):
    return (lower_precision(grad),)
lower_precision.defvjp(low_keep, low_pass)
low_back.defvjp(back_keep, back_low)

def matmul(left_side, right_side):
    return jnp.dot(left_side, right_side, precision=lax.Precision.HIGHEST, preferred_element_type=jnp.float32)

def swap_halves(values):
    old_shape = values.shape
    split = values.reshape(old_shape[:-1] + (2, 2, old_shape[-1] // 4))
    return split[..., ::-1, :].reshape(old_shape)

def layer_norm(hidden, norm_gain, norm_shift):
    centred = hidden - lax.optimization_barrier(jnp.mean(hidden, axis=-1, keepdims=True))
    variance = lax.optimization_barrier(jnp.mean(centred * centred, axis=-1, keepdims=True))
    return centred * lax.rsqrt(variance + 1e-05) * norm_gain + norm_shift

def box_tables(boxes, resolution, length):
    widths = (612 + 204 * resolution).astype(jnp.float32)
    heights = (792 + 264 * resolution).astype(jnp.float32)
    total = boxes.shape[1]
    across = jnp.repeat(widths, length, total_repeat_length=total)
    downward = jnp.repeat(heights, length, total_repeat_length=total)
    centre_x = (boxes[0] + boxes[2]).astype(jnp.float32) * 500.0 / across
    centre_y = (boxes[1] + boxes[3]).astype(jnp.float32) * 500.0 / downward
    quarter = E // 4
    freqs = jnp.exp(jnp.arange(quarter).astype(jnp.float32) * (-math.log(10000.0) / quarter))
    angle_x = centre_x[:, None] * freqs[None, :]
    angle_y = centre_y[:, None] * freqs[None, :]
    sin_x, cos_x = (jnp.sin(angle_x), jnp.cos(angle_x))
    sin_y, cos_y = (jnp.sin(angle_y), jnp.cos(angle_y))
    sine_part = jnp.concatenate([sin_x, sin_x, sin_y, sin_y], axis=1)
    cosine_part = jnp.concatenate([cos_x, -cos_x, cos_y, -cos_y], axis=1)
    key_codes = jnp.concatenate([cos_x, sin_x, cos_y, sin_y], axis=1)
    return (sine_part, cosine_part, key_codes)

def page_attention(page_item, box_heads):
    query_matrix, key_matrix, value_matrix, sine_part, cosine_part, key_codes = page_item
    highest_precision = lax.Precision.HIGHEST
    offsets = low_back(jnp.einsum('lhd,ehd->hle', query_matrix, box_heads, precision=highest_precision))
    mixed = low_back(lower_precision(offsets * sine_part + swap_halves(offsets) * cosine_part))
    codes = lower_precision(key_codes)
    direct_path = jnp.einsum('bps,vps->pbv', query_matrix, key_matrix, precision=highest_precision)
    boxed = jnp.einsum('hle,me->hlm', mixed, codes, precision=highest_precision)
    scores = low_back((direct_path + boxed) * 0.125)
    attention_probabilities = jax.nn.softmax(scores, axis=-1)
    context_output = jnp.einsum('fiy,yfr->ifr', lower_precision(attention_probabilities), value_matrix, precision=highest_precision)
    return low_back(lower_precision(context_output)).reshape(PAGE, D)

def layer_forward(inputs, weights, sine_rows, cosine_rows, code_rows, group_pages):
    w_query, bias_query, w_key, w_value, bias_value, w_box, w_out, bias_out, norm1_gain, norm1_bias, w_in, bias_in, w_back, bias_back, norm2_gain, norm2_bias = weights
    row_count = inputs.shape[0]
    query_matrix = low_back(lower_precision(matmul(inputs, w_query) + bias_query))
    key_matrix = low_back(lower_precision(matmul(inputs, w_key)))
    value_matrix = low_back(lower_precision(matmul(inputs, w_value) + bias_value))

    def paged_heads(array):
        return array.reshape(group_pages, PAGE, HEADS, HEAD)

    def paged(array):
        return array.reshape(group_pages, PAGE, E)
    box_heads = w_box.reshape(E, HEADS, HEAD)
    page_fn = jax.checkpoint(lambda page_item: page_attention(page_item, box_heads))
    context_output = lax.map(page_fn, (paged_heads(query_matrix), paged_heads(key_matrix), paged_heads(value_matrix), paged(sine_rows), paged(cosine_rows), paged(code_rows)))
    context_output = context_output.reshape(row_count, D)
    attention = low_back(matmul(context_output, w_out))
    first_sum = inputs + attention + bias_out
    normed = layer_norm(first_sum, norm1_gain, norm1_bias)
    pre_act = low_back(matmul(lower_precision(normed), w_in) + bias_in)
    activated = low_back(lower_precision(jax.nn.gelu(pre_act, approximate=False)))
    branch = low_back(matmul(activated, w_back))
    second_sum = normed + branch + bias_back
    return layer_norm(second_sum, norm2_gain, norm2_bias)

def add_grads(running, update):
    return running + update

def reference(tokens, boxes, resolution, w_query, bias_query, w_key, w_value, bias_value, w_box, w_out, bias_out, norm1_gain, norm1_bias, w_in, bias_in, w_back, bias_back, norm2_gain, norm2_bias, grad_out):
    params = tuple((weight_arg.astype(jnp.float32) for weight_arg in (w_query, bias_query, w_key, w_value, bias_value, w_box, w_out, bias_out, norm1_gain, norm1_bias, w_in, bias_in, w_back, bias_back, norm2_gain, norm2_bias)))
    sine_part, cosine_part, key_codes = box_tables(boxes, resolution, PAGE)
    group_pages = math.gcd(PAGES, 8)
    group_rows = group_pages * PAGE
    groups = PAGES // group_pages

    def split_rows(array):
        return array.reshape(groups, group_rows, array.shape[-1])

    def one_group(totals, group_item):
        token_rows, grad_rows, sine_rows, cosine_rows, code_rows = group_item

        def run_layer(inputs, weights):
            return layer_forward(inputs, weights, sine_rows, cosine_rows, code_rows, group_pages)
        outputs, backward = jax.vjp(run_layer, token_rows.astype(jnp.float32), params)
        grad_inputs, grad_weights = backward(grad_rows.astype(jnp.float32))
        totals = jax.tree.map(add_grads, totals, grad_weights)
        return (totals, (outputs.astype(jnp.bfloat16), grad_inputs))
    zero_grads = jax.tree.map(jnp.zeros_like, params)
    totals, (outputs, grad_inputs) = lax.scan(one_group, zero_grads, (split_rows(tokens), split_rows(grad_out), split_rows(sine_part), split_rows(cosine_part), split_rows(key_codes)))
    return (outputs.reshape(TOKENS, D), grad_inputs.reshape(TOKENS, D), totals[0], totals[1], totals[2], totals[3], totals[4], totals[5], totals[6], totals[7], totals[8], totals[9], totals[10], totals[11], totals[12], totals[13], totals[14], totals[15])
```

```python
from functools import partial
import math

import jax
import jax.numpy as jnp
from jax import lax
from jax.experimental import pallas as pl
from jax.experimental.pallas import tpu as pltpu
from jax.sharding import PartitionSpec as P

HEAD = 64
F32 = jnp.float32
BF16 = jnp.bfloat16
VMEM_LIMIT = 58 * 1024 * 1024


def mm(a, b):
    return jnp.dot(a, b, preferred_element_type=F32)


def mm_nt(a, b):
    return lax.dot_general(a, b, (((1,), (1,)), ((), ())), preferred_element_type=F32)


def params(steps):
    return pltpu.CompilerParams(
        dimension_semantics=("arbitrary",) * steps, vmem_limit_bytes=VMEM_LIMIT
    )


def cost(flops, nbytes, trans=0):
    return pl.CostEstimate(flops=int(flops), bytes_accessed=int(nbytes), transcendentals=int(trans))


def sin_cos(angle):
    turns = jnp.floor(angle * (2.0 / math.pi) + 0.5)
    r = angle - turns * 1.5703125
    r = r - turns * 4.837512969970703125e-4
    r = r - turns * 7.54978995489188216e-8
    r2 = r * r
    s = r + r * r2 * (
        -1.6666654611e-1 + r2 * (8.3321608736e-3 + r2 * -1.9515295891e-4)
    )
    c = 1.0 - 0.5 * r2 + r2 * r2 * (
        4.166664568298827e-2 + r2 * (-1.388731625493765e-3 + r2 * 2.443315711809948e-5)
    )
    quad = turns.astype(jnp.int32)
    odd = (quad & 1) == 1
    sine = jnp.where(odd, c, s)
    cosine = jnp.where(odd, s, c)
    sine = jnp.where((quad & 2) == 2, -sine, sine)
    cosine = jnp.where(((quad + 1) & 2) == 2, -cosine, cosine)
    return sine, cosine


def lane_mask(shape, which):
    lanes = lax.broadcasted_iota(jnp.int32, shape, 1)
    return (lanes < HEAD) if which == 0 else (lanes >= HEAD)


def row_mask(shape, which):
    rows = lax.broadcasted_iota(jnp.int32, shape, 0)
    return (rows < HEAD) if which == 0 else (rows >= HEAD)


def keep(mask, x):
    return jnp.where(mask, x, jnp.zeros_like(x))


def attn_fwd_kernel(
    groups, sel, tok_ref, cxy_ref, freq_ref, wq_ref, wk_ref, wv_ref, bq_ref, bv_ref, wbt_ref, wo_ref,
    part_ref, p_ref, q_ref, k_ref, v_ref, ctx_ref, s_ref, c_ref, tok_t_ref, codes, acc,
):
    step = pl.program_id(0)
    half = s_ref.shape[1]

    @pl.when(step == 0)
    def _():
        rows = s_ref.shape[0]
        lanes = lax.broadcasted_iota(jnp.int32, (rows, half), 1)
        centre = jnp.where(lanes < half // 2, cxy_ref[:, 0:1], cxy_ref[:, 1:2])
        sine, cosine = sin_cos(centre * freq_ref[...])
        s_ref[...] = sine
        c_ref[...] = cosine
        codes[:, :half] = cosine.astype(BF16)
        codes[:, half:] = sine.astype(BF16)
        acc[...] = jnp.zeros_like(acc)
        tok_t = split_rows(tok_ref[...].T, groups)
        tok_t_ref[0] = tok_t[:half]
        tok_t_ref[1] = tok_t[half:]

    tok = tok_ref[...]
    q2 = (mm(tok, wq_ref[...]) + bq_ref[...].astype(F32)).astype(BF16) * BF16(0.125)
    k2 = mm(tok, wk_ref[...]).astype(BF16)
    v2 = (mm(tok, wv_ref[...]) + bv_ref[...].astype(F32)).astype(BF16)
    q_ref[...] = q2
    k_ref[...] = k2
    v_ref[...] = v2
    sine, cosine = s_ref[...], c_ref[...]
    parts = []
    for which in range(2):
        qm = keep(lane_mask(q2.shape, which), q2)
        off = mm(qm, wbt_ref[...])
        a, b = off[:, :half], off[:, half:]
        first = (a * sine + b * cosine).astype(BF16)
        second = (b * sine - a * cosine).astype(BF16)
        scores = mm_nt(first, codes[:, :half]) + mm_nt(second, codes[:, half:]) + mm_nt(qm, k2)
        top = jnp.max(scores, axis=1, keepdims=True)
        raised = jnp.exp(scores - top)
        total = jnp.sum(raised, axis=1, keepdims=True)
        prob = (raised * (1.0 / total)).astype(BF16)
        p_ref[which] = prob
        parts.append(mm(prob, v2))
    ctx2 = jnp.where(lane_mask(parts[0].shape, 0), parts[0], parts[1]).astype(BF16)
    ctx_ref[...] = ctx2
    acc[...] += mm(ctx2, wo_ref[...])

    @pl.when(step == pl.num_programs(0) - 1)
    def _():
        part_ref[...] = acc[...].astype(BF16)


def attn_fwd(sel, tokens, cxy, freq, wq, wk, wv, bq, bv, wbt, wo, length, groups):
    dim = tokens.shape[1]
    inner = wq.shape[1]
    heads = inner // HEAD
    pairs = heads // 2
    wide = 2 * HEAD
    page = lambda i, sel: (sel[0], 0)
    fixed = lambda i, sel: (0, 0)
    cols = lambda i, sel: (0, i)
    rows = lambda i, sel: (i, 0)
    flops = 2 * length * (dim * inner * 4 + heads * (HEAD * dim + length * (dim + 2 * HEAD)))
    return pl.pallas_call(
        partial(attn_fwd_kernel, groups),
        grid_spec=pltpu.PrefetchScalarGridSpec(
            num_scalar_prefetch=1,
            grid=(pairs,),
            in_specs=[
                pl.BlockSpec((length, dim), page),
                pl.BlockSpec((length, 2), page),
                pl.BlockSpec((1, dim // 2), fixed),
                pl.BlockSpec((dim, wide), cols),
                pl.BlockSpec((dim, wide), cols),
                pl.BlockSpec((dim, wide), cols),
                pl.BlockSpec((1, wide), cols),
                pl.BlockSpec((1, wide), cols),
                pl.BlockSpec((wide, dim), rows),
                pl.BlockSpec((wide, dim), rows),
            ],
            out_specs=[
                pl.BlockSpec((length, dim), fixed),
                pl.BlockSpec((2, length, length), lambda i, sel: (i, 0, 0)),
                pl.BlockSpec((length, wide), cols),
                pl.BlockSpec((length, wide), cols),
                pl.BlockSpec((length, wide), cols),
                pl.BlockSpec((length, wide), cols),
                pl.BlockSpec((length, dim // 2), fixed),
                pl.BlockSpec((length, dim // 2), fixed),
                pl.BlockSpec((2, dim // 2, length), lambda i, sel: (0, 0, 0)),
            ],
            scratch_shapes=[
                pltpu.VMEM((length, dim), BF16),
                pltpu.VMEM((length, dim), F32),
            ],
        ),
        out_shape=[
            jax.ShapeDtypeStruct((length, dim), BF16),
            jax.ShapeDtypeStruct((heads, length, length), BF16),
            jax.ShapeDtypeStruct((length, inner), BF16),
            jax.ShapeDtypeStruct((length, inner), BF16),
            jax.ShapeDtypeStruct((length, inner), BF16),
            jax.ShapeDtypeStruct((length, inner), BF16),
            jax.ShapeDtypeStruct((length, dim // 2), F32),
            jax.ShapeDtypeStruct((length, dim // 2), F32),
            jax.ShapeDtypeStruct((2, dim // 2, length), BF16),
        ],
        compiler_params=params(1),
        cost_estimate=cost(flops, 10e6, heads * length * length),
        name="attn_fwd",
    )(sel, tokens, cxy, freq, wq, wk, wv, bq, bv, wbt, wo)


def attn_bwd_kernel(
    groups, box_groups, first, df_ref, wo_ref, q_ref, k_ref, v_ref, p_ref, s_ref, c_ref, wbt_ref, wq_ref, wk_ref, wv_ref,
    *refs,
):
    if first:
        prev_ref = None
    else:
        prev_ref, *refs = refs
    dq_ref, dk_ref, dv_ref, dwb_ref, inp_ref, bq_ref, bv_ref, df_t_ref, codes, acc = refs
    step = pl.program_id(0)
    half = s_ref.shape[1]

    @pl.when(step == 0)
    def _():
        codes[:, :half] = c_ref[...].astype(BF16)
        codes[:, half:] = s_ref[...].astype(BF16)
        acc[...] = jnp.zeros_like(acc)
        df_t = split_rows(df_ref[...].T, groups)
        df_t_ref[0] = df_t[:half]
        df_t_ref[1] = df_t[half:]

    sine, cosine = s_ref[...], c_ref[...]
    q2, k2, v2 = q_ref[...], k_ref[...], v_ref[...]
    dctx = mm_nt(df_ref[...], wo_ref[...]).astype(BF16)
    dctx_t = dctx.T
    q_t = q2.T
    wbt = wbt_ref[...]
    dq = jnp.zeros(q2.shape, F32)
    dk_t, dv_t, dwb = [], [], []
    for which in range(2):
        low, high = which * HEAD, (which + 1) * HEAD
        dm = keep(lane_mask(dctx.shape, which), dctx)
        prob = p_ref[which]
        grad_probs = mm_nt(dm, v2)
        dv_t.append(mm(dctx_t[low:high], prob))
        wide_prob = prob.astype(F32)
        both = wide_prob * grad_probs
        inner = jnp.sum(both, axis=1, keepdims=True)
        ds = (both - wide_prob * inner).astype(BF16)
        dk_t.append(mm(q_t[low:high], ds))
        km = keep(lane_mask(k2.shape, which), k2)
        ga = mm(ds, codes[:, :half]).astype(BF16).astype(F32)
        gb = mm(ds, codes[:, half:]).astype(BF16).astype(F32)
        oa = (ga * sine - gb * cosine).astype(BF16)
        ob = (gb * sine + ga * cosine).astype(BF16)
        wm = keep(row_mask(wbt.shape, which), wbt)
        dq = dq + (mm(ds, km) + mm_nt(oa, wm[:, :half]) + mm_nt(ob, wm[:, half:]))
        dwb.append(jnp.concatenate([mm(q_t[low:high], oa), mm(q_t[low:high], ob)], axis=1))
    dq2 = (dq * 0.125).astype(BF16)
    dk2 = jnp.concatenate(dk_t, axis=0).T.astype(BF16)
    dv2 = jnp.concatenate(dv_t, axis=0).T.astype(BF16)
    dq_ref[...] = dq2
    dk_ref[...] = dk2
    dv_ref[...] = dv2
    dwb = jnp.concatenate(dwb, axis=0)
    if prev_ref is None:
        dwb_ref[...] = dwb
    else:
        box = split_rows((dwb + prev_ref[...]).T, box_groups)
        dwb_ref[0] = box[:half]
        dwb_ref[1] = box[half:]
    bq_ref[...] = jnp.sum(dq2.astype(F32), axis=0, keepdims=True)
    bv_ref[...] = jnp.sum(dv2.astype(F32), axis=0, keepdims=True)
    acc[...] += mm_nt(dq2, wq_ref[...]) + mm_nt(dk2, wk_ref[...]) + mm_nt(dv2, wv_ref[...])

    @pl.when(step == pl.num_programs(0) - 1)
    def _():
        inp_ref[...] = acc[...].astype(BF16)


def attn_bwd(df, wo, q, k, v, prob, sine, cosine, wbt, wq, wk, wv, prev, groups, box_groups):
    length, dim = df.shape
    inner = wq.shape[1]
    heads = inner // HEAD
    pairs = heads // 2
    wide = 2 * HEAD
    fixed = lambda i: (0, 0)
    cols = lambda i: (0, i)
    rows = lambda i: (i, 0)
    flops = 2 * length * (dim * inner * 4 + heads * (3 * HEAD * dim + length * (dim + 4 * HEAD)))
    return pl.pallas_call(
        partial(attn_bwd_kernel, groups, box_groups, prev is None),
        grid=(pairs,),
        in_specs=[
            pl.BlockSpec((length, dim), fixed),
            pl.BlockSpec((wide, dim), rows),
            pl.BlockSpec((length, wide), cols),
            pl.BlockSpec((length, wide), cols),
            pl.BlockSpec((length, wide), cols),
            pl.BlockSpec((2, length, length), lambda i: (i, 0, 0)),
            pl.BlockSpec((length, dim // 2), fixed),
            pl.BlockSpec((length, dim // 2), fixed),
            pl.BlockSpec((wide, dim), rows),
            pl.BlockSpec((dim, wide), cols),
            pl.BlockSpec((dim, wide), cols),
            pl.BlockSpec((dim, wide), cols),
        ]
        + ([] if prev is None else [pl.BlockSpec((wide, dim), rows)]),
        out_specs=[
            pl.BlockSpec((length, wide), cols),
            pl.BlockSpec((length, wide), cols),
            pl.BlockSpec((length, wide), cols),
            pl.BlockSpec((wide, dim), rows)
            if prev is None
            else pl.BlockSpec((2, dim // 2, wide), lambda i: (0, 0, i)),
            pl.BlockSpec((length, dim), fixed),
            pl.BlockSpec((1, wide), cols),
            pl.BlockSpec((1, wide), cols),
            pl.BlockSpec((2, dim // 2, length), lambda i: (0, 0, 0)),
        ],
        out_shape=[
            jax.ShapeDtypeStruct((length, inner), BF16),
            jax.ShapeDtypeStruct((length, inner), BF16),
            jax.ShapeDtypeStruct((length, inner), BF16),
            jax.ShapeDtypeStruct((inner, dim) if prev is None else (2, dim // 2, inner), F32),
            jax.ShapeDtypeStruct((length, dim), BF16),
            jax.ShapeDtypeStruct((1, inner), F32),
            jax.ShapeDtypeStruct((1, inner), F32),
            jax.ShapeDtypeStruct((2, dim // 2, length), BF16),
        ],
        scratch_shapes=[
            pltpu.VMEM((length, dim), BF16),
            pltpu.VMEM((length, dim), F32),
        ],
        compiler_params=params(1),
        cost_estimate=cost(flops, 12e6),
        name="attn_bwd",
    )(df, wo, q, k, v, prob, sine, cosine, wbt, wq, wk, wv, *(() if prev is None else (prev,)))


def split_rows(x_t, groups):
    return jnp.concatenate([x_t[start : start + count] for start, count in groups], axis=0)


def shard_groups(dim, shards):
    rows = dim // shards
    if not fast_path(dim, shards):
        return [(0, dim)]
    order = [z * 4 + x * 2 + c for c in range(2) for z in range(shards // 4) for x in range(2)]
    return [(block * rows, rows) for block in order]


def fast_path(dim, shards):
    return shards == 16 and (dim // shards) % 16 == 0


def gelu_parts(v):
    e = jnp.exp(v * v * -0.5)
    t = 1.0 / (1.0 + (0.3275911 * math.sqrt(0.5)) * jnp.abs(v))
    poly = t * (
        0.5 * 0.254829592
        + t * (0.5 * -0.284496736 + t * (0.5 * 1.421413741 + t * (0.5 * -1.453152027 + t * (0.5 * 1.061405429))))
    )
    tail = poly * e
    phi = jnp.where(v >= 0, 1.0 - tail, tail)
    return phi, phi + v * (e * (1.0 / math.sqrt(2.0 * math.pi)))


def norm_stats(hidden):
    centred = hidden - jnp.mean(hidden, axis=1, keepdims=True)
    variance = jnp.mean(centred * centred, axis=1, keepdims=True)
    inv = lax.rsqrt(variance + 1e-05)
    return centred * inv, inv


def norm_back(grad, scaled, inv):
    return inv * (
        grad
        - jnp.mean(grad, axis=1, keepdims=True)
        - scaled * jnp.mean(grad * scaled, axis=1, keepdims=True)
    )


def column_sum(x):
    return jnp.sum(x, axis=0, keepdims=True)


def ff_kernel(
    groups, table, tok_ref, part_ref, got_ref, gout_ref, bo_ref, g1_ref, b1_ref, bb_ref, g2_ref, b2_ref, bi_ref,
    wi_here, wb_here, wi0, wi1, wi2, wi3, wb0, wb1, wb2, wb3,
    out_ref, df_ref, lhs_ref, rhs_ref, sm_ref, bin_ref,
    wi, wb, slope, norm_low, grad_low, acc, wide, sems,
):
    blocks, dim, cols = wi.shape
    here = blocks // 2
    copies = []
    for j in range(here):
        copies.append((wi_here.at[:, j * cols : (j + 1) * cols], wb_here.at[j * cols : (j + 1) * cols, :]))
    copies += [(wi0, wb0), (wi1, wb1), (wi2, wb2), (wi3, wb3)]
    for j, (a, b) in enumerate(copies):
        pltpu.make_async_copy(a, wi.at[j], sems.at[0, j]).start()
        pltpu.make_async_copy(b, wb.at[j], sems.at[1, j]).start()

    first_sum = (
        tok_ref[...].astype(F32)
        + (part_ref[...].astype(F32) + got_ref[...].astype(F32))
        + bo_ref[...]
    )
    scaled1, inv1 = norm_stats(first_sum)
    normed = scaled1 * g1_ref[...] + b1_ref[...]
    low = normed.astype(BF16)
    norm_low[...] = low
    wide[...] = normed + bb_ref[...]
    acc[...] = jnp.zeros_like(acc)
    low_t = split_rows(low.T, groups)
    split = low_t.shape[0] // 2
    lhs_ref[0, 0] = low_t[:split]
    lhs_ref[1, 0] = low_t[split:]

    def forward(j, _):
        pltpu.make_async_copy(wi0, wi.at[j], sems.at[0, j]).wait()
        pltpu.make_async_copy(wb0, wb.at[j], sems.at[1, j]).wait()
        pre = mm(norm_low[...], wi[j]) + bi_ref[pl.ds(table[j], 1), :]
        phi, step = gelu_parts(pre)
        act = (pre * phi).astype(BF16)
        rhs_ref[1, j] = act
        slope[j] = step
        acc[...] += mm(act, wb[j])
        return 0

    lax.fori_loop(0, blocks, forward, 0)
    scaled2, inv2 = norm_stats(wide[...] + acc[...])
    out_ref[...] = (scaled2 * g2_ref[...] + b2_ref[...]).astype(BF16)
    gout = gout_ref[...].astype(F32)
    sm_ref[0:1] = column_sum(gout * scaled2)
    sm_ref[1:2] = column_sum(gout)
    grad_second = norm_back(gout * g2_ref[...], scaled2, inv2)
    sm_ref[2:3] = column_sum(grad_second)
    low2 = grad_second.astype(BF16)
    grad_low[...] = low2
    low2_t = split_rows(low2.T, groups)
    lhs_ref[0, 1] = low2_t[:split]
    lhs_ref[1, 1] = low2_t[split:]
    acc[...] = grad_second

    def backward(j, _):
        grad_act = mm_nt(grad_low[...], wb[j]).astype(BF16).astype(F32)
        grad_pre = (grad_act * slope[j]).astype(BF16)
        rhs_ref[0, j] = grad_pre
        bin_ref[pl.ds(table[j], 1), :] = column_sum(grad_pre.astype(F32))
        acc[...] += mm_nt(grad_pre, wi[j])
        return 0

    lax.fori_loop(0, blocks, backward, 0)
    grad_normed = acc[...]
    first_sum = (
        tok_ref[...].astype(F32)
        + (part_ref[...].astype(F32) + got_ref[...].astype(F32))
        + bo_ref[...]
    )
    scaled1, inv1 = norm_stats(first_sum)
    sm_ref[3:4] = column_sum(grad_normed * scaled1)
    sm_ref[4:5] = column_sum(grad_normed)
    grad_first = norm_back(grad_normed * g1_ref[...], scaled1, inv1)
    sm_ref[5:6] = column_sum(grad_first)
    df_ref[...] = grad_first.astype(BF16)


def feed_forward(sel, table, tokens, part, got, grad_out, rows, bias_in, wi_here, wb_here, wi_pieces, wb_pieces, groups):
    length, dim = part.shape
    blocks, cols = bias_in.shape
    page = lambda i, sel, table: (sel[0], 0)
    fixed = lambda i, sel, table: (0, 0)
    row = pl.BlockSpec((1, dim), fixed)
    whole = pl.BlockSpec((length, dim), fixed)
    anywhere = pl.BlockSpec(memory_space=pl.ANY)
    body = lambda sel, *refs: ff_kernel(groups, *refs)
    hidden = blocks * cols
    return pl.pallas_call(
        body,
        grid_spec=pltpu.PrefetchScalarGridSpec(
            num_scalar_prefetch=2,
            grid=(1,),
            in_specs=[
                pl.BlockSpec((length, dim), page),
                whole,
                whole,
                pl.BlockSpec((length, dim), page),
                row, row, row, row, row, row,
                pl.BlockSpec((blocks, cols), fixed),
            ]
            + [anywhere] * 10,
            out_specs=[
                whole,
                whole,
                pl.BlockSpec((2, 2, dim // 2, length), lambda i, sel, table: (0, 0, 0, 0)),
                pl.BlockSpec((2, blocks, length, cols), lambda i, sel, table: (0, 0, 0, 0)),
                pl.BlockSpec((8, dim), fixed),
                pl.BlockSpec((blocks, cols), fixed),
            ],
            scratch_shapes=[
                pltpu.VMEM((blocks, dim, cols), BF16),
                pltpu.VMEM((blocks, cols, dim), BF16),
                pltpu.VMEM((blocks, length, cols), F32),
                pltpu.VMEM((length, dim), BF16),
                pltpu.VMEM((length, dim), BF16),
                pltpu.VMEM((length, dim), F32),
                pltpu.VMEM((length, dim), F32),
                pltpu.SemaphoreType.DMA((2, blocks)),
            ],
        ),
        out_shape=[
            jax.ShapeDtypeStruct((length, dim), BF16),
            jax.ShapeDtypeStruct((length, dim), BF16),
            jax.ShapeDtypeStruct((2, 2, dim // 2, length), BF16),
            jax.ShapeDtypeStruct((2, blocks, length, cols), BF16),
            jax.ShapeDtypeStruct((8, dim), F32),
            jax.ShapeDtypeStruct((blocks, cols), F32),
        ],
        compiler_params=params(1),
        cost_estimate=cost(8 * length * dim * hidden, 4 * dim * hidden + 8 * length * hidden, length * hidden),
        name="feed_forward",
    )(sel, table, tokens, part, got, grad_out, *rows, bias_in, wi_here, wb_here, *wi_pieces, *wb_pieces)


def send_kernel(*refs):
    pick_ref, lhs_ref, rhs_ref, out_ref = refs
    del pick_ref
    out_ref[0] = mm(lhs_ref[0, 0], rhs_ref[0, 0]).astype(BF16)


def ff_send(pick, lhs, rhs, remote):
    _, mats, rows, length = lhs.shape
    _, blocks, _, cols = rhs.shape
    half = blocks // 2
    base = half if remote else 0
    return pl.pallas_call(
        send_kernel,
        grid_spec=pltpu.PrefetchScalarGridSpec(
            num_scalar_prefetch=1,
            grid=(mats, half),
            in_specs=[
                pl.BlockSpec((1, 1, rows, length), lambda m, j, pick: (pick[0], m, 0, 0)),
                pl.BlockSpec((1, 1, length, cols), lambda m, j, pick: (m, base + j, 0, 0)),
            ],
            out_specs=pl.BlockSpec(
                (1, rows, cols),
                (lambda m, j, pick: (m, 0, j ^ pick[1])) if remote else (lambda m, j, pick: (m, 0, j)),
            ),
        ),
        out_shape=jax.ShapeDtypeStruct((mats, rows, half * cols), BF16),
        compiler_params=params(2),
        cost_estimate=cost(2 * mats * rows * length * half * cols, 8e6),
        name="ff_grad_send",
    )(pick, lhs, rhs)


def scatter_x(acc, xs_ref, xk_ref, x_index, lead):
    depth, rows = xs_ref.shape[1], xs_ref.shape[2]
    for z in range(depth):
        away = pl.multiple_of((2 * z + 1 - x_index) * rows, 8)
        mine = pl.multiple_of((2 * z + x_index) * rows, 8)
        xs_ref[lead, z] = acc[pl.ds(away, rows), :].astype(BF16)
        xk_ref[lead, z] = acc[pl.ds(mine, rows), :].astype(BF16)


def keep_kernel(pick_ref, lhs_ref, rhs_ref, got_ref, small_ref, small_got_ref, xs_ref, xk_ref, small_out, acc):
    acc[...] = mm(lhs_ref[0, 0], rhs_ref[0, 0]) + got_ref[0].astype(F32)
    scatter_x(acc, xs_ref, xk_ref, pick_ref[2], 0)
    small_out[...] = small_ref[...] + small_got_ref[...]


def ff_keep(pick, lhs, rhs, got, small, small_got, remote, depth):
    _, mats, rows, length = lhs.shape
    _, blocks, _, cols = rhs.shape
    half = blocks // 2
    base = half if remote else 0
    shard = rows // (2 * depth)
    dest = (lambda j, pick: j ^ pick[1]) if remote else (lambda j, pick: j)
    out_spec = pl.BlockSpec((1, depth, shard, cols), lambda m, j, pick: (m, 0, 0, dest(j, pick)))
    small_spec = pl.BlockSpec(small.shape, lambda m, j, pick: (0, 0))
    out = jax.ShapeDtypeStruct((mats, depth, shard, half * cols), BF16)
    return pl.pallas_call(
        keep_kernel,
        grid_spec=pltpu.PrefetchScalarGridSpec(
            num_scalar_prefetch=1,
            grid=(mats, half),
            in_specs=[
                pl.BlockSpec((1, 1, rows, length), lambda m, j, pick: (pick[0], m, 0, 0)),
                pl.BlockSpec((1, 1, length, cols), lambda m, j, pick: (m, base + j, 0, 0)),
                pl.BlockSpec((1, rows, cols), lambda m, j, pick: (m, 0, dest(j, pick))),
                small_spec,
                small_spec,
            ],
            out_specs=[out_spec, out_spec, small_spec],
            scratch_shapes=[pltpu.VMEM((rows, cols), F32)],
        ),
        out_shape=[out, out, jax.ShapeDtypeStruct(small.shape, F32)],
        compiler_params=params(2),
        cost_estimate=cost(2 * mats * rows * length * half * cols, 10e6),
        name="ff_grad_keep",
    )(pick, lhs, rhs, got, small, small_got)


def attn_grad_kernel(scatter, *refs):
    if scatter:
        (pick_ref, tok_a, tok_b, df_a, df_b, qa, qb, ka, kb, va, vb, ca, cb, box_ref,
         got_ref, small_ref, small_got_ref, xs_ref, xk_ref, small_out, acc) = refs
    else:
        pick_ref, tok_a, tok_b, df_a, df_b, qa, qb, ka, kb, va, vb, ca, cb, box_ref, out_ref = refs
    cols = qa.shape[1]
    terms = [
        lambda: mm(tok_a[0], qa[...]) + mm(tok_b[0], qb[...]),
        lambda: mm(tok_a[0], ka[...]) + mm(tok_b[0], kb[...]),
        lambda: mm(tok_a[0], va[...]) + mm(tok_b[0], vb[...]),
        lambda: mm(df_a[0], ca[...]) + mm(df_b[0], cb[...]),
        lambda: box_ref[0],
    ]
    for i, term in enumerate(terms):
        span = slice(i * cols, (i + 1) * cols)
        if not scatter:
            out_ref[:, span] = term().astype(BF16)
            continue
        acc[...] = term() + got_ref[:, span].astype(F32)
        x_index = pick_ref[2]
        depth, rows = xs_ref.shape[1], xs_ref.shape[2]
        for z in range(depth):
            away = pl.multiple_of((2 * z + 1 - x_index) * rows, 8)
            mine = pl.multiple_of((2 * z + x_index) * rows, 8)
            xs_ref[0, z, :, span] = acc[pl.ds(away, rows), :].astype(BF16)
            xk_ref[0, z, :, span] = acc[pl.ds(mine, rows), :].astype(BF16)
    if scatter:
        small_out[...] = small_ref[...] + small_got_ref[...]


def attn_grad(pick, tok_t, df_t, dq, dk, dv, ctx, box, got=None, small=None, small_got=None, depth=None):
    rows, length = tok_t[0].shape[1:]
    cols = dq[0].shape[1]
    scatter = got is not None
    turned = pl.BlockSpec((1, rows, length), lambda i, pick: (pick[0], 0, 0))
    flat = pl.BlockSpec((length, cols), lambda i, pick: (0, 0))
    in_specs = [turned] * 4 + [flat] * 8 + [pl.BlockSpec((1, rows, cols), lambda i, pick: (pick[0], 0, 0))]
    args = [*tok_t, *df_t, *dq, *dk, *dv, *ctx, box]
    scratch = []
    if scatter:
        shard = rows // (2 * depth)
        small_spec = pl.BlockSpec(small.shape, lambda i, pick: (0, 0))
        in_specs += [pl.BlockSpec((rows, 5 * cols), lambda i, pick: (0, 0)), small_spec, small_spec]
        args += [got, small, small_got]
        spec = pl.BlockSpec((1, depth, shard, 5 * cols), lambda i, pick: (0, 0, 0, 0))
        out_specs = [spec, spec, small_spec]
        out = jax.ShapeDtypeStruct((1, depth, shard, 5 * cols), BF16)
        out_shape = [out, out, jax.ShapeDtypeStruct(small.shape, F32)]
        scratch = [pltpu.VMEM((rows, cols), F32)]
    else:
        out_specs = pl.BlockSpec((rows, 5 * cols), lambda i, pick: (0, 0))
        out_shape = jax.ShapeDtypeStruct((rows, 5 * cols), BF16)
    return pl.pallas_call(
        partial(attn_grad_kernel, scatter),
        grid_spec=pltpu.PrefetchScalarGridSpec(
            num_scalar_prefetch=1, grid=(1,), in_specs=in_specs, out_specs=out_specs, scratch_shapes=scratch
        ),
        out_shape=out_shape,
        compiler_params=params(1),
        cost_estimate=cost(16 * rows * length * cols, 8e6),
        name="attn_grad_keep" if scatter else "attn_grad_send",
    )(pick, *args)


def add_x_kernel(pick_ref, keep_ref, got_ref, small_ref, small_got_ref, own, s1, s2, s3, small_out):
    z = pick_ref[3]
    for d, ref in enumerate((own, s1, s2, s3)):
        ref[...] = (keep_ref[:, z ^ d].astype(F32) + got_ref[:, z ^ d].astype(F32)).astype(BF16)
    small_out[...] = small_ref[...] + small_got_ref[...]


def add_x(pick, kept, got, small, small_got):
    mats, depth, rows, cols = kept.shape
    block = jax.ShapeDtypeStruct((mats, rows, cols), BF16)
    full = lambda s: pl.BlockSpec(s.shape, lambda i, pick: (0,) * len(s.shape))
    return pl.pallas_call(
        add_x_kernel,
        grid_spec=pltpu.PrefetchScalarGridSpec(
            num_scalar_prefetch=1,
            grid=(1,),
            in_specs=[full(kept), full(got), full(small), full(small)],
            out_specs=[full(block)] * 4 + [full(small)],
        ),
        out_shape=[block] * 4 + [jax.ShapeDtypeStruct(small.shape, F32)],
        compiler_params=params(1),
        cost_estimate=cost(kept.size, 6 * kept.size),
        name="add_x",
    )(pick, kept, got, small, small_got)


def sum4(own, r1, r2, r3):
    return (own.astype(F32) + r1.astype(F32)) + (r2.astype(F32) + r3.astype(F32))


def add_z_kernel(own, r1, r2, r3, sm, m1, m2, m3, out, small_out):
    out[...] = sum4(own[...], r1[...], r2[...], r3[...]).astype(BF16)
    small_out[...] = sum4(sm[...], m1[...], m2[...], m3[...])


def add_z(blocks, smalls):
    return pl.pallas_call(
        add_z_kernel,
        out_shape=[
            jax.ShapeDtypeStruct(blocks[0].shape, BF16),
            jax.ShapeDtypeStruct(smalls[0].shape, F32),
        ],
        compiler_params=pltpu.CompilerParams(vmem_limit_bytes=VMEM_LIMIT),
        cost_estimate=cost(4 * blocks[0].size, 10 * blocks[0].size),
        name="add_z",
    )(*blocks, *smalls)


def ff_last_kernel(own, r1, r2, r3, got, sm, sm_got, in_out, back_out, small_out):
    in_out[...] = sum4(own[0], r1[0], r2[0], r3[0]) + got[0].astype(F32)
    back_out[...] = (sum4(own[1], r1[1], r2[1], r3[1]) + got[1].astype(F32)).T
    small_out[...] = sm[...] + sm_got[...]


def ff_last(blocks, got, small, small_got):
    _, rows, cols = got.shape
    return pl.pallas_call(
        ff_last_kernel,
        out_shape=[
            jax.ShapeDtypeStruct((rows, cols), F32),
            jax.ShapeDtypeStruct((cols, rows), F32),
            jax.ShapeDtypeStruct(small.shape, F32),
        ],
        compiler_params=pltpu.CompilerParams(vmem_limit_bytes=VMEM_LIMIT),
        cost_estimate=cost(10 * got.size, 20 * got.size),
        name="ff_last",
    )(*blocks, got, small, small_got)


def attn_last_kernel(own, r1, r2, r3, sm, m1, m2, m3, q_out, k_out, v_out, box_out, wo_out, small_out):
    cols = q_out.shape[1]
    for i, ref in enumerate((q_out, k_out, v_out, wo_out, box_out)):
        span = slice(i * cols, (i + 1) * cols)
        total = sum4(own[0, :, span], r1[0, :, span], r2[0, :, span], r3[0, :, span])
        ref[...] = total.T if ref is wo_out else total
    small_out[...] = sum4(sm[...], m1[...], m2[...], m3[...])


def attn_last(blocks, smalls):
    _, rows, cols = blocks[0].shape
    cols = cols // 5
    tall = jax.ShapeDtypeStruct((rows, cols), F32)
    return pl.pallas_call(
        attn_last_kernel,
        out_shape=[tall] * 4
        + [jax.ShapeDtypeStruct((cols, rows), F32), jax.ShapeDtypeStruct(smalls[0].shape, F32)],
        compiler_params=pltpu.CompilerParams(vmem_limit_bytes=VMEM_LIMIT),
        cost_estimate=cost(4 * blocks[0].size, 12 * blocks[0].size),
        name="attn_last",
    )(*blocks, *smalls)


def place_grad_kernel(sel, df_ref, a_ref, b_ref, *refs):
    refs[-1][...] = df_ref[...].astype(F32) + (a_ref[...].astype(F32) + b_ref[...].astype(F32))


def place_grad(sel, df, mine, got, pages, into=None):
    length, dim = df.shape
    whole = pl.BlockSpec((length, dim), lambda i, sel: (0, 0))
    args = [df, mine, got] + ([] if into is None else [into])
    return pl.pallas_call(
        place_grad_kernel,
        grid_spec=pltpu.PrefetchScalarGridSpec(
            num_scalar_prefetch=1,
            grid=(1,),
            in_specs=[whole] * 3 + ([] if into is None else [pl.BlockSpec(memory_space=pl.ANY)]),
            out_specs=pl.BlockSpec((length, dim), lambda i, sel: (sel[0], 0)),
        ),
        out_shape=jax.ShapeDtypeStruct((pages * length, dim), F32),
        input_output_aliases={} if into is None else {4: 0},
        compiler_params=params(1),
        cost_estimate=cost(3 * df.size, 10 * df.size),
        name="place_grad",
    )(sel, *args)


def place_output_kernel(sel, a_ref, b_ref, out_ref):
    length = a_ref.shape[0]
    own = pl.multiple_of(sel[0] * length, length)
    other = pl.multiple_of((1 - sel[0]) * length, length)
    out_ref[pl.ds(own, length), :] = a_ref[...]
    out_ref[pl.ds(other, length), :] = b_ref[...]


def place_output(sel, mine, got):
    length, dim = mine.shape
    whole = pl.BlockSpec((length, dim), lambda i, sel: (0, 0))
    return pl.pallas_call(
        place_output_kernel,
        grid_spec=pltpu.PrefetchScalarGridSpec(
            num_scalar_prefetch=1,
            grid=(1,),
            in_specs=[whole] * 2,
            out_specs=pl.BlockSpec((2 * length, dim), lambda i, sel: (0, 0)),
        ),
        out_shape=jax.ShapeDtypeStruct((2 * length, dim), BF16),
        compiler_params=params(1),
        cost_estimate=cost(mine.size, 8 * mine.size),
        name="place_output",
    )(sel, mine, got)


def swap_perm(size, flip):
    return [(i, i ^ flip) for i in range(size)]


def encoding_rows(w_box):
    rows, cols = w_box.shape
    quarters = w_box.reshape(4, rows // 4, cols)
    return jnp.concatenate([quarters[i] for i in (0, 2, 1, 3)], axis=0)


def encoding_groups(groups, dim):
    quarter = dim // 4
    place = (0, 2, 1, 3)
    out = []
    for start, count in groups:
        while count:
            size = min(count, quarter - start % quarter)
            out.append((place[start // quarter] * quarter + start % quarter, size))
            start, count = start + size, count - size
    return out


def shards(
    shards_dp,
    tokens,
    boxes,
    resolution,
    w_query,
    bias_query,
    w_key,
    w_value,
    bias_value,
    w_box,
    w_out,
    bias_out,
    norm1_gain,
    norm1_bias,
    w_in,
    bias_in,
    w_back,
    bias_back,
    norm2_gain,
    norm2_bias,
    grad_out,
):
    row_count, dim = tokens.shape
    pages = resolution.shape[0]
    length = row_count // pages
    hidden = w_in.shape[1]
    piece = hidden // 4
    here = lax.axis_index("head").astype(jnp.int32)
    spot = lax.axis_index("dp").astype(jnp.int32)
    core, x_index, z_index, corner = spot % 2, (spot // 2) % 2, spot // 4, spot % 4
    own = here.reshape(1)
    other = (1 - here).reshape(1)
    groups = shard_groups(dim, shards_dp)
    fast = fast_path(dim, shards_dp)

    def over_head(value):
        return lax.ppermute(value, "head", [(0, 1), (1, 0)])

    def over_dp(value, flip):
        return lax.ppermute(value, "dp", swap_perm(shards_dp, flip))

    in_first = over_head(lax.dynamic_slice_in_dim(w_in, corner * piece, piece, 1))
    back_first = over_head(lax.dynamic_slice_in_dim(w_back, corner * piece, piece, 0))
    in_second, back_second = over_dp(in_first, 2), over_dp(back_first, 2)
    in_pieces = [in_first, over_dp(in_first, 1), in_second, over_dp(in_second, 1)]
    back_pieces = [back_first, over_dp(back_first, 1), back_second, over_dp(back_second, 1)]
    bias_there = over_head(bias_in)
    bias_rows = jnp.where(
        here == 0, jnp.concatenate([bias_in, bias_there]), jnp.concatenate([bias_there, bias_in])
    )
    bias_rows = bias_rows.astype(F32).reshape(8, piece)
    table = jnp.concatenate(
        [here * 4 + jnp.arange(4, dtype=jnp.int32), (1 - here) * 4 + (corner ^ jnp.arange(4, dtype=jnp.int32))]
    )

    widths = (612 + 204 * resolution).astype(F32)
    heights = (792 + 264 * resolution).astype(F32)
    across = jnp.repeat(widths, length, total_repeat_length=row_count)
    downward = jnp.repeat(heights, length, total_repeat_length=row_count)
    centre_x = (boxes[0] + boxes[2]).astype(F32) * 500.0 / across
    centre_y = (boxes[1] + boxes[3]).astype(F32) * 500.0 / downward
    centres = jnp.stack([centre_x, centre_y], axis=1)
    quarter = w_box.shape[0] // 4
    freqs = jnp.exp(jnp.arange(quarter).astype(F32) * (-math.log(10000.0) / quarter))
    freqs = jnp.concatenate([freqs, freqs])[None, :]
    box_t = encoding_rows(w_box).T

    attend = lambda sel: attn_fwd(
        sel, tokens, centres, freqs, w_query, w_key, w_value, bias_query[None, :], bias_value[None, :],
        box_t, w_out, length, groups,
    )
    part_other, *saved_other = attend(other)
    got = over_head(part_other)
    part_own, *saved_own = attend(own)

    rows = [v.astype(F32)[None, :] for v in (bias_out, norm1_gain, norm1_bias, bias_back, norm2_gain, norm2_bias)]
    out_own, df_own, lhs, rhs, small, bin_sum = feed_forward(
        own, table, tokens, part_own, got, grad_out, rows, bias_rows, w_in, w_back, in_pieces, back_pieces, groups
    )
    df_other = over_head(df_own)
    output = place_output(own, out_own, over_head(out_own))
    ff_small = jnp.concatenate([small[:6].reshape(12, piece), bin_sum, jnp.zeros((4, piece), F32)])

    box_groups = encoding_groups(groups, w_box.shape[0])

    def attend_back(df, saved, prev):
        prob, q, k, v, _, sine, cosine, _ = saved
        return attn_bwd(
            df, w_out, q, k, v, prob, sine, cosine, box_t, w_query, w_key, w_value, prev, groups, box_groups
        )

    pick_send = jnp.stack([1 - core, corner, x_index, z_index])
    pick_keep = jnp.stack([core, corner, x_index, z_index])

    if fast:
        depth = shards_dp // 4
        send_a = over_dp(ff_send(pick_send, lhs, rhs, True), 1)
        send_b = over_dp(ff_send(pick_send, lhs, rhs, False), 1)
        small_got = over_dp(ff_small, 1)
        xs_a, xk_a, small_1 = ff_keep(pick_keep, lhs, rhs, send_a, ff_small, small_got, True, depth)
        xs_b, xk_b, _ = ff_keep(pick_keep, lhs, rhs, send_b, ff_small, small_got, False, depth)
        xg_a, xg_b = over_dp(xs_a, 2), over_dp(xs_b, 2)
        small_1_got = over_dp(small_1, 2)

    dq_a, dk_a, dv_a, box_a, inp_own, bq_a, bv_a, df_t_a = attend_back(df_own, saved_own, None)
    inp_own_got = over_head(inp_own)

    if fast:
        *z_a, small_2 = add_x(pick_keep, xk_a, xg_a, small_1, small_1_got)
        zg_a = [z_a[0]] + [over_dp(z_a[d], 4 * d) for d in (1, 2, 3)]
        small_z = [small_2] + [over_dp(small_2, 4 * d) for d in (1, 2, 3)]
        *z_b, _ = add_x(pick_keep, xk_b, xg_b, small_1, small_1_got)
        zg_b = [z_b[0]] + [over_dp(z_b[d], 4 * d) for d in (1, 2, 3)]

    dq_b, dk_b, dv_b, box, inp_other, bq_b, bv_b, df_t_b = attend_back(df_other, saved_other, box_a)
    inp_other_got = over_head(inp_other)
    grad_terms = (
        (saved_own[7], saved_other[7]), (df_t_a, df_t_b), (dq_a, dq_b), (dk_a, dk_b), (dv_a, dv_b),
        (saved_own[4], saved_other[4]), box,
    )
    attn_small = jnp.concatenate([bq_a, bv_a, bq_b, bv_b, jnp.zeros((4, bq_a.shape[1]), F32)])

    if fast:
        sent = over_dp(attn_grad(pick_send, *grad_terms), 1)
        small_got = over_dp(attn_small, 1)
        xs, xk, a_small = attn_grad(pick_keep, *grad_terms, sent, attn_small, small_got, depth)
        *blocks, a_small = add_x(pick_keep, xk, over_dp(xs, 2), a_small, over_dp(a_small, 2))
        blocks = [blocks[0]] + [over_dp(blocks[d], 4 * d) for d in (1, 2, 3)]
        a_smalls = [a_small] + [over_dp(a_small, 4 * d) for d in (1, 2, 3)]
        grad_q, grad_k, grad_v, grad_box, grad_wo, a_small = attn_last(blocks, a_smalls)
        a_sum, small_3 = add_z(zg_a, small_z)
        grad_in, grad_back, ff_small = ff_last(zg_b, over_head(a_sum), small_3, over_head(small_3))
    else:
        both = [pick_keep.at[0].set(c) for c in (0, 1)]
        scatter = lambda value, axis: lax.psum_scatter(
            value.astype(F32), "dp", scatter_dimension=axis, tiled=True
        )
        halves = [
            scatter(jnp.concatenate([ff_send(pick, lhs, rhs, remote) for pick in both], axis=1), 1)
            for remote in (True, False)
        ]
        total = halves[1] + over_head(halves[0])
        grad_in, grad_back = total[0], total[1].T
        total = scatter(jnp.concatenate([attn_grad(pick, *grad_terms) for pick in both], axis=0), 0)
        grad_q, grad_k, grad_v, grad_wo, grad_box = jnp.split(total, 5, axis=1)
        grad_wo = grad_wo.T
        ff_small = lax.psum(ff_small, ("dp", "head"))
        a_small = lax.psum(attn_small, "dp")

    grad_input = place_grad(other, df_other, inp_other, inp_own_got, pages)
    grad_input = place_grad(own, df_own, inp_own, inp_other_got, pages, grad_input)
    rows = ff_small[:12].reshape(6, dim)
    bin_rows = lax.dynamic_slice_in_dim(ff_small[12:20], here * 4, 4, 0).reshape(hidden)
    a_rows = a_small[0:2] + a_small[2:4]
    return (
        output,
        grad_input,
        grad_q,
        a_rows[0],
        grad_k,
        grad_v,
        a_rows[1],
        grad_box,
        grad_wo,
        rows[5],
        rows[3],
        rows[4],
        grad_in,
        bin_rows,
        grad_back,
        rows[2],
        rows[0],
        rows[1],
    )


def solution(mesh):
    placed = (
        P("dp", None),
        P(None, "dp"),
        P("dp"),
        P(None, "head"),
        P("head"),
        P(None, "head"),
        P(None, "head"),
        P("head"),
        P(None, "head"),
        P("head", None),
        P(),
        P(),
        P(),
        P(None, "head"),
        P("head"),
        P("head", None),
        P(),
        P(),
        P(),
        P("dp", None),
    )
    return jax.shard_map(
        partial(shards, mesh.shape["dp"]),
        mesh=mesh,
        in_specs=placed,
        out_specs=(
            P("dp", None),
            P("dp", None),
            P("dp", "head"),
            P("head"),
            P("dp", "head"),
            P("dp", "head"),
            P("head"),
            P("dp", "head"),
            P("head", "dp"),
            P(),
            P(),
            P(),
            P("dp", "head"),
            P("head"),
            P("head", "dp"),
            P(),
            P(),
            P(),
        ),
        check_vma=False,
    )
```

```python
from functools import partial
import math

import jax
import numpy as np
import jax.numpy as jnp
from jax import lax
from jax.experimental import pallas as pl
from jax.experimental.pallas import tpu as pltpu
from jax.sharding import PartitionSpec as P

HEAD = 64
F32 = jnp.float32
BF16 = jnp.bfloat16
VMEM_LIMIT = 63 * 1024 * 1024


def hbm(shape, dtype):
    return pltpu.HBM(tuple(shape), dtype)


def mm(a, b):
    return jnp.dot(a, b, preferred_element_type=F32)


def mm_nt(a, b):
    return lax.dot_general(a, b, (((1,), (1,)), ((), ())), preferred_element_type=F32)


def params(steps):
    return pltpu.CompilerParams(
        dimension_semantics=("arbitrary",) * steps, vmem_limit_bytes=VMEM_LIMIT
    )


def cost(flops, nbytes, trans=0):
    return pl.CostEstimate(flops=int(flops), bytes_accessed=int(nbytes), transcendentals=int(trans))


def sin_cos(angle):
    turns = jnp.floor(angle * (2.0 / math.pi) + 0.5)
    r = angle - turns * 1.5703125
    r = r - turns * 4.837512969970703125e-4
    r = r - turns * 7.54978995489188216e-8
    r2 = r * r
    s = r + r * r2 * (
        -1.6666654611e-1 + r2 * (8.3321608736e-3 + r2 * -1.9515295891e-4)
    )
    c = 1.0 - 0.5 * r2 + r2 * r2 * (
        4.166664568298827e-2 + r2 * (-1.388731625493765e-3 + r2 * 2.443315711809948e-5)
    )
    quad = turns.astype(jnp.int32)
    odd = (quad & 1) == 1
    sine = jnp.where(odd, c, s)
    cosine = jnp.where(odd, s, c)
    sine = jnp.where((quad & 2) == 2, -sine, sine)
    cosine = jnp.where(((quad + 1) & 2) == 2, -cosine, cosine)
    return sine, cosine


def lane_mask(shape, which):
    lanes = lax.broadcasted_iota(jnp.int32, shape, 1)
    return (lanes < HEAD) if which == 0 else (lanes >= HEAD)


def row_mask(shape, which):
    rows = lax.broadcasted_iota(jnp.int32, shape, 0)
    return (rows < HEAD) if which == 0 else (rows >= HEAD)


def keep(mask, x):
    return jnp.where(mask, x, jnp.zeros_like(x))


def attn_fwd_kernel(
    groups, which_page, pick, res, tok_ref, box_ref, freq_ref, wq_ref, wk_ref, wv_ref, bq_ref, bv_ref, wbt_ref, wo_ref,
    part_ref, p_ref, q_ref, k_ref, v_ref, ctx_ref, s_ref, c_ref, tok_t_ref, codes, mixed, acc, biases,
):
    step = pl.program_id(0)
    half = s_ref.shape[1]

    @pl.when(step == 0)
    def _():
        rows = s_ref.shape[0]
        lanes = lax.broadcasted_iota(jnp.int32, (rows, half), 1)
        level = res[pick[which_page]]
        width = (612 + 204 * level).astype(F32)
        height = (792 + 264 * level).astype(F32)
        corners = box_ref[...]
        centre_x = (corners[0:1] + corners[2:3]).astype(F32) * 500.0 / width
        centre_y = (corners[1:2] + corners[3:4]).astype(F32) * 500.0 / height
        both = jnp.concatenate([centre_x, centre_y, jnp.zeros((6, rows), F32)], axis=0).T
        centre = jnp.where(lanes < half // 2, both[:, 0:1], both[:, 1:2])
        sine, cosine = sin_cos(centre * freq_ref[...])
        s_ref[...] = sine
        c_ref[...] = cosine
        codes[:, :half] = cosine.astype(BF16)
        codes[:, half : 2 * half] = sine.astype(BF16)
        acc[...] = jnp.zeros_like(acc)
        biases[0:1] = bq_ref[...].astype(F32).reshape(1, -1)
        biases[1:2] = bv_ref[...].astype(F32).reshape(1, -1)
        tok_t = split_rows(tok_ref[...].T, groups)
        tok_t_ref[0] = tok_t[:half]
        tok_t_ref[1] = tok_t[half:]

    tok = tok_ref[...]
    rows = tok.shape[0]
    wide = wq_ref.shape[1]
    span = pl.ds(pl.multiple_of(step * wide, wide), wide)
    q2 = (mm(tok, wq_ref[...]) + biases[0:1, span]).astype(BF16) * BF16(0.125)
    k2 = mm(tok, wk_ref[...]).astype(BF16)
    v2 = (mm(tok, wv_ref[...]) + biases[1:2, span]).astype(BF16)
    q_ref[...] = q2
    k_ref[...] = k2
    v_ref[...] = v2
    codes[:, 2 * half :] = k2
    sine, cosine = s_ref[...], c_ref[...]
    for which in range(2):
        span = slice(which * rows, (which + 1) * rows)
        qm = keep(lane_mask(q2.shape, which), q2)
        off = mm(qm, wbt_ref[...])
        a, b = off[:, :half], off[:, half:]
        mixed[span, :half] = (a * sine + b * cosine).astype(BF16)
        mixed[span, half : 2 * half] = (b * sine - a * cosine).astype(BF16)
        mixed[span, 2 * half :] = qm
    parts = []
    for which in range(2):
        span = slice(which * rows, (which + 1) * rows)
        scores = mm_nt(mixed[span], codes[...])
        top = jnp.max(scores, axis=1, keepdims=True)
        raised = jnp.exp(scores - top)
        total = jnp.sum(raised, axis=1, keepdims=True)
        prob = (raised * (1.0 / total)).astype(BF16)
        p_ref[which] = prob
        parts.append(mm(prob, v2))
    ctx2 = jnp.where(lane_mask(parts[0].shape, 0), parts[0], parts[1]).astype(BF16)
    ctx_ref[...] = ctx2
    acc[...] += mm(ctx2, wo_ref[...])

    @pl.when(step == pl.num_programs(0) - 1)
    def _():
        part_ref[...] = acc[...].astype(BF16)


def attn_fwd(which_page, pick, res, tokens, boxes, freq, wq, wk, wv, bq, bv, wbt, wo, length, groups):
    dim = tokens.shape[1]
    inner = wq.shape[1]
    heads = inner // HEAD
    pairs = heads // 2
    wide = 2 * HEAD
    page = lambda i, pick, res: (pick[which_page], 0)
    fixed = lambda i, pick, res: (0, 0)
    cols = lambda i, pick, res: (0, i)
    rows = lambda i, pick, res: (i, 0)
    flops = 2 * length * (dim * inner * 4 + heads * (HEAD * dim + length * (dim + 2 * HEAD)))
    return pl.pallas_call(
        partial(attn_fwd_kernel, groups, which_page),
        grid_spec=pltpu.PrefetchScalarGridSpec(
            num_scalar_prefetch=2,
            grid=(pairs,),
            in_specs=[
                pl.BlockSpec((length, dim), page),
                pl.BlockSpec((4, length), lambda i, pick, res: (0, pick[which_page])),
                pl.BlockSpec((1, dim // 2), fixed),
                pl.BlockSpec((dim, wide), cols),
                pl.BlockSpec((dim, wide), cols),
                pl.BlockSpec((dim, wide), cols),
                pl.BlockSpec((inner,), lambda i, pick, res: (0,)),
                pl.BlockSpec((inner,), lambda i, pick, res: (0,)),
                pl.BlockSpec((wide, dim), rows),
                pl.BlockSpec((wide, dim), rows),
            ],
            out_specs=[
                pl.BlockSpec((length, dim), fixed),
                pl.BlockSpec((2, length, length), lambda i, pick, res: (i, 0, 0)),
                pl.BlockSpec((length, wide), cols),
                pl.BlockSpec((length, wide), cols),
                pl.BlockSpec((length, wide), cols),
                pl.BlockSpec((length, wide), cols),
                pl.BlockSpec((length, dim // 2), fixed),
                pl.BlockSpec((length, dim // 2), fixed),
                pl.BlockSpec((2, dim // 2, length), lambda i, pick, res: (0, 0, 0)),
            ],
            scratch_shapes=[
                pltpu.VMEM((length, dim + wide), BF16),
                pltpu.VMEM((2 * length, dim + wide), BF16),
                pltpu.VMEM((length, dim), F32),
                pltpu.VMEM((8, inner), F32),
            ],
        ),
        out_shape=[
            hbm((length, dim), BF16),
            hbm((heads, length, length), BF16),
            hbm((length, inner), BF16),
            hbm((length, inner), BF16),
            hbm((length, inner), BF16),
            hbm((length, inner), BF16),
            hbm((length, dim // 2), F32),
            hbm((length, dim // 2), F32),
            hbm((2, dim // 2, length), BF16),
        ],
        compiler_params=params(1),
        cost_estimate=cost(flops, 10e6, heads * length * length),
        name="attn_fwd",
    )(pick, res, tokens, boxes, freq, wq, wk, wv, bq, bv, wbt, wo)


def attn_bwd_kernel(
    groups, box_groups, first, df_ref, wo_ref, q_ref, k_ref, v_ref, p_ref, s_ref, c_ref, wbt_ref, wq_ref, wk_ref, wv_ref,
    *refs,
):
    if first:
        prev_ref = None
    else:
        prev_ref, *refs = refs
    dq_ref, dk_ref, dv_ref, dwb_ref, inp_ref, bq_ref, bv_ref, df_t_ref, codes, acc = refs
    step = pl.program_id(0)
    half = s_ref.shape[1]

    @pl.when(step == 0)
    def _():
        codes[:, :half] = c_ref[...].astype(BF16)
        codes[:, half:] = s_ref[...].astype(BF16)
        acc[...] = jnp.zeros_like(acc)
        df_t = split_rows(df_ref[...].T, groups)
        df_t_ref[0] = df_t[:half]
        df_t_ref[1] = df_t[half:]

    sine, cosine = s_ref[...], c_ref[...]
    q2, k2, v2 = q_ref[...], k_ref[...], v_ref[...]
    dctx = mm_nt(df_ref[...], wo_ref[...]).astype(BF16)
    dctx_t = dctx.T
    q_t = q2.T
    wbt = wbt_ref[...]
    dq = jnp.zeros(q2.shape, F32)
    dk_t, dv_t, dwb = [], [], []
    for which in range(2):
        low, high = which * HEAD, (which + 1) * HEAD
        dm = keep(lane_mask(dctx.shape, which), dctx)
        prob = p_ref[which]
        grad_probs = mm_nt(dm, v2)
        dv_t.append(mm(dctx_t[low:high], prob))
        wide_prob = prob.astype(F32)
        both = wide_prob * grad_probs
        inner = jnp.sum(both, axis=1, keepdims=True)
        ds = (both - wide_prob * inner).astype(BF16)
        dk_t.append(mm(q_t[low:high], ds))
        km = keep(lane_mask(k2.shape, which), k2)
        ga = mm(ds, codes[:, :half]).astype(BF16).astype(F32)
        gb = mm(ds, codes[:, half:]).astype(BF16).astype(F32)
        oa = (ga * sine - gb * cosine).astype(BF16)
        ob = (gb * sine + ga * cosine).astype(BF16)
        wm = keep(row_mask(wbt.shape, which), wbt)
        dq = dq + (mm(ds, km) + mm_nt(oa, wm[:, :half]) + mm_nt(ob, wm[:, half:]))
        dwb.append(jnp.concatenate([mm(q_t[low:high], oa), mm(q_t[low:high], ob)], axis=1))
    dq2 = (dq * 0.125).astype(BF16)
    dk2 = jnp.concatenate(dk_t, axis=0).T.astype(BF16)
    dv2 = jnp.concatenate(dv_t, axis=0).T.astype(BF16)
    dq_ref[...] = dq2
    dk_ref[...] = dk2
    dv_ref[...] = dv2
    dwb = jnp.concatenate(dwb, axis=0)
    if prev_ref is None:
        dwb_ref[...] = dwb
    else:
        box = split_rows((dwb + prev_ref[...]).T, box_groups)
        dwb_ref[0] = box[:half]
        dwb_ref[1] = box[half:]
    bq_ref[...] = jnp.sum(dq2.astype(F32), axis=0, keepdims=True)
    bv_ref[...] = jnp.sum(dv2.astype(F32), axis=0, keepdims=True)
    acc[...] += mm_nt(dq2, wq_ref[...]) + mm_nt(dk2, wk_ref[...]) + mm_nt(dv2, wv_ref[...])

    @pl.when(step == pl.num_programs(0) - 1)
    def _():
        inp_ref[...] = acc[...].astype(BF16)


def attn_bwd(df, wo, q, k, v, prob, sine, cosine, wbt, wq, wk, wv, prev, groups, box_groups):
    length, dim = df.shape
    inner = wq.shape[1]
    heads = inner // HEAD
    pairs = heads // 2
    wide = 2 * HEAD
    fixed = lambda i: (0, 0)
    cols = lambda i: (0, i)
    rows = lambda i: (i, 0)
    flops = 2 * length * (dim * inner * 4 + heads * (3 * HEAD * dim + length * (dim + 4 * HEAD)))
    return pl.pallas_call(
        partial(attn_bwd_kernel, groups, box_groups, prev is None),
        grid=(pairs,),
        in_specs=[
            pl.BlockSpec((length, dim), fixed),
            pl.BlockSpec((wide, dim), rows),
            pl.BlockSpec((length, wide), cols),
            pl.BlockSpec((length, wide), cols),
            pl.BlockSpec((length, wide), cols),
            pl.BlockSpec((2, length, length), lambda i: (i, 0, 0)),
            pl.BlockSpec((length, dim // 2), fixed),
            pl.BlockSpec((length, dim // 2), fixed),
            pl.BlockSpec((wide, dim), rows),
            pl.BlockSpec((dim, wide), cols),
            pl.BlockSpec((dim, wide), cols),
            pl.BlockSpec((dim, wide), cols),
        ]
        + ([] if prev is None else [pl.BlockSpec((wide, dim), rows)]),
        out_specs=[
            pl.BlockSpec((length, wide), cols),
            pl.BlockSpec((length, wide), cols),
            pl.BlockSpec((length, wide), cols),
            pl.BlockSpec((wide, dim), rows)
            if prev is None
            else pl.BlockSpec((2, dim // 2, wide), lambda i: (0, 0, i)),
            pl.BlockSpec((length, dim), fixed),
            pl.BlockSpec((1, wide), cols),
            pl.BlockSpec((1, wide), cols),
            pl.BlockSpec((2, dim // 2, length), lambda i: (0, 0, 0)),
        ],
        out_shape=[
            hbm((length, inner), BF16),
            hbm((length, inner), BF16),
            hbm((length, inner), BF16),
            hbm((inner, dim) if prev is None else (2, dim // 2, inner), F32),
            hbm((length, dim), BF16),
            hbm((1, inner), F32),
            hbm((1, inner), F32),
            hbm((2, dim // 2, length), BF16),
        ],
        scratch_shapes=[
            pltpu.VMEM((length, dim), BF16),
            pltpu.VMEM((length, dim), F32),
        ],
        compiler_params=params(1),
        cost_estimate=cost(flops, 12e6),
        name="attn_bwd",
    )(df, wo, q, k, v, prob, sine, cosine, wbt, wq, wk, wv, *(() if prev is None else (prev,)))


def split_rows(x_t, groups):
    return jnp.concatenate([x_t[start : start + count] for start, count in groups], axis=0)


def shard_groups(dim, shards):
    rows = dim // shards
    if not fast_path(dim, shards):
        return [(0, dim)]
    order = [z * 4 + x * 2 + c for c in range(2) for z in range(shards // 4) for x in range(2)]
    return [(block * rows, rows) for block in order]


def fast_path(dim, shards):
    return shards == 16 and (dim // shards) % 16 == 0


def gelu_parts(v):
    e = jnp.exp(v * v * -0.5)
    t = 1.0 / (1.0 + (0.3275911 * math.sqrt(0.5)) * jnp.abs(v))
    poly = t * (
        0.5 * 0.254829592
        + t * (0.5 * -0.284496736 + t * (0.5 * 1.421413741 + t * (0.5 * -1.453152027 + t * (0.5 * 1.061405429))))
    )
    tail = poly * e
    phi = jnp.where(v >= 0, 1.0 - tail, tail)
    return phi, phi + v * (e * (1.0 / math.sqrt(2.0 * math.pi)))


def norm_stats(hidden):
    centred = hidden - jnp.mean(hidden, axis=1, keepdims=True)
    variance = jnp.mean(centred * centred, axis=1, keepdims=True)
    inv = lax.rsqrt(variance + 1e-05)
    return centred * inv, inv


def norm_back(grad, scaled, inv):
    return inv * (
        grad
        - jnp.mean(grad, axis=1, keepdims=True)
        - scaled * jnp.mean(grad * scaled, axis=1, keepdims=True)
    )


def column_sum(x):
    return jnp.sum(x, axis=0, keepdims=True)


def ff_kernel(
    groups, pick, tok_ref, part_ref, got_ref, gout_ref, bo_ref, g1_ref, b1_ref, bb_ref, g2_ref, b2_ref,
    bi_here, bi_there,
    wi_here, wb_here, wi0, wi1, wi2, wi3, wb0, wb1, wb2, wb3,
    out_ref, df_ref, lhs_ref, rhs_ref, small_ref,
    wi, wb, slope, norm_low, grad_low, acc, wide, bi_ref, sems,
):
    blocks, dim, cols = wi.shape
    here = blocks // 2
    piece = cols // 2
    remote = [(wi0, wb0), (wi1, wb1), (wi2, wb2), (wi3, wb3)]
    for p in range(2 * blocks):
        if p < blocks:
            at = (p % 2) * piece
            span = pl.ds(at, piece)
            source = (wi_here.at[:, pl.ds(p * piece, piece)], wb_here.at[pl.ds(p * piece, piece), :])
        else:
            span = pl.ds(pl.multiple_of(((pick[6] ^ p) & 1) * piece, piece), piece)
            source = remote[p - blocks]
        pltpu.make_async_copy(source[0], wi.at[p // 2, :, span], sems.at[0, p]).start()
        pltpu.make_async_copy(source[1], wb.at[p // 2, span, :], sems.at[1, p]).start()

    def vec(ref):
        return ref[...].astype(F32).reshape(1, -1)

    here_at, there_at = pick[0] * here, pick[1] * here
    bias_here, bias_there = vec(bi_here), vec(bi_there)
    for j in range(here):
        bi_ref[pl.ds(here_at + j, 1), :] = bias_here[:, j * cols : (j + 1) * cols]
        bi_ref[pl.ds(there_at + j, 1), :] = bias_there[:, j * cols : (j + 1) * cols]

    def place(j):
        return jnp.where(j < here, here_at + j, there_at + (pick[7] ^ (j - here)))

    bo, g1, b1, bb, g2, b2 = (vec(r) for r in (bo_ref, g1_ref, b1_ref, bb_ref, g2_ref, b2_ref))
    first_sum = (
        tok_ref[...].astype(F32)
        + (part_ref[...].astype(F32) + got_ref[...].astype(F32))
        + bo
    )
    scaled1, inv1 = norm_stats(first_sum)
    normed = scaled1 * g1 + b1
    low = normed.astype(BF16)
    norm_low[...] = low
    wide[...] = normed + bb
    acc[...] = jnp.zeros_like(acc)
    low_t = split_rows(low.T, groups)
    split = low_t.shape[0] // 2
    lhs_ref[0, 0] = low_t[:split]
    lhs_ref[1, 0] = low_t[split:]

    def forward(j, _):
        for p in range(2):
            pltpu.make_async_copy(wi0, wi.at[j, :, pl.ds(0, piece)], sems.at[0, 2 * j + p]).wait()
            pltpu.make_async_copy(wb0, wb.at[j, pl.ds(0, piece), :], sems.at[1, 2 * j + p]).wait()
        pre = mm(norm_low[...], wi[j]) + bi_ref[pl.ds(place(j), 1), :]
        phi, step = gelu_parts(pre)
        act = (pre * phi).astype(BF16)
        rhs_ref[1, j] = act
        slope[j] = step
        acc[...] += mm(act, wb[j])
        return 0

    lax.fori_loop(0, blocks, forward, 0)
    scaled2, inv2 = norm_stats(wide[...] + acc[...])
    out_ref[...] = (scaled2 * g2 + b2).astype(BF16)
    gout = gout_ref[...].astype(F32)
    small_gain2 = column_sum(gout * scaled2)
    small_bias2 = column_sum(gout)
    grad_second = norm_back(gout * g2, scaled2, inv2)
    small_back = column_sum(grad_second)
    low2 = grad_second.astype(BF16)
    grad_low[...] = low2
    low2_t = split_rows(low2.T, groups)
    lhs_ref[0, 1] = low2_t[:split]
    lhs_ref[1, 1] = low2_t[split:]
    acc[...] = grad_second

    def backward(j, _):
        grad_act = mm_nt(grad_low[...], wb[j]).astype(BF16).astype(F32)
        grad_pre = (grad_act * slope[j]).astype(BF16)
        rhs_ref[0, j] = grad_pre
        bi_ref[pl.ds(place(j), 1), :] = column_sum(grad_pre.astype(F32))
        acc[...] += mm_nt(grad_pre, wi[j])
        return 0

    lax.fori_loop(0, blocks, backward, 0)
    grad_normed = acc[...]
    first_sum = (
        tok_ref[...].astype(F32)
        + (part_ref[...].astype(F32) + got_ref[...].astype(F32))
        + bo
    )
    scaled1, inv1 = norm_stats(first_sum)
    small_gain1 = column_sum(grad_normed * scaled1)
    small_bias1 = column_sum(grad_normed)
    grad_first = norm_back(grad_normed * g1, scaled1, inv1)
    small_out = column_sum(grad_first)
    df_ref[...] = grad_first.astype(BF16)
    small_ref[...] = jnp.concatenate(
        [
            jnp.concatenate([small_gain2, small_bias2], axis=1),
            jnp.concatenate([small_back, small_gain1], axis=1),
            jnp.concatenate([small_bias1, small_out], axis=1),
            jnp.concatenate([bi_ref[j : j + 1] for j in range(here)], axis=1),
            jnp.concatenate([bi_ref[j : j + 1] for j in range(here, blocks)], axis=1),
            jnp.zeros((3, 2 * dim), F32),
        ],
        axis=0,
    )


def feed_forward(pick, tokens, part, got, grad_out, rows, bias_in, bias_there, wi_here, wb_here, wi_pieces, wb_pieces, groups):
    length, dim = part.shape
    cols = 2 * wi_pieces[0].shape[1]
    blocks = 2 * wi_here.shape[1] // cols
    page = lambda i, pick: (pick[0], 0)
    fixed = lambda i, pick: (0, 0)
    row = pl.BlockSpec((dim,), lambda i, pick: (0,))
    bias_row = pl.BlockSpec(bias_in.shape, lambda i, pick: (0,))
    whole = pl.BlockSpec((length, dim), fixed)
    anywhere = pl.BlockSpec(memory_space=pl.ANY)
    hidden = blocks * cols
    return pl.pallas_call(
        partial(ff_kernel, groups),
        grid_spec=pltpu.PrefetchScalarGridSpec(
            num_scalar_prefetch=1,
            grid=(1,),
            in_specs=[
                pl.BlockSpec((length, dim), page),
                whole,
                whole,
                pl.BlockSpec((length, dim), page),
                row, row, row, row, row, row,
                bias_row, bias_row,
            ]
            + [anywhere] * 10,
            out_specs=[
                whole,
                whole,
                pl.BlockSpec((2, 2, dim // 2, length), lambda i, pick: (0, 0, 0, 0)),
                pl.BlockSpec((2, blocks, length, cols), lambda i, pick: (0, 0, 0, 0)),
                pl.BlockSpec((8, 2 * dim), fixed),
            ],
            scratch_shapes=[
                pltpu.VMEM((blocks, dim, cols), BF16),
                pltpu.VMEM((blocks, cols, dim), BF16),
                pltpu.VMEM((blocks, length, cols), F32),
                pltpu.VMEM((length, dim), BF16),
                pltpu.VMEM((length, dim), BF16),
                pltpu.VMEM((length, dim), F32),
                pltpu.VMEM((length, dim), F32),
                pltpu.VMEM((blocks, cols), F32),
                pltpu.SemaphoreType.DMA((2, 2 * blocks)),
            ],
        ),
        out_shape=[
            hbm((length, dim), BF16),
            hbm((length, dim), BF16),
            hbm((2, 2, dim // 2, length), BF16),
            hbm((2, blocks, length, cols), BF16),
            hbm((8, 2 * dim), F32),
        ],
        compiler_params=params(1),
        cost_estimate=cost(8 * length * dim * hidden, 4 * dim * hidden + 8 * length * hidden, length * hidden),
        name="feed_forward",
    )(pick, tokens, part, got, grad_out, *rows, bias_in, bias_there, wi_here, wb_here, *wi_pieces, *wb_pieces)


TAIL = 16


def split2(x):
    high = x.astype(BF16)
    return high, (x - high.astype(F32)).astype(BF16)


def rounded(x):
    high, low = split2(x)
    return high.astype(F32) + low.astype(F32)


def tall(x):
    return jnp.concatenate([x, jnp.zeros((TAIL - x.shape[0],) + x.shape[1:], x.dtype)], axis=0)


def ff_send_kernel(pick, lhs_ref, rhs_ref, small_ref, out_ref):
    rows = lhs_ref.shape[2]
    for m in range(2):
        out_ref[m, :rows] = mm(lhs_ref[0, m], rhs_ref[m, 0]).astype(BF16)
    for m, term in enumerate(split2(small_ref[...])):
        out_ref[m, rows:] = tall(term)


def ff_keep_kernel(pick, lhs_ref, rhs_ref, got_ref, small_ref, xs_ref, xk_ref, small_out, acc):
    rows = lhs_ref.shape[2]
    shard = acc.shape[0] // 8
    x_index = pick[4]
    for m in range(2):
        acc[...] = mm(lhs_ref[0, m], rhs_ref[m, 0]) + got_ref[m, :rows].astype(F32)
        for z in range(4):
            away = pl.multiple_of((2 * z + 1 - x_index) * shard, 8)
            mine = pl.multiple_of((2 * z + x_index) * shard, 8)
            xs_ref[m, z * shard : (z + 1) * shard] = acc[pl.ds(away, shard), :].astype(BF16)
            xk_ref[m, z * shard : (z + 1) * shard] = acc[pl.ds(mine, shard), :].astype(BF16)
    small = rounded(small_ref[...]) + (got_ref[0, rows : rows + 8].astype(F32) + got_ref[1, rows : rows + 8].astype(F32))
    small_out[...] = small
    for m, term in enumerate(split2(small)):
        xs_ref[m, 4 * shard :] = tall(term)


def ff_grad(pick, lhs, rhs, small, remote, got=None):
    _, mats, rows, length = lhs.shape
    _, blocks, _, cols = rhs.shape
    half = blocks // 2
    base = half if remote else 0
    which = 2 if got is not None else 3
    dest = (lambda j, pick: j ^ pick[7]) if remote else (lambda j, pick: j)
    column = lambda height: pl.BlockSpec((2, height, cols), lambda j, pick: (0, 0, dest(j, pick)))
    small_spec = pl.BlockSpec((8, cols), lambda j, pick: (0, dest(j, pick)))
    in_specs = [
        pl.BlockSpec((1, mats, rows, length), lambda j, pick: (pick[which], 0, 0, 0)),
        pl.BlockSpec((2, 1, length, cols), lambda j, pick: (0, base + j, 0, 0)),
    ]
    wide = half * cols
    estimate = cost(2 * mats * rows * length * wide, 10e6)
    if got is None:
        return pl.pallas_call(
            ff_send_kernel,
            grid_spec=pltpu.PrefetchScalarGridSpec(
                num_scalar_prefetch=1,
                grid=(half,),
                in_specs=in_specs + [small_spec],
                out_specs=column(rows + TAIL),
            ),
            out_shape=hbm((2, rows + TAIL, wide), BF16),
            compiler_params=params(1),
            cost_estimate=estimate,
            name="ff_grad_send",
        )(pick, lhs, rhs, small)
    return pl.pallas_call(
        ff_keep_kernel,
        grid_spec=pltpu.PrefetchScalarGridSpec(
            num_scalar_prefetch=1,
            grid=(half,),
            in_specs=in_specs + [column(rows + TAIL), small_spec],
            out_specs=[column(rows // 2 + TAIL), column(rows // 2), small_spec],
            scratch_shapes=[pltpu.VMEM((rows, cols), F32)],
        ),
        out_shape=[
            hbm((2, rows // 2 + TAIL, wide), BF16),
            hbm((2, rows // 2, wide), BF16),
            hbm((8, wide), F32),
        ],
        compiler_params=params(1),
        cost_estimate=estimate,
        name="ff_grad_keep",
    )(pick, lhs, rhs, got, small)


def wide_tail(vector):
    high, low = split2(vector)
    return tall(jnp.concatenate([high, low], axis=0))


def attn_grad_kernel(scatter, *refs):
    if scatter:
        (pick, tok_a, tok_b, df_a, df_b, qa, qb, ka, kb, va, vb, ca, cb, box_ref, bqa, bqb, bva, bvb,
         got_ref, xs_ref, xk_ref, small_out, acc) = refs
    else:
        (pick, tok_a, tok_b, df_a, df_b, qa, qb, ka, kb, va, vb, ca, cb, box_ref, bqa, bqb, bva, bvb,
         out_ref) = refs
    cols = qa.shape[1]
    rows = tok_a.shape[1]
    terms = [
        lambda: mm(tok_a[0], qa[...]) + mm(tok_b[0], qb[...]),
        lambda: mm(tok_a[0], ka[...]) + mm(tok_b[0], kb[...]),
        lambda: mm(tok_a[0], va[...]) + mm(tok_b[0], vb[...]),
        lambda: mm(df_a[0], ca[...]) + mm(df_b[0], cb[...]),
        lambda: box_ref[0],
    ]
    small = jnp.concatenate(
        [bqa[...] + bqb[...], bva[...] + bvb[...], jnp.zeros((1, 3 * cols), F32)], axis=1
    )
    for i, term in enumerate(terms):
        span = slice(i * cols, (i + 1) * cols)
        if not scatter:
            out_ref[:rows, span] = term().astype(BF16)
            continue
        acc[...] = term() + got_ref[:rows, span].astype(F32)
        x_index = pick[4]
        shard = rows // 8
        for z in range(4):
            away = pl.multiple_of((2 * z + 1 - x_index) * shard, 8)
            mine = pl.multiple_of((2 * z + x_index) * shard, 8)
            xs_ref[0, z * shard : (z + 1) * shard, span] = acc[pl.ds(away, shard), :].astype(BF16)
            xk_ref[0, z * shard : (z + 1) * shard, span] = acc[pl.ds(mine, shard), :].astype(BF16)
    if scatter:
        small = rounded(small) + (got_ref[rows : rows + 1].astype(F32) + got_ref[rows + 1 : rows + 2].astype(F32))
        small_out[...] = jnp.concatenate([small, jnp.zeros((7, 5 * cols), F32)], axis=0)
        xs_ref[0, rows // 2 :] = wide_tail(small)
    else:
        out_ref[rows:] = wide_tail(small)


def attn_grad(pick, tok_t, df_t, dq, dk, dv, ctx, box, bq, bv, got=None, which=None):
    rows, length = tok_t[0].shape[1:]
    cols = dq[0].shape[1]
    scatter = got is not None
    if which is None:
        which = 2 if scatter else 3
    turned = pl.BlockSpec((1, rows, length), lambda i, pick: (pick[which], 0, 0))
    flat = pl.BlockSpec((length, cols), lambda i, pick: (0, 0))
    row = pl.BlockSpec((1, cols), lambda i, pick: (0, 0))
    in_specs = [turned] * 4 + [flat] * 8 + [pl.BlockSpec((1, rows, cols), lambda i, pick: (pick[which], 0, 0))]
    in_specs += [row] * 4
    args = [*tok_t, *df_t, *dq, *dk, *dv, *ctx, box, *bq, *bv]
    scratch = []
    if scatter:
        in_specs += [pl.BlockSpec((rows + TAIL, 5 * cols), lambda i, pick: (0, 0))]
        args += [got]
        whole = lambda height: pl.BlockSpec((1, height, 5 * cols), lambda i, pick: (0, 0, 0))
        out_specs = [whole(rows // 2 + TAIL), whole(rows // 2), pl.BlockSpec((8, 5 * cols), lambda i, pick: (0, 0))]
        out_shape = [
            hbm((1, rows // 2 + TAIL, 5 * cols), BF16),
            hbm((1, rows // 2, 5 * cols), BF16),
            hbm((8, 5 * cols), F32),
        ]
        scratch = [pltpu.VMEM((rows, cols), F32)]
    else:
        out_specs = pl.BlockSpec((rows + TAIL, 5 * cols), lambda i, pick: (0, 0))
        out_shape = hbm((rows + TAIL, 5 * cols), BF16)
    return pl.pallas_call(
        partial(attn_grad_kernel, scatter),
        grid_spec=pltpu.PrefetchScalarGridSpec(
            num_scalar_prefetch=1, grid=(1,), in_specs=in_specs, out_specs=out_specs, scratch_shapes=scratch
        ),
        out_shape=out_shape,
        compiler_params=params(1),
        cost_estimate=cost(16 * rows * length * cols, 8e6),
        name="attn_grad_keep" if scatter else "attn_grad_send",
    )(pick, *args)


def tail_sum(ref, at):
    if ref.shape[0] == 2:
        return ref[0, at : at + 8].astype(F32) + ref[1, at : at + 8].astype(F32)
    one = ref[0, at : at + 1].astype(F32) + ref[0, at + 1 : at + 2].astype(F32)
    return jnp.concatenate([one, jnp.zeros((7, one.shape[1]), F32)], axis=0)


def put_tail(ref, at, small):
    if ref.shape[0] == 2:
        for m, term in enumerate(split2(small)):
            ref[m, at:] = tall(term)
    else:
        ref[0, at:] = wide_tail(small[0:1])


def add_x_kernel(tailed, pick, keep_ref, got_ref, small_ref, own, s1, s2, s3, *rest):
    shard = own.shape[1]
    z = pick[5]
    if tailed:
        small = rounded(small_ref[...]) + tail_sum(got_ref, 4 * shard)
        rest[0][...] = small
    for d, ref in enumerate((own, s1, s2, s3)):
        at = pl.multiple_of((z ^ d) * shard, 16)
        ref[:, :shard] = (
            keep_ref[:, pl.ds(at, shard), :].astype(F32) + got_ref[:, pl.ds(at, shard), :].astype(F32)
        ).astype(BF16)
        if d and tailed:
            put_tail(ref, shard, small)


def add_x(pick, kept, got, small, tailed):
    mats, rows, cols = kept.shape
    shard = rows // 4
    own = hbm((mats, shard, cols), BF16)
    sent = hbm((mats, shard + (TAIL if tailed else 0), cols), BF16)
    full = lambda s: pl.BlockSpec(s.shape, lambda i, pick: (0,) * len(s.shape))
    extra = [hbm(small.shape, F32)] if tailed else []
    return pl.pallas_call(
        partial(add_x_kernel, tailed),
        grid_spec=pltpu.PrefetchScalarGridSpec(
            num_scalar_prefetch=1,
            grid=(1,),
            in_specs=[full(kept), full(got), full(small)],
            out_specs=[full(own)] + [full(sent)] * 3 + [full(s) for s in extra],
        ),
        out_shape=[own] + [sent] * 3 + extra,
        compiler_params=params(1),
        cost_estimate=cost(kept.size, 6 * kept.size),
        name="add_x",
    )(pick, kept, got, small)


def sum4(own, r1, r2, r3):
    return (own.astype(F32) + r1.astype(F32)) + (r2.astype(F32) + r3.astype(F32))


def small4(small_ref, others, at):
    terms = [tail_sum(r, at) for r in others]
    return (rounded(small_ref[...]) + terms[0]) + (terms[1] + terms[2])


def add_z_kernel(own, r1, r2, r3, small_ref, out, small_out):
    shard = own.shape[1]
    out[:, :shard] = sum4(own[...], r1[:, :shard], r2[:, :shard], r3[:, :shard]).astype(BF16)
    small = small4(small_ref, (r1, r2, r3), shard)
    small_out[...] = small
    put_tail(out, shard, small)


def add_z(blocks, small):
    return pl.pallas_call(
        add_z_kernel,
        out_shape=[
            hbm(blocks[1].shape, BF16),
            hbm(small.shape, F32),
        ],
        compiler_params=pltpu.CompilerParams(vmem_limit_bytes=VMEM_LIMIT),
        cost_estimate=cost(4 * blocks[0].size, 10 * blocks[0].size),
        name="add_z",
    )(*blocks, small)


def ff_last_kernel(pick, own, r1, r2, r3, got, small_ref, in_out, back_out, *vectors):
    small_out = vectors[-1]
    shard = own.shape[1]
    in_out[...] = sum4(own[0], r1[0], r2[0], r3[0]) + got[0, :shard].astype(F32)
    back_out[...] = (sum4(own[1], r1[1], r2[1], r3[1]) + got[1, :shard].astype(F32)).T
    small = rounded(small_ref[...]) + tail_sum(got, shard)
    small_out[...] = small
    dim = small.shape[1] // 2
    for i in range(6):
        vectors[i][...] = small[i // 2 : i // 2 + 1, (i % 2) * dim : (i % 2 + 1) * dim].reshape(dim)
    vectors[6][...] = small_out[pl.ds(3 + pick[0], 1), :].reshape(2 * dim)


def ff_last(pick, blocks, got, small):
    _, rows, cols = blocks[0].shape
    dim = cols // 2
    full = lambda s: pl.BlockSpec(s.shape, lambda i, pick: (0,) * len(s.shape))
    out_shape = (
        [hbm((rows, cols), F32), hbm((cols, rows), F32)]
        + [hbm((dim,), F32)] * 6
        + [hbm((cols,), F32)]
    )
    return pl.pallas_call(
        ff_last_kernel,
        grid_spec=pltpu.PrefetchScalarGridSpec(
            num_scalar_prefetch=1,
            grid=(1,),
            in_specs=[full(b) for b in blocks] + [full(got), full(small)],
            out_specs=[full(s) for s in out_shape],
            scratch_shapes=[pltpu.VMEM(small.shape, F32)],
        ),
        out_shape=out_shape,
        compiler_params=params(1),
        cost_estimate=cost(10 * got.size, 20 * got.size),
        name="ff_last",
    )(pick, *blocks, got, small)


def attn_last_kernel(own, r1, r2, r3, small_ref, q_out, k_out, v_out, box_out, wo_out, bq_out, bv_out):
    cols = q_out.shape[1]
    shard = own.shape[1]
    for i, ref in enumerate((q_out, k_out, v_out, wo_out, box_out)):
        span = slice(i * cols, (i + 1) * cols)
        total = sum4(own[0, :, span], r1[0, :shard, span], r2[0, :shard, span], r3[0, :shard, span])
        ref[...] = total.T if ref is wo_out else total
    small = small4(small_ref, (r1, r2, r3), shard)
    bq_out[...] = small[0:1, :cols].reshape(cols)
    bv_out[...] = small[0:1, cols : 2 * cols].reshape(cols)


def attn_last(blocks, small):
    _, rows, cols = blocks[0].shape
    cols = cols // 5
    flat = hbm((rows, cols), F32)
    vector = hbm((cols,), F32)
    return pl.pallas_call(
        attn_last_kernel,
        out_shape=[flat] * 4 + [hbm((cols, rows), F32), vector, vector],
        compiler_params=pltpu.CompilerParams(vmem_limit_bytes=VMEM_LIMIT),
        cost_estimate=cost(4 * blocks[0].size, 12 * blocks[0].size),
        name="attn_last",
    )(*blocks, small)


def place_grad_kernel(pick, df_ref, a_ref, b_ref, *refs):
    refs[-1][...] = df_ref[...].astype(F32) + (a_ref[...].astype(F32) + b_ref[...].astype(F32))


def place_grad(which, pick, df, mine, got, pages, into=None):
    length, dim = df.shape
    steps = 2
    part = pl.BlockSpec((length // steps, dim), lambda i, pick: (i, 0))
    args = [df, mine, got] + ([] if into is None else [into])
    return pl.pallas_call(
        place_grad_kernel,
        grid_spec=pltpu.PrefetchScalarGridSpec(
            num_scalar_prefetch=1,
            grid=(steps,),
            in_specs=[part] * 3 + ([] if into is None else [pl.BlockSpec(memory_space=pl.ANY)]),
            out_specs=pl.BlockSpec((length // steps, dim), lambda i, pick: (pick[which] * steps + i, 0)),
        ),
        out_shape=hbm((pages * length, dim), F32),
        input_output_aliases={} if into is None else {4: 0},
        compiler_params=params(1),
        cost_estimate=cost(3 * df.size, 10 * df.size),
        name="place_grad",
    )(pick, *args)


def place_output_kernel(pick, a_ref, b_ref, out_ref):
    length = a_ref.shape[0]
    own = pl.multiple_of(pick[0] * length, length)
    other = pl.multiple_of(pick[1] * length, length)
    out_ref[pl.ds(own, length), :] = a_ref[...]
    out_ref[pl.ds(other, length), :] = b_ref[...]


def place_output(pick, mine, got):
    length, dim = mine.shape
    whole = pl.BlockSpec((length, dim), lambda i, pick: (0, 0))
    return pl.pallas_call(
        place_output_kernel,
        grid_spec=pltpu.PrefetchScalarGridSpec(
            num_scalar_prefetch=1,
            grid=(1,),
            in_specs=[whole] * 2,
            out_specs=pl.BlockSpec((2 * length, dim), lambda i, pick: (0, 0)),
        ),
        out_shape=hbm((2 * length, dim), BF16),
        compiler_params=params(1),
        cost_estimate=cost(mine.size, 8 * mine.size),
        name="place_output",
    )(pick, mine, got)


def swap_perm(size, flip):
    return [(i, i ^ flip) for i in range(size)]


def encoding_rows(w_box):
    rows, cols = w_box.shape
    quarters = w_box.reshape(4, rows // 4, cols)
    return jnp.concatenate([quarters[i] for i in (0, 2, 1, 3)], axis=0)


def encoding_groups(groups, dim):
    quarter = dim // 4
    place = (0, 2, 1, 3)
    out = []
    for start, count in groups:
        while count:
            size = min(count, quarter - start % quarter)
            out.append((place[start // quarter] * quarter + start % quarter, size))
            start, count = start + size, count - size
    return out


def shards(
    shards_dp,
    tokens,
    boxes,
    resolution,
    w_query,
    bias_query,
    w_key,
    w_value,
    bias_value,
    w_box,
    w_out,
    bias_out,
    norm1_gain,
    norm1_bias,
    w_in,
    bias_in,
    w_back,
    bias_back,
    norm2_gain,
    norm2_bias,
    grad_out,
):
    dim = tokens.shape[1]
    pages = resolution.shape[0]
    length = tokens.shape[0] // pages
    hidden = w_in.shape[1]
    piece = hidden // 4
    here = lax.axis_index("head").astype(jnp.int32)
    spot = lax.axis_index("dp").astype(jnp.int32)
    core, x_index, z_index, corner = spot % 2, (spot // 2) % 2, spot // 4, spot % 4
    pick = jnp.stack([here, 1 - here, core, 1 - core, x_index, z_index, corner, corner // 2])
    groups = shard_groups(dim, shards_dp)
    fast = fast_path(dim, shards_dp)

    def over_head(value):
        return lax.ppermute(value, "head", [(0, 1), (1, 0)])

    def over_dp(value, flip):
        return lax.ppermute(value, "dp", swap_perm(shards_dp, flip))

    def after(value, *others):
        return lax.optimization_barrier((value, others))[0]

    in_first = over_head(lax.dynamic_slice_in_dim(w_in, corner * piece, piece, 1))
    back_first = over_head(lax.dynamic_slice_in_dim(w_back, corner * piece, piece, 0))
    bias_there = over_head(bias_in)

    quarter = w_box.shape[0] // 4
    freqs = np.exp(np.arange(quarter, dtype=np.float32) * np.float32(-math.log(10000.0) / quarter))
    freqs = jnp.asarray(np.concatenate([freqs, freqs])[None, :])
    box_t = encoding_rows(w_box).T

    def attend(which, tok):
        return attn_fwd(
            which, pick, resolution, tok, boxes, freqs, w_query, w_key, w_value, bias_query, bias_value,
            box_t, w_out, length, groups,
        )

    part_other, *saved_other = attend(1, tokens)
    got = over_head(part_other)
    in_first, back_first = after((in_first, back_first), part_other)
    in_second, back_second = over_dp(in_first, 2), over_dp(back_first, 2)
    in_near, back_near = over_dp(in_first, 1), over_dp(back_first, 1)
    part_own, *saved_own = attend(0, after(tokens, part_other))
    in_second, back_second = after((in_second, back_second), part_own)
    in_pieces = [in_first, in_near, in_second, over_dp(in_second, 1)]
    back_pieces = [back_first, back_near, back_second, over_dp(back_second, 1)]

    out_own, df_own, lhs, rhs, small = feed_forward(
        pick, tokens, part_own, got, grad_out,
        (bias_out, norm1_gain, norm1_bias, bias_back, norm2_gain, norm2_bias),
        bias_in, bias_there, w_in, w_back, in_pieces, back_pieces, groups,
    )
    df_other = over_head(df_own)
    box_groups = encoding_groups(groups, w_box.shape[0])

    def attend_back(df, saved, prev):
        prob, q, k, v, _, sine, cosine, _ = saved
        return attn_bwd(
            df, w_out, q, k, v, prob, sine, cosine, box_t, w_query, w_key, w_value, prev, groups, box_groups
        )

    if fast:
        sent_a = ff_grad(pick, lhs, rhs, small, True)
        got_a = over_dp(sent_a, 1)
        sent_b = ff_grad(pick, lhs, after(rhs, sent_a), small, False)
        got_b = over_dp(sent_b, 1)
        xs_a, xk_a, small_1 = ff_grad(pick, lhs, after(rhs, sent_b), small, True, got_a)
        xg_a = over_dp(xs_a, 2)
        got_b = after(got_b, xs_a)
        xs_b, xk_b, small_b = ff_grad(pick, lhs, after(rhs, xs_a), small, False, got_b)
        df_other, df_own, out_send = after((df_other, df_own, out_own), xs_b)
        df_own = after(df_own, df_other)
    else:
        out_send = out_own
    out_other = over_head(out_send)

    dq_a, dk_a, dv_a, box_a, inp_own, bq_a, bv_a, df_t_a = attend_back(df_own, saved_own, None)
    inp_own_got = over_head(inp_own)

    if fast:
        xg_a, out_other, xs_b = after((xg_a, out_other, xs_b), inp_own)
        xg_b = over_dp(xs_b, 2)
        *z_a, small_2 = add_x(pick, xk_a, after(xg_a, out_other), small_1, True)
        zg_a = [z_a[0]] + [over_dp(z_a[d], 4 * d) for d in (1, 2, 3)]
        df_other = after(df_other, z_a[0])

    dq_b, dk_b, dv_b, box, inp_other, bq_b, bv_b, df_t_b = attend_back(df_other, saved_other, box_a)
    inp_other_got = over_head(inp_other)
    grad_terms = (
        (saved_own[7], saved_other[7]), (df_t_a, df_t_b), (dq_a, dq_b), (dk_a, dk_b), (dv_a, dv_b),
        (saved_own[4], saved_other[4]), box, (bq_a, bq_b), (bv_a, bv_b),
    )

    if fast:
        xg_b, zg_a, inp_own_got = after((xg_b, zg_a, inp_own_got), inp_other)
        sent = attn_grad(pick, *grad_terms[:-1], after(grad_terms[-1], zg_a, xg_b, inp_own_got))
        sent_got = over_dp(sent, 1)
        z_b = add_x(pick, after(xk_b, sent), xg_b, small_b, False)
        output = place_output(pick, after(out_own, z_b), out_other)
        xs, xk, a_small = attn_grad(pick, *grad_terms, after(sent_got, output))
        xg = over_dp(xs, 2)
        z_b = after(z_b, xs)
        zg_b = [z_b[0]] + [over_dp(z_b[d], 4 * d) for d in (1, 2, 3)]
        a_sum, small_3 = add_z([after(zg_a[0], xs)] + zg_a[1:], small_2)
        grad_input = place_grad(1, pick, after(df_other, a_sum), inp_other, inp_own_got, pages)
        *blocks, a_small = add_x(pick, after(xk, grad_input), xg, a_small, True)
        zg_b, inp_other_got = after((zg_b, inp_other_got), blocks)
        blocks, a_sum = after((blocks, a_sum), zg_b)
        blocks = [blocks[0]] + [over_dp(blocks[d], 4 * d) for d in (1, 2, 3)]
        a_sum = over_head(a_sum)
        grad_input = place_grad(0, pick, after(df_own, zg_b), inp_own, inp_other_got, pages, grad_input)
        grad_in, grad_back, n2g, n2b, bias_back_sum, n1g, n1b, bias_out_sum, bias_in_sum = ff_last(
            pick, after(zg_b, grad_input), a_sum, small_3
        )
        blocks = after(blocks, grad_in)
        grad_q, grad_k, grad_v, grad_box, grad_wo, bq_sum, bv_sum = attn_last(blocks, a_small)
    else:
        scatter = lambda value, axis: lax.psum_scatter(
            value.astype(F32), "dp", scatter_dimension=axis, tiled=True
        )
        cores = [pick.at[3].set(c) for c in (0, 1)]
        halves = [
            scatter(
                jnp.concatenate([ff_grad(p, lhs, rhs, small, remote)[:, : dim // 2] for p in cores], axis=1), 1
            )
            for remote in (True, False)
        ]
        total = halves[1] + over_head(halves[0])
        grad_in, grad_back = total[0], total[1].T
        total = scatter(
            jnp.concatenate([attn_grad(p, *grad_terms)[: dim // 2] for p in cores], axis=0), 0
        )
        grad_q, grad_k, grad_v, grad_wo, grad_box = jnp.split(total, 5, axis=1)
        grad_wo = grad_wo.T
        small = lax.psum(small, ("dp", "head"))
        n2g, n2b, bias_back_sum, n1g, n1b, bias_out_sum = small[:3].reshape(6, dim)
        bias_in_sum = lax.dynamic_index_in_dim(small, 3 + here, 0, keepdims=False)
        bq_sum, bv_sum = lax.psum(((bq_a + bq_b)[0], (bv_a + bv_b)[0]), "dp")
        output = place_output(pick, out_own, out_other)
        grad_input = place_grad(1, pick, df_other, inp_other, inp_own_got, pages)
        grad_input = place_grad(0, pick, df_own, inp_own, inp_other_got, pages, grad_input)
    return (
        output,
        grad_input,
        grad_q,
        bq_sum,
        grad_k,
        grad_v,
        bv_sum,
        grad_box,
        grad_wo,
        bias_out_sum,
        n1g,
        n1b,
        grad_in,
        bias_in_sum,
        grad_back,
        bias_back_sum,
        n2g,
        n2b,
    )


def solution(mesh):
    placed = (
        P("dp", None),
        P(None, "dp"),
        P("dp"),
        P(None, "head"),
        P("head"),
        P(None, "head"),
        P(None, "head"),
        P("head"),
        P(None, "head"),
        P("head", None),
        P(),
        P(),
        P(),
        P(None, "head"),
        P("head"),
        P("head", None),
        P(),
        P(),
        P(),
        P("dp", None),
    )
    return jax.shard_map(
        partial(shards, mesh.shape["dp"]),
        mesh=mesh,
        in_specs=placed,
        out_specs=(
            P("dp", None),
            P("dp", None),
            P("dp", "head"),
            P("head"),
            P("dp", "head"),
            P("dp", "head"),
            P("head"),
            P("dp", "head"),
            P("head", "dp"),
            P(),
            P(),
            P(),
            P("dp", "head"),
            P("head"),
            P("head", "dp"),
            P(),
            P(),
            P(),
        ),
        check_vma=False,
    )
```

```python
from functools import partial
import math

import jax
import numpy as np
import jax.numpy as jnp
from jax import lax
from jax.experimental import pallas as pl
from jax.experimental.pallas import tpu as pltpu
from jax.sharding import PartitionSpec as P

HEAD = 64
F32 = jnp.float32
BF16 = jnp.bfloat16
VMEM_LIMIT = 63 * 1024 * 1024


def hbm(shape, dtype):
    return pltpu.HBM(tuple(shape), dtype)


def mm(a, b):
    return jnp.dot(a, b, preferred_element_type=F32)


def mm_nt(a, b):
    return lax.dot_general(a, b, (((1,), (1,)), ((), ())), preferred_element_type=F32)


def params(steps):
    return pltpu.CompilerParams(
        dimension_semantics=("arbitrary",) * steps, vmem_limit_bytes=VMEM_LIMIT
    )


def cost(flops, nbytes, trans=0):
    return pl.CostEstimate(flops=int(flops), bytes_accessed=int(nbytes), transcendentals=int(trans))


def sin_cos(angle):
    turns = jnp.floor(angle * (2.0 / math.pi) + 0.5)
    r = angle - turns * 1.5703125
    r = r - turns * 4.837512969970703125e-4
    r = r - turns * 7.54978995489188216e-8
    r2 = r * r
    s = r + r * r2 * (
        -1.6666654611e-1 + r2 * (8.3321608736e-3 + r2 * -1.9515295891e-4)
    )
    c = 1.0 - 0.5 * r2 + r2 * r2 * (
        4.166664568298827e-2 + r2 * (-1.388731625493765e-3 + r2 * 2.443315711809948e-5)
    )
    quad = turns.astype(jnp.int32)
    odd = (quad & 1) == 1
    sine = jnp.where(odd, c, s)
    cosine = jnp.where(odd, s, c)
    sine = jnp.where((quad & 2) == 2, -sine, sine)
    cosine = jnp.where(((quad + 1) & 2) == 2, -cosine, cosine)
    return sine, cosine


def lane_mask(shape, which):
    lanes = lax.broadcasted_iota(jnp.int32, shape, 1)
    return (lanes < HEAD) if which == 0 else (lanes >= HEAD)


def row_mask(shape, which):
    rows = lax.broadcasted_iota(jnp.int32, shape, 0)
    return (rows < HEAD) if which == 0 else (rows >= HEAD)


def keep(mask, x):
    return jnp.where(mask, x, jnp.zeros_like(x))


def attn_fwd_kernel(
    groups, which_page, pick, res, tok_ref, box_ref, freq_ref, wq_ref, wk_ref, wv_ref, bq_ref, bv_ref, wbt_ref, wo_ref,
    part_ref, p_ref, q_ref, k_ref, v_ref, ctx_ref, s_ref, c_ref, tok_t_ref, codes, mixed, acc, biases,
):
    step = pl.program_id(0)
    half = s_ref.shape[1]

    @pl.when(step == 0)
    def _():
        rows = s_ref.shape[0]
        lanes = lax.broadcasted_iota(jnp.int32, (rows, half), 1)
        level = res[pick[which_page]]
        width = (612 + 204 * level).astype(F32)
        height = (792 + 264 * level).astype(F32)
        corners = box_ref[...]
        centre_x = (corners[0:1] + corners[2:3]).astype(F32) * 500.0 / width
        centre_y = (corners[1:2] + corners[3:4]).astype(F32) * 500.0 / height
        both = jnp.concatenate([centre_x, centre_y, jnp.zeros((6, rows), F32)], axis=0).T
        centre = jnp.where(lanes < half // 2, both[:, 0:1], both[:, 1:2])
        sine, cosine = sin_cos(centre * freq_ref[...])
        s_ref[...] = sine
        c_ref[...] = cosine
        codes[:, :half] = cosine.astype(BF16)
        codes[:, half : 2 * half] = sine.astype(BF16)
        acc[...] = jnp.zeros_like(acc)
        biases[0:1] = bq_ref[...].astype(F32).reshape(1, -1)
        biases[1:2] = bv_ref[...].astype(F32).reshape(1, -1)
        tok_t = split_rows(tok_ref[...].T, groups)
        tok_t_ref[0] = tok_t[:half]
        tok_t_ref[1] = tok_t[half:]

    tok = tok_ref[...]
    rows = tok.shape[0]
    wide = wq_ref.shape[1]
    span = pl.ds(pl.multiple_of(step * wide, wide), wide)
    qkv = mm(tok, jnp.concatenate([wq_ref[...], wk_ref[...], wv_ref[...]], axis=1))
    q2 = (qkv[:, :wide] + biases[0:1, span]).astype(BF16) * BF16(0.125)
    k2 = qkv[:, wide : 2 * wide].astype(BF16)
    v2 = (qkv[:, 2 * wide :] + biases[1:2, span]).astype(BF16)
    q_ref[...] = q2
    k_ref[...] = k2
    v_ref[...] = v2
    codes[:, 2 * half :] = k2
    sine, cosine = s_ref[...], c_ref[...]
    for which in range(2):
        span = slice(which * rows, (which + 1) * rows)
        qm = keep(lane_mask(q2.shape, which), q2)
        off = mm(qm, wbt_ref[...])
        a, b = off[:, :half], off[:, half:]
        mixed[span, :half] = (a * sine + b * cosine).astype(BF16)
        mixed[span, half : 2 * half] = (b * sine - a * cosine).astype(BF16)
        mixed[span, 2 * half :] = qm
    parts = []
    for which in range(2):
        span = slice(which * rows, (which + 1) * rows)
        scores = mm_nt(mixed[span], codes[...])
        top = jnp.max(scores, axis=1, keepdims=True)
        raised = jnp.exp(scores - top)
        total = jnp.sum(raised, axis=1, keepdims=True)
        prob = (raised * (1.0 / total)).astype(BF16)
        p_ref[which] = prob
        parts.append(mm(prob, v2))
    ctx2 = jnp.where(lane_mask(parts[0].shape, 0), parts[0], parts[1]).astype(BF16)
    ctx_ref[...] = ctx2
    acc[...] += mm(ctx2, wo_ref[...])

    @pl.when(step == pl.num_programs(0) - 1)
    def _():
        part_ref[...] = acc[...].astype(BF16)


def attn_fwd(which_page, pick, res, tokens, boxes, freq, wq, wk, wv, bq, bv, wbt, wo, length, groups):
    dim = tokens.shape[1]
    inner = wq.shape[1]
    heads = inner // HEAD
    pairs = heads // 2
    wide = 2 * HEAD
    page = lambda i, pick, res: (pick[which_page], 0)
    fixed = lambda i, pick, res: (0, 0)
    cols = lambda i, pick, res: (0, i)
    rows = lambda i, pick, res: (i, 0)
    flops = 2 * length * (dim * inner * 4 + heads * (HEAD * dim + length * (dim + 2 * HEAD)))
    return pl.pallas_call(
        partial(attn_fwd_kernel, groups, which_page),
        grid_spec=pltpu.PrefetchScalarGridSpec(
            num_scalar_prefetch=2,
            grid=(pairs,),
            in_specs=[
                pl.BlockSpec((length, dim), page),
                pl.BlockSpec((4, length), lambda i, pick, res: (0, pick[which_page])),
                pl.BlockSpec((1, dim // 2), fixed),
                pl.BlockSpec((dim, wide), cols),
                pl.BlockSpec((dim, wide), cols),
                pl.BlockSpec((dim, wide), cols),
                pl.BlockSpec((inner,), lambda i, pick, res: (0,)),
                pl.BlockSpec((inner,), lambda i, pick, res: (0,)),
                pl.BlockSpec((wide, dim), rows),
                pl.BlockSpec((wide, dim), rows),
            ],
            out_specs=[
                pl.BlockSpec((length, dim), fixed),
                pl.BlockSpec((2, length, length), lambda i, pick, res: (i, 0, 0)),
                pl.BlockSpec((length, wide), cols),
                pl.BlockSpec((length, wide), cols),
                pl.BlockSpec((length, wide), cols),
                pl.BlockSpec((length, wide), cols),
                pl.BlockSpec((length, dim // 2), fixed),
                pl.BlockSpec((length, dim // 2), fixed),
                pl.BlockSpec((2, dim // 2, length), lambda i, pick, res: (0, 0, 0)),
            ],
            scratch_shapes=[
                pltpu.VMEM((length, dim + wide), BF16),
                pltpu.VMEM((2 * length, dim + wide), BF16),
                pltpu.VMEM((length, dim), F32),
                pltpu.VMEM((8, inner), F32),
            ],
        ),
        out_shape=[
            hbm((length, dim), BF16),
            hbm((heads, length, length), BF16),
            hbm((length, inner), BF16),
            hbm((length, inner), BF16),
            hbm((length, inner), BF16),
            hbm((length, inner), BF16),
            hbm((length, dim // 2), F32),
            hbm((length, dim // 2), F32),
            hbm((2, dim // 2, length), BF16),
        ],
        compiler_params=params(1),
        cost_estimate=cost(flops, 10e6, heads * length * length),
        name="attn_fwd",
    )(pick, res, tokens, boxes, freq, wq, wk, wv, bq, bv, wbt, wo)


def attn_bwd_kernel(groups, box_groups, first, pick, *refs):
    (df_ref, tok_t_ref, ctx_ref, wo_ref, q_ref, k_ref, v_ref, p_ref, s_ref, c_ref, wbt_ref,
     wq_ref, wk_ref, wv_ref, *refs) = refs
    if first:
        part_ref, small_ref, inp_ref, codes, acc, df_t = refs
    else:
        prev_ref, prev_small_ref, extra_ref, *refs = refs
        sent_ref, kept_ref, small_ref, inp_ref, codes, acc, df_t, grads = refs
    step = pl.program_id(0)
    half = s_ref.shape[1]

    @pl.when(step == 0)
    def _():
        codes[:, :half] = c_ref[...].astype(BF16)
        codes[:, half:] = s_ref[...].astype(BF16)
        acc[...] = jnp.zeros_like(acc)
        turned = split_rows(df_ref[...].T, groups)
        df_t[0] = turned[:half]
        df_t[1] = turned[half:]

    sine, cosine = s_ref[...], c_ref[...]
    q2, k2, v2 = q_ref[...], k_ref[...], v_ref[...]
    dctx = mm_nt(df_ref[...], wo_ref[...]).astype(BF16)
    dctx_t = dctx.T
    q_t = q2.T
    wbt = wbt_ref[...]
    dq = jnp.zeros(q2.shape, F32)
    dk_t, dv_t, dwb = [], [], []
    for which in range(2):
        low, high = which * HEAD, (which + 1) * HEAD
        dm = keep(lane_mask(dctx.shape, which), dctx)
        prob = p_ref[which]
        grad_probs = mm_nt(dm, v2)
        dv_t.append(mm(dctx_t[low:high], prob))
        wide_prob = prob.astype(F32)
        both = wide_prob * grad_probs
        inner = jnp.sum(both, axis=1, keepdims=True)
        ds = (both - wide_prob * inner).astype(BF16)
        dk_t.append(mm(q_t[low:high], ds))
        km = keep(lane_mask(k2.shape, which), k2)
        ga = mm(ds, codes[:, :half]).astype(BF16).astype(F32)
        gb = mm(ds, codes[:, half:]).astype(BF16).astype(F32)
        oa = (ga * sine - gb * cosine).astype(BF16)
        ob = (gb * sine + ga * cosine).astype(BF16)
        wm = keep(row_mask(wbt.shape, which), wbt)
        dq = dq + (mm(ds, km) + mm_nt(oa, wm[:, :half]) + mm_nt(ob, wm[:, half:]))
        dwb.append(jnp.concatenate([mm(q_t[low:high], oa), mm(q_t[low:high], ob)], axis=1))
    dq2 = (dq * 0.125).astype(BF16)
    dk2 = jnp.concatenate(dk_t, axis=0).T.astype(BF16)
    dv2 = jnp.concatenate(dv_t, axis=0).T.astype(BF16)
    sides = jnp.concatenate([dq2, dk2, dv2], axis=1)
    acc[...] += mm_nt(sides, jnp.concatenate([wq_ref[...], wk_ref[...], wv_ref[...]], axis=1))

    box = split_rows(jnp.concatenate(dwb, axis=0).T, box_groups)
    ctx2 = ctx_ref[...]
    zeros = jnp.zeros((1, 3 * q2.shape[1]), F32)
    small = jnp.concatenate(
        [column_sum(dq2.astype(F32)), column_sum(dv2.astype(F32)), zeros], axis=1
    )
    if not first:
        small = small + prev_small_ref[...]
    small_ref[...] = small
    for h in range(2):
        grad = jnp.concatenate(
            [mm(tok_t_ref[h], sides), mm(df_t[h], ctx2), box[h * half : (h + 1) * half]], axis=1
        )
        if first:
            part_ref[h] = grad.astype(BF16)
        else:
            grads[h] = (grad + prev_ref[h].astype(F32)).astype(BF16)
    if not first:
        sent_ref[:half] = grads[pick[3]]
        sent_ref[half:] = wide_tail(small)
        kept_ref[...] = grads[pick[2]]

    @pl.when(step == pl.num_programs(0) - 1)
    def _():
        rows = acc.shape[0]
        inp_ref[:rows] = acc[...].astype(BF16)
        if not first:
            inp_ref[rows:] = extra_ref[...]


def attn_bwd(pick, df, saved, wo, wbt, wq, wk, wv, groups, box_groups, prev=None, extra=None):
    prob, q, k, v, ctx, sine, cosine, tok_t = saved
    length, dim = df.shape
    inner = wq.shape[1]
    heads = inner // HEAD
    pairs = heads // 2
    wide = 2 * HEAD
    first = prev is None
    sent = length if first else 2 * length
    fixed = lambda i, pick: (0, 0)
    cols = lambda i, pick: (0, i)
    rows = lambda i, pick: (i, 0)
    block = lambda i, pick: (0, 0, i)
    flops = 2 * length * (dim * inner * 8 + heads * (3 * HEAD * dim + length * (dim + 4 * HEAD)))
    part = pl.BlockSpec((2, dim // 2, 5 * wide), block)
    small = pl.BlockSpec((1, 5 * wide), cols)
    small_shape = hbm((1, 5 * inner), F32)
    inp = pl.BlockSpec((sent, dim), fixed)
    inp_shape = hbm((sent, dim), BF16)
    scratch = [
        pltpu.VMEM((length, dim), BF16),
        pltpu.VMEM((length, dim), F32),
        pltpu.VMEM((2, dim // 2, length), BF16),
    ]
    if first:
        out_specs = [part, small, inp]
        out_shape = [hbm((2, dim // 2, 5 * inner), BF16), small_shape, inp_shape]
        more_specs, more = [], []
    else:
        out_specs = [
            pl.BlockSpec((dim // 2 + TAIL, 5 * wide), cols), pl.BlockSpec((dim // 2, 5 * wide), cols), small, inp,
        ]
        out_shape = [
            hbm((dim // 2 + TAIL, 5 * inner), BF16), hbm((dim // 2, 5 * inner), BF16), small_shape, inp_shape,
        ]
        more_specs, more = [part, small, pl.BlockSpec((length, dim), fixed)], [*prev, extra]
        scratch.append(pltpu.VMEM((2, dim // 2, 5 * wide), BF16))
    return pl.pallas_call(
        partial(attn_bwd_kernel, groups, box_groups, first),
        grid_spec=pltpu.PrefetchScalarGridSpec(
            num_scalar_prefetch=1,
            grid=(pairs,),
            in_specs=[
                pl.BlockSpec((length, dim), fixed),
                pl.BlockSpec((2, dim // 2, length), lambda i, pick: (0, 0, 0)),
                pl.BlockSpec((length, wide), cols),
                pl.BlockSpec((wide, dim), rows),
                pl.BlockSpec((length, wide), cols),
                pl.BlockSpec((length, wide), cols),
                pl.BlockSpec((length, wide), cols),
                pl.BlockSpec((2, length, length), lambda i, pick: (i, 0, 0)),
                pl.BlockSpec((length, dim // 2), fixed),
                pl.BlockSpec((length, dim // 2), fixed),
                pl.BlockSpec((wide, dim), rows),
                pl.BlockSpec((dim, wide), cols),
                pl.BlockSpec((dim, wide), cols),
                pl.BlockSpec((dim, wide), cols),
            ]
            + more_specs,
            out_specs=out_specs,
            scratch_shapes=scratch,
        ),
        out_shape=out_shape,
        compiler_params=params(1),
        cost_estimate=cost(flops, 14e6),
        name="attn_bwd",
    )(pick, df, tok_t, ctx, wo, q, k, v, prob, sine, cosine, wbt, wq, wk, wv, *more)


def split_rows(x_t, groups):
    return jnp.concatenate([x_t[start : start + count] for start, count in groups], axis=0)


def shard_groups(dim, shards):
    rows = dim // shards
    if not fast_path(dim, shards):
        return [(0, dim)]
    order = [z * 4 + x * 2 + c for c in range(2) for z in range(shards // 4) for x in range(2)]
    return [(block * rows, rows) for block in order]


def fast_path(dim, shards):
    return shards == 16 and (dim // shards) % 16 == 0


def gelu_parts(v):
    e = jnp.exp(v * v * -0.5)
    t = 1.0 / (1.0 + (0.3275911 * math.sqrt(0.5)) * jnp.abs(v))
    poly = t * (
        0.5 * 0.254829592
        + t * (0.5 * -0.284496736 + t * (0.5 * 1.421413741 + t * (0.5 * -1.453152027 + t * (0.5 * 1.061405429))))
    )
    tail = poly * e
    phi = jnp.where(v >= 0, 1.0 - tail, tail)
    return phi, phi + v * (e * (1.0 / math.sqrt(2.0 * math.pi)))


def norm_stats(hidden):
    centred = hidden - jnp.mean(hidden, axis=1, keepdims=True)
    variance = jnp.mean(centred * centred, axis=1, keepdims=True)
    inv = lax.rsqrt(variance + 1e-05)
    return centred * inv, inv


def norm_back(grad, scaled, inv):
    return inv * (
        grad
        - jnp.mean(grad, axis=1, keepdims=True)
        - scaled * jnp.mean(grad * scaled, axis=1, keepdims=True)
    )


def column_sum(x):
    return jnp.sum(x, axis=0, keepdims=True)


def ff_kernel(
    groups, pick, tok_ref, part_ref, got_ref, gout_ref, bo_ref, g1_ref, b1_ref, bb_ref, g2_ref, b2_ref,
    bi_here, bi_there,
    wi_here, wb_here, wi0, wi1, wi2, wi3, wb0, wb1, wb2, wb3,
    out_ref, df_ref, lhs_ref, rhs_ref, small_ref,
    wi, wb, slope, norm_low, grad_low, acc, wide, bi_ref, sems,
):
    blocks, dim, cols = wi.shape
    here = blocks // 2
    piece = cols // 2
    remote = [(wi0, wb0), (wi1, wb1), (wi2, wb2), (wi3, wb3)]
    for p in range(2 * blocks):
        if p < blocks:
            at = (p % 2) * piece
            span = pl.ds(at, piece)
            source = (wi_here.at[:, pl.ds(p * piece, piece)], wb_here.at[pl.ds(p * piece, piece), :])
        else:
            span = pl.ds(pl.multiple_of(((pick[6] ^ p) & 1) * piece, piece), piece)
            source = remote[p - blocks]
            slot = here + ((((pick[8] ^ p) & 3) >> 1) ^ pick[7])
            span_back = pl.ds(pl.multiple_of(((pick[8] ^ p) & 1) * piece, piece), piece)
        pltpu.make_async_copy(source[0], wi.at[p // 2, :, span], sems.at[0, p]).start()
        if p < blocks:
            pltpu.make_async_copy(source[1], wb.at[p // 2, span, :], sems.at[1, p // 2]).start()
        else:
            pltpu.make_async_copy(source[1], wb.at[slot, span_back, :], sems.at[1, slot]).start()

    def vec(ref):
        return ref[...].astype(F32).reshape(1, -1)

    here_at, there_at = pick[0] * here, pick[1] * here
    bias_here, bias_there = vec(bi_here), vec(bi_there)
    for j in range(here):
        bi_ref[pl.ds(here_at + j, 1), :] = bias_here[:, j * cols : (j + 1) * cols]
        bi_ref[pl.ds(there_at + j, 1), :] = bias_there[:, j * cols : (j + 1) * cols]

    def place(j):
        return jnp.where(j < here, here_at + j, there_at + (pick[7] ^ (j - here)))

    bo, g1, b1, bb, g2, b2 = (vec(r) for r in (bo_ref, g1_ref, b1_ref, bb_ref, g2_ref, b2_ref))
    first_sum = (
        tok_ref[...].astype(F32)
        + (part_ref[...].astype(F32) + got_ref[...].astype(F32))
        + bo
    )
    scaled1, inv1 = norm_stats(first_sum)
    normed = scaled1 * g1 + b1
    low = normed.astype(BF16)
    norm_low[...] = low
    wide[...] = normed + bb
    acc[...] = jnp.zeros_like(acc)
    low_t = split_rows(low.T, groups)
    split = low_t.shape[0] // 2
    lhs_ref[0, 0] = low_t[:split]
    lhs_ref[1, 0] = low_t[split:]

    def forward(j, _):
        for p in range(2):
            pltpu.make_async_copy(wi0, wi.at[j, :, pl.ds(0, piece)], sems.at[0, 2 * j + p]).wait()
        pltpu.make_async_copy(wb.at[j], wb.at[j], sems.at[1, j]).wait()
        pre = mm(norm_low[...], wi[j]) + bi_ref[pl.ds(place(j), 1), :]
        phi, step = gelu_parts(pre)
        act = (pre * phi).astype(BF16)
        rhs_ref[1, j] = act
        slope[j] = step
        acc[...] += mm(act, wb[j])
        return 0

    lax.fori_loop(0, blocks, forward, 0)
    scaled2, inv2 = norm_stats(wide[...] + acc[...])
    out_ref[...] = (scaled2 * g2 + b2).astype(BF16)
    gout = gout_ref[...].astype(F32)
    small_gain2 = column_sum(gout * scaled2)
    small_bias2 = column_sum(gout)
    grad_second = norm_back(gout * g2, scaled2, inv2)
    small_back = column_sum(grad_second)
    low2 = grad_second.astype(BF16)
    grad_low[...] = low2
    low2_t = split_rows(low2.T, groups)
    lhs_ref[0, 1] = low2_t[:split]
    lhs_ref[1, 1] = low2_t[split:]
    acc[...] = grad_second

    def backward(j, _):
        grad_act = mm_nt(grad_low[...], wb[j]).astype(BF16).astype(F32)
        grad_pre = (grad_act * slope[j]).astype(BF16)
        rhs_ref[0, j] = grad_pre
        bi_ref[pl.ds(place(j), 1), :] = column_sum(grad_pre.astype(F32))
        acc[...] += mm_nt(grad_pre, wi[j])
        return 0

    lax.fori_loop(0, blocks, backward, 0)
    grad_normed = acc[...]
    first_sum = (
        tok_ref[...].astype(F32)
        + (part_ref[...].astype(F32) + got_ref[...].astype(F32))
        + bo
    )
    scaled1, inv1 = norm_stats(first_sum)
    small_gain1 = column_sum(grad_normed * scaled1)
    small_bias1 = column_sum(grad_normed)
    grad_first = norm_back(grad_normed * g1, scaled1, inv1)
    small_out = column_sum(grad_first)
    df_ref[...] = grad_first.astype(BF16)
    small_ref[...] = jnp.concatenate(
        [
            jnp.concatenate([small_gain2, small_bias2], axis=1),
            jnp.concatenate([small_back, small_gain1], axis=1),
            jnp.concatenate([small_bias1, small_out], axis=1),
            jnp.concatenate([bi_ref[j : j + 1] for j in range(here)], axis=1),
            jnp.concatenate([bi_ref[j : j + 1] for j in range(here, blocks)], axis=1),
            jnp.zeros((3, 2 * dim), F32),
        ],
        axis=0,
    )


def feed_forward(pick, tokens, part, got, grad_out, rows, bias_in, bias_there, wi_here, wb_here, wi_pieces, wb_pieces, groups):
    length, dim = part.shape
    cols = 2 * wi_pieces[0].shape[1]
    blocks = 2 * wi_here.shape[1] // cols
    page = lambda i, pick: (pick[0], 0)
    fixed = lambda i, pick: (0, 0)
    row = pl.BlockSpec((dim,), lambda i, pick: (0,))
    bias_row = pl.BlockSpec(bias_in.shape, lambda i, pick: (0,))
    whole = pl.BlockSpec((length, dim), fixed)
    anywhere = pl.BlockSpec(memory_space=pl.ANY)
    hidden = blocks * cols
    return pl.pallas_call(
        partial(ff_kernel, groups),
        grid_spec=pltpu.PrefetchScalarGridSpec(
            num_scalar_prefetch=1,
            grid=(1,),
            in_specs=[
                pl.BlockSpec((length, dim), page),
                whole,
                whole,
                pl.BlockSpec((length, dim), page),
                row, row, row, row, row, row,
                bias_row, bias_row,
            ]
            + [anywhere] * 10,
            out_specs=[
                whole,
                whole,
                pl.BlockSpec((2, 2, dim // 2, length), lambda i, pick: (0, 0, 0, 0)),
                pl.BlockSpec((2, blocks, length, cols), lambda i, pick: (0, 0, 0, 0)),
                pl.BlockSpec((8, 2 * dim), fixed),
            ],
            scratch_shapes=[
                pltpu.VMEM((blocks, dim, cols), BF16),
                pltpu.VMEM((blocks, cols, dim), BF16),
                pltpu.VMEM((blocks, length, cols), F32),
                pltpu.VMEM((length, dim), BF16),
                pltpu.VMEM((length, dim), BF16),
                pltpu.VMEM((length, dim), F32),
                pltpu.VMEM((length, dim), F32),
                pltpu.VMEM((blocks, cols), F32),
                pltpu.SemaphoreType.DMA((2, 2 * blocks)),
            ],
        ),
        out_shape=[
            hbm((length, dim), BF16),
            hbm((length, dim), BF16),
            hbm((2, 2, dim // 2, length), BF16),
            hbm((2, blocks, length, cols), BF16),
            hbm((8, 2 * dim), F32),
        ],
        compiler_params=params(1),
        cost_estimate=cost(8 * length * dim * hidden, 4 * dim * hidden + 8 * length * hidden, length * hidden),
        name="feed_forward",
    )(pick, tokens, part, got, grad_out, *rows, bias_in, bias_there, wi_here, wb_here, *wi_pieces, *wb_pieces)


TAIL = 16


def split2(x):
    high = x.astype(BF16)
    return high, (x - high.astype(F32)).astype(BF16)


def rounded(x):
    high, low = split2(x)
    return high.astype(F32) + low.astype(F32)


def tall(x):
    return jnp.concatenate([x, jnp.zeros((TAIL - x.shape[0],) + x.shape[1:], x.dtype)], axis=0)


def ff_send_kernel(pick, lhs_ref, rhs_ref, small_ref, out_ref):
    rows = lhs_ref.shape[2]
    for m in range(2):
        out_ref[m, :rows] = mm(lhs_ref[0, m], rhs_ref[m, 0]).astype(BF16)
    for m, term in enumerate(split2(small_ref[...])):
        out_ref[m, rows:] = tall(term)


def ff_keep_kernel(pick, lhs_ref, rhs_ref, got_ref, small_ref, xs_ref, xk_ref, small_out, acc):
    rows = lhs_ref.shape[2]
    shard = acc.shape[0] // 8
    x_index = pick[4]
    for m in range(2):
        acc[...] = mm(lhs_ref[0, m], rhs_ref[m, 0]) + got_ref[m, :rows].astype(F32)
        for z in range(4):
            away = pl.multiple_of((2 * z + 1 - x_index) * shard, 8)
            mine = pl.multiple_of((2 * z + x_index) * shard, 8)
            xs_ref[m, z * shard : (z + 1) * shard] = acc[pl.ds(away, shard), :].astype(BF16)
            xk_ref[m, z * shard : (z + 1) * shard] = acc[pl.ds(mine, shard), :].astype(BF16)
    small = rounded(small_ref[...]) + (got_ref[0, rows : rows + 8].astype(F32) + got_ref[1, rows : rows + 8].astype(F32))
    small_out[...] = small
    for m, term in enumerate(split2(small)):
        xs_ref[m, 4 * shard :] = tall(term)


def ff_grad(pick, lhs, rhs, small, remote, got=None):
    _, mats, rows, length = lhs.shape
    _, blocks, _, cols = rhs.shape
    half = blocks // 2
    base = half if remote else 0
    which = 2 if got is not None else 3
    dest = (lambda j, pick: j ^ pick[7]) if remote else (lambda j, pick: j)
    column = lambda height: pl.BlockSpec((2, height, cols), lambda j, pick: (0, 0, dest(j, pick)))
    small_spec = pl.BlockSpec((8, cols), lambda j, pick: (0, dest(j, pick)))
    in_specs = [
        pl.BlockSpec((1, mats, rows, length), lambda j, pick: (pick[which], 0, 0, 0)),
        pl.BlockSpec((2, 1, length, cols), lambda j, pick: (0, base + j, 0, 0)),
    ]
    wide = half * cols
    estimate = cost(2 * mats * rows * length * wide, 10e6)
    if got is None:
        return pl.pallas_call(
            ff_send_kernel,
            grid_spec=pltpu.PrefetchScalarGridSpec(
                num_scalar_prefetch=1,
                grid=(half,),
                in_specs=in_specs + [small_spec],
                out_specs=column(rows + TAIL),
            ),
            out_shape=hbm((2, rows + TAIL, wide), BF16),
            compiler_params=params(1),
            cost_estimate=estimate,
            name="ff_grad_send",
        )(pick, lhs, rhs, small)
    return pl.pallas_call(
        ff_keep_kernel,
        grid_spec=pltpu.PrefetchScalarGridSpec(
            num_scalar_prefetch=1,
            grid=(half,),
            in_specs=in_specs + [column(rows + TAIL), small_spec],
            out_specs=[column(rows // 2 + TAIL), column(rows // 2), small_spec],
            scratch_shapes=[pltpu.VMEM((rows, cols), F32)],
        ),
        out_shape=[
            hbm((2, rows // 2 + TAIL, wide), BF16),
            hbm((2, rows // 2, wide), BF16),
            hbm((8, wide), F32),
        ],
        compiler_params=params(1),
        cost_estimate=estimate,
        name="ff_grad_keep",
    )(pick, lhs, rhs, got, small)


def wide_tail(vector):
    high, low = split2(vector)
    return tall(jnp.concatenate([high, low], axis=0))


def attn_split_kernel(pick, kept_ref, got_ref, small_ref, xs_ref, xk_ref, small_out, acc):
    rows = kept_ref.shape[0]
    acc[...] = kept_ref[...].astype(F32) + got_ref[:rows].astype(F32)
    x_index = pick[4]
    shard = rows // 8
    for z in range(4):
        away = pl.multiple_of((2 * z + 1 - x_index) * shard, 8)
        mine = pl.multiple_of((2 * z + x_index) * shard, 8)
        xs_ref[0, z * shard : (z + 1) * shard] = acc[pl.ds(away, shard), :].astype(BF16)
        xk_ref[0, z * shard : (z + 1) * shard] = acc[pl.ds(mine, shard), :].astype(BF16)
    small = rounded(small_ref[...]) + (
        got_ref[rows : rows + 1].astype(F32) + got_ref[rows + 1 : rows + 2].astype(F32)
    )
    small_out[...] = jnp.concatenate([small, jnp.zeros((7, small.shape[1]), F32)], axis=0)
    xs_ref[0, 4 * shard :] = wide_tail(small)


def attn_split(pick, kept, got, small):
    rows, cols = kept.shape
    steps = 3
    column = lambda height: pl.BlockSpec((height, cols // steps), lambda i, pick: (0, i))
    deep = lambda height: pl.BlockSpec((1, height, cols // steps), lambda i, pick: (0, 0, i))
    return pl.pallas_call(
        attn_split_kernel,
        grid_spec=pltpu.PrefetchScalarGridSpec(
            num_scalar_prefetch=1,
            grid=(steps,),
            in_specs=[column(rows), column(rows + TAIL), column(1)],
            out_specs=[deep(rows // 2 + TAIL), deep(rows // 2), column(8)],
            scratch_shapes=[pltpu.VMEM((rows, cols // steps), F32)],
        ),
        out_shape=[
            hbm((1, rows // 2 + TAIL, cols), BF16),
            hbm((1, rows // 2, cols), BF16),
            hbm((8, cols), F32),
        ],
        compiler_params=params(1),
        cost_estimate=cost(kept.size, 6 * kept.size),
        name="attn_split",
    )(pick, kept, got, small)


def tail_sum(ref, at):
    if ref.shape[0] == 2:
        return ref[0, at : at + 8].astype(F32) + ref[1, at : at + 8].astype(F32)
    one = ref[0, at : at + 1].astype(F32) + ref[0, at + 1 : at + 2].astype(F32)
    return jnp.concatenate([one, jnp.zeros((7, one.shape[1]), F32)], axis=0)


def put_tail(ref, at, small):
    if ref.shape[0] == 2:
        for m, term in enumerate(split2(small)):
            ref[m, at:] = tall(term)
    else:
        ref[0, at:] = wide_tail(small[0:1])


def add_x_kernel(tailed, pick, keep_ref, got_ref, small_ref, own, s1, s2, s3, *rest):
    shard = own.shape[1]
    z = pick[5]
    if tailed:
        small = rounded(small_ref[...]) + tail_sum(got_ref, 4 * shard)
        rest[0][...] = small
    for d, ref in enumerate((own, s1, s2, s3)):
        at = pl.multiple_of((z ^ d) * shard, 16)
        ref[:, :shard] = (
            keep_ref[:, pl.ds(at, shard), :].astype(F32) + got_ref[:, pl.ds(at, shard), :].astype(F32)
        ).astype(BF16)
        if d and tailed:
            put_tail(ref, shard, small)


def add_x(pick, kept, got, small, tailed):
    mats, rows, cols = kept.shape
    shard = rows // 4
    own = hbm((mats, shard, cols), BF16)
    sent = hbm((mats, shard + (TAIL if tailed else 0), cols), BF16)
    full = lambda s: pl.BlockSpec(s.shape, lambda i, pick: (0,) * len(s.shape))
    extra = [hbm(small.shape, F32)] if tailed else []
    return pl.pallas_call(
        partial(add_x_kernel, tailed),
        grid_spec=pltpu.PrefetchScalarGridSpec(
            num_scalar_prefetch=1,
            grid=(1,),
            in_specs=[full(kept), full(got), full(small)],
            out_specs=[full(own)] + [full(sent)] * 3 + [full(s) for s in extra],
        ),
        out_shape=[own] + [sent] * 3 + extra,
        compiler_params=params(1),
        cost_estimate=cost(kept.size, 6 * kept.size),
        name="add_x",
    )(pick, kept, got, small)


def sum4(own, r1, r2, r3):
    return (own.astype(F32) + r1.astype(F32)) + (r2.astype(F32) + r3.astype(F32))


def small4(small_ref, others, at):
    terms = [tail_sum(r, at) for r in others]
    return (rounded(small_ref[...]) + terms[0]) + (terms[1] + terms[2])


def add_z_kernel(own, r1, r2, r3, small_ref, out, small_out):
    shard = own.shape[1]
    out[:, :shard] = sum4(own[...], r1[:, :shard], r2[:, :shard], r3[:, :shard]).astype(BF16)
    small = small4(small_ref, (r1, r2, r3), shard)
    small_out[...] = small
    put_tail(out, shard, small)


def add_z(blocks, small):
    return pl.pallas_call(
        add_z_kernel,
        out_shape=[
            hbm(blocks[1].shape, BF16),
            hbm(small.shape, F32),
        ],
        compiler_params=pltpu.CompilerParams(vmem_limit_bytes=VMEM_LIMIT),
        cost_estimate=cost(4 * blocks[0].size, 10 * blocks[0].size),
        name="add_z",
    )(*blocks, small)


def ff_last_kernel(pick, own, r1, r2, r3, got, small_ref, in_out, back_out, *vectors):
    small_out = vectors[-1]
    shard = own.shape[1]
    in_out[...] = sum4(own[0], r1[0], r2[0], r3[0]) + got[0, :shard].astype(F32)
    back_out[...] = sum4(own[1], r1[1, :shard], r2[1, :shard], r3[1, :shard]) + got[1, :shard].astype(F32)
    small = rounded(small_ref[...]) + tail_sum(got, shard)
    small_out[...] = small
    dim = small.shape[1] // 2
    for i in range(6):
        vectors[i][...] = small[i // 2 : i // 2 + 1, (i % 2) * dim : (i % 2 + 1) * dim].reshape(dim)
    vectors[6][...] = small_out[pl.ds(3 + pick[0], 1), :].reshape(2 * dim)


def ff_last(pick, blocks, got, small):
    _, rows, cols = blocks[0].shape
    dim = cols // 2
    full = lambda s: pl.BlockSpec(s.shape, lambda i, pick: (0,) * len(s.shape))
    out_shape = (
        [hbm((rows, cols), F32)] * 2
        + [hbm((dim,), F32)] * 6
        + [hbm((cols,), F32)]
    )
    return pl.pallas_call(
        ff_last_kernel,
        grid_spec=pltpu.PrefetchScalarGridSpec(
            num_scalar_prefetch=1,
            grid=(1,),
            in_specs=[full(b) for b in blocks] + [full(got), full(small)],
            out_specs=[full(s) for s in out_shape],
            scratch_shapes=[pltpu.VMEM(small.shape, F32)],
        ),
        out_shape=out_shape,
        compiler_params=params(1),
        cost_estimate=cost(10 * got.size, 20 * got.size),
        name="ff_last",
    )(pick, *blocks, got, small)


def attn_last_kernel(own, r1, r2, r3, small_ref, q_out, k_out, v_out, box_out, wo_out, bq_out, bv_out):
    shard = own.shape[1]
    wide = 2 * HEAD
    pairs = q_out.shape[1] // wide
    small = small4(small_ref, (r1, r2, r3), shard)
    for p in range(pairs):
        at = slice(p * wide, (p + 1) * wide)
        for i, ref in enumerate((q_out, k_out, v_out, wo_out, box_out)):
            span = slice((5 * p + i) * wide, (5 * p + i + 1) * wide)
            ref[:, at] = sum4(own[0, :, span], r1[0, :shard, span], r2[0, :shard, span], r3[0, :shard, span])
    for i, ref in enumerate((bq_out, bv_out)):
        row = [small[0:1, (5 * p + i) * wide : (5 * p + i + 1) * wide] for p in range(pairs)]
        ref[...] = jnp.concatenate(row, axis=1).reshape(pairs * wide)


def attn_last(blocks, small):
    _, rows, cols = blocks[0].shape
    cols = cols // 5
    flat = hbm((rows, cols), F32)
    vector = hbm((cols,), F32)
    return pl.pallas_call(
        attn_last_kernel,
        out_shape=[flat] * 5 + [vector, vector],
        compiler_params=pltpu.CompilerParams(vmem_limit_bytes=VMEM_LIMIT),
        cost_estimate=cost(4 * blocks[0].size, 12 * blocks[0].size),
        name="attn_last",
    )(*blocks, small)


def place_grad_kernel(pick, df_ref, a_ref, b_ref, *refs):
    refs[-1][...] = df_ref[...].astype(F32) + (a_ref[...].astype(F32) + b_ref[...].astype(F32))


def place_grad(which, pick, df, mine, got, pages, into=None):
    length, dim = df.shape
    steps = 2
    part = pl.BlockSpec((length // steps, dim), lambda i, pick: (i, 0))
    args = [df, mine, got] + ([] if into is None else [into])
    return pl.pallas_call(
        place_grad_kernel,
        grid_spec=pltpu.PrefetchScalarGridSpec(
            num_scalar_prefetch=1,
            grid=(steps,),
            in_specs=[part] * 3 + ([] if into is None else [pl.BlockSpec(memory_space=pl.ANY)]),
            out_specs=pl.BlockSpec((length // steps, dim), lambda i, pick: (pick[which] * steps + i, 0)),
        ),
        out_shape=hbm((pages * length, dim), F32),
        input_output_aliases={} if into is None else {4: 0},
        compiler_params=params(1),
        cost_estimate=cost(3 * df.size, 10 * df.size),
        name="place_grad",
    )(pick, *args)


def place_output_kernel(pick, a_ref, b_ref, out_ref):
    length = a_ref.shape[0]
    own = pl.multiple_of(pick[0] * length, length)
    other = pl.multiple_of(pick[1] * length, length)
    out_ref[pl.ds(own, length), :] = a_ref[...]
    out_ref[pl.ds(other, length), :] = b_ref[...]


def place_output(pick, mine, got):
    length, dim = mine.shape
    whole = pl.BlockSpec((length, dim), lambda i, pick: (0, 0))
    return pl.pallas_call(
        place_output_kernel,
        grid_spec=pltpu.PrefetchScalarGridSpec(
            num_scalar_prefetch=1,
            grid=(1,),
            in_specs=[whole, pl.BlockSpec((length, dim), lambda i, pick: (1, 0))],
            out_specs=pl.BlockSpec((2 * length, dim), lambda i, pick: (0, 0)),
        ),
        out_shape=hbm((2 * length, dim), BF16),
        compiler_params=params(1),
        cost_estimate=cost(mine.size, 8 * mine.size),
        name="place_output",
    )(pick, mine, got)


def swap_perm(size, flip):
    return [(i, i ^ flip) for i in range(size)]


def encoding_rows(w_box):
    rows, cols = w_box.shape
    quarters = w_box.reshape(4, rows // 4, cols)
    return jnp.concatenate([quarters[i] for i in (0, 2, 1, 3)], axis=0)


def encoding_groups(groups, dim):
    quarter = dim // 4
    place = (0, 2, 1, 3)
    out = []
    for start, count in groups:
        while count:
            size = min(count, quarter - start % quarter)
            out.append((place[start // quarter] * quarter + start % quarter, size))
            start, count = start + size, count - size
    return out


def shards(
    shards_dp,
    tokens,
    boxes,
    resolution,
    w_query,
    bias_query,
    w_key,
    w_value,
    bias_value,
    w_box,
    w_out,
    bias_out,
    norm1_gain,
    norm1_bias,
    w_in,
    bias_in,
    w_back,
    bias_back,
    norm2_gain,
    norm2_bias,
    grad_out,
):
    dim = tokens.shape[1]
    pages = resolution.shape[0]
    length = tokens.shape[0] // pages
    hidden = w_in.shape[1]
    piece = hidden // 4
    here = lax.axis_index("head").astype(jnp.int32)
    spot = lax.axis_index("dp").astype(jnp.int32)
    core, x_index, z_index, corner = spot % 2, (spot // 2) % 2, spot // 4, spot % 4
    corner_z = (z_index % 2) * 2 + core
    pick = jnp.stack([here, 1 - here, core, 1 - core, x_index, z_index, corner, corner // 2, corner_z])
    groups = shard_groups(dim, shards_dp)
    fast = fast_path(dim, shards_dp)

    def over_head(value):
        return lax.ppermute(value, "head", [(0, 1), (1, 0)])

    def over_dp(value, flip):
        return lax.ppermute(value, "dp", swap_perm(shards_dp, flip))

    def after(value, *others):
        return lax.optimization_barrier((value, others))[0]

    in_first = over_head(lax.dynamic_slice_in_dim(w_in, corner * piece, piece, 1))
    back_first = over_head(lax.dynamic_slice_in_dim(w_back, corner_z * piece, piece, 0))
    bias_there = over_head(bias_in)

    quarter = w_box.shape[0] // 4
    freqs = np.exp(np.arange(quarter, dtype=np.float32) * np.float32(-math.log(10000.0) / quarter))
    freqs = jnp.asarray(np.concatenate([freqs, freqs])[None, :])
    box_t = encoding_rows(w_box).T

    def attend(which, tok):
        return attn_fwd(
            which, pick, resolution, tok, boxes, freqs, w_query, w_key, w_value, bias_query, bias_value,
            box_t, w_out, length, groups,
        )

    part_other, *saved_other = attend(1, tokens)
    got = over_head(part_other)
    in_first, back_first = after((in_first, back_first), part_other)
    in_second, back_second = over_dp(in_first, 2), over_dp(back_first, 4)
    in_near, back_near = over_dp(in_first, 1), over_dp(back_first, 1)
    part_own, *saved_own = attend(0, after(tokens, part_other))
    in_second, back_second = after((in_second, back_second), part_own)
    in_pieces = [in_first, in_near, in_second, over_dp(in_second, 1)]
    back_pieces = [back_first, back_near, back_second, over_dp(back_second, 1)]

    out_own, df_own, lhs, rhs, small = feed_forward(
        pick, tokens, part_own, got, grad_out,
        (bias_out, norm1_gain, norm1_bias, bias_back, norm2_gain, norm2_bias),
        bias_in, bias_there, w_in, w_back, in_pieces, back_pieces, groups,
    )
    df_other = over_head(df_own)
    box_groups = encoding_groups(groups, w_box.shape[0])

    def attend_back(df, saved, prev=None, extra=None, pick=pick):
        return attn_bwd(
            pick, df, saved, w_out, box_t, w_query, w_key, w_value, groups, box_groups, prev, extra
        )

    if fast:
        sent_a = ff_grad(pick, lhs, rhs, small, True)
        got_a = over_dp(sent_a, 1)
        sent_b = ff_grad(pick, lhs, after(rhs, sent_a), small, False)
        got_b = over_dp(sent_b, 1)
        xs_a, xk_a, small_1 = ff_grad(pick, lhs, after(rhs, sent_b), small, True, got_a)
        xg_a = over_dp(xs_a, 2)
        got_b = after(got_b, xs_a)
        xs_b, xk_b, small_b = ff_grad(pick, lhs, after(rhs, xs_a), small, False, got_b)
        df_own = after(df_own, xs_b)
    *part_a, inp_own = attend_back(df_own, saved_own)
    inp_own_got = over_head(inp_own)

    if fast:
        xg_a, df_other, xs_b = after((xg_a, df_other, xs_b), inp_own)
        xg_b = over_dp(xs_b, 2)
        *z_a, small_2 = add_x(pick, xk_a, after(xg_a, df_other), small_1, True)
        zg_a = [z_a[0]] + [over_dp(z_a[d], 4 * d) for d in (1, 2, 3)]
        df_other = after(df_other, z_a[0])

    pick_back = pick if fast else pick.at[2:4].set(jnp.arange(2, dtype=jnp.int32))
    sent, kept, a_small, inp_other = attend_back(df_other, saved_other, part_a, out_own, pick_back)
    inp_other_got = over_head(inp_other)

    if fast:
        xg_b, zg_a, inp_own_got = after((xg_b, zg_a, inp_own_got), inp_other)
        sent, xk_b = after((sent, xk_b), xg_b, zg_a, inp_own_got)
        sent_got = over_dp(sent, 1)
        z_b = add_x(pick, xk_b, xg_b, small_b, False)
        a_sum, small_3 = add_z([after(zg_a[0], z_b[0])] + zg_a[1:], small_2)
        xs, xk, a_small = attn_split(pick, kept, after(sent_got, a_sum), a_small)
        xg = over_dp(xs, 2)
        z_b = after(z_b, xs)
        zg_b = [z_b[0]] + [over_dp(z_b[d], 4 * d) for d in (1, 2, 3)]
        grad_input = place_grad(1, pick, after(df_other, xs), inp_other, inp_own_got, pages)
        *blocks, a_small = add_x(pick, after(xk, grad_input), xg, a_small, True)
        zg_b = after(zg_b, blocks)
        blocks, a_sum, df_own = after((blocks, a_sum, df_own), zg_b)
        blocks = [blocks[0]] + [over_dp(blocks[d], 4 * d) for d in (1, 2, 3)]
        a_sum = over_head(a_sum)
        grad_input = place_grad(0, pick, df_own, inp_own, inp_other_got, pages, grad_input)
        grad_in, grad_back, n2g, n2b, bias_back_sum, n1g, n1b, bias_out_sum, bias_in_sum = ff_last(
            pick, after(zg_b, grad_input), a_sum, small_3
        )
        output = place_output(pick, after(out_own, grad_in), inp_other_got)
        blocks = after(blocks, output)
        grad_q, grad_k, grad_v, grad_box, grad_wo, bq_sum, bv_sum = attn_last(blocks, a_small)
        grad_back, grad_wo = grad_back.T, grad_wo.T
    else:
        scatter = lambda value, axis: lax.psum_scatter(
            value.astype(F32), "dp", scatter_dimension=axis, tiled=True
        )
        cores = [pick.at[3].set(c) for c in (0, 1)]
        halves = [
            scatter(
                jnp.concatenate([ff_grad(p, lhs, rhs, small, remote)[:, : dim // 2] for p in cores], axis=1), 1
            )
            for remote in (True, False)
        ]
        total = halves[1] + over_head(halves[0])
        grad_in, grad_back = total[0], total[1].T
        total = scatter(jnp.concatenate([kept, sent[: dim // 2]], axis=0), 0)
        total = total.reshape(total.shape[0], -1, 5, 2 * HEAD).transpose(2, 0, 1, 3)
        grad_q, grad_k, grad_v, grad_wo, grad_box = total.reshape(5, total.shape[1], -1)
        grad_wo = grad_wo.T
        small = lax.psum(small, ("dp", "head"))
        n2g, n2b, bias_back_sum, n1g, n1b, bias_out_sum = small[:3].reshape(6, dim)
        bias_in_sum = lax.dynamic_index_in_dim(small, 3 + here, 0, keepdims=False)
        bq_sum, bv_sum = lax.psum(a_small, "dp").reshape(-1, 5, 2 * HEAD)[:, :2].transpose(1, 0, 2).reshape(2, -1)
        output = place_output(pick, out_own, inp_other_got)
        grad_input = place_grad(1, pick, df_other, inp_other, inp_own_got, pages)
        grad_input = place_grad(0, pick, df_own, inp_own, inp_other_got, pages, grad_input)
    return (
        output,
        grad_input,
        grad_q,
        bq_sum,
        grad_k,
        grad_v,
        bv_sum,
        grad_box,
        grad_wo,
        bias_out_sum,
        n1g,
        n1b,
        grad_in,
        bias_in_sum,
        grad_back,
        bias_back_sum,
        n2g,
        n2b,
    )


def solution(mesh):
    placed = (
        P("dp", None),
        P(None, "dp"),
        P("dp"),
        P(None, "head"),
        P("head"),
        P(None, "head"),
        P(None, "head"),
        P("head"),
        P(None, "head"),
        P("head", None),
        P(),
        P(),
        P(),
        P(None, "head"),
        P("head"),
        P("head", None),
        P(),
        P(),
        P(),
        P("dp", None),
    )
    return jax.shard_map(
        partial(shards, mesh.shape["dp"]),
        mesh=mesh,
        in_specs=placed,
        out_specs=(
            P("dp", None),
            P("dp", None),
            P("dp", "head"),
            P("head"),
            P("dp", "head"),
            P("dp", "head"),
            P("head"),
            P("dp", "head"),
            P("head", "dp"),
            P(),
            P(),
            P(),
            P("dp", "head"),
            P("head"),
            P("head", "dp"),
            P(),
            P(),
            P(),
        ),
        check_vma=False,
    )
```

```python
from functools import partial
import math

import jax
import numpy as np
import jax.numpy as jnp
from jax import lax
from jax.experimental import pallas as pl
from jax.experimental.pallas import tpu as pltpu
from jax.sharding import PartitionSpec as P

HEAD = 64
F32 = jnp.float32
BF16 = jnp.bfloat16
VMEM_LIMIT = 63 * 1024 * 1024


def hbm(shape, dtype):
    return pltpu.HBM(tuple(shape), dtype)


def mm(a, b):
    return jnp.dot(a, b, preferred_element_type=F32)


def mm_nt(a, b):
    return lax.dot_general(a, b, (((1,), (1,)), ((), ())), preferred_element_type=F32)


def params(steps):
    return pltpu.CompilerParams(
        dimension_semantics=("arbitrary",) * steps, vmem_limit_bytes=VMEM_LIMIT
    )


def cost(flops, nbytes, trans=0):
    return pl.CostEstimate(flops=int(flops), bytes_accessed=int(nbytes), transcendentals=int(trans))


def sin_cos(angle):
    turns = jnp.floor(angle * (2.0 / math.pi) + 0.5)
    r = angle - turns * 1.5703125
    r = r - turns * 4.837512969970703125e-4
    r = r - turns * 7.54978995489188216e-8
    r2 = r * r
    s = r + r * r2 * (
        -1.6666654611e-1 + r2 * (8.3321608736e-3 + r2 * -1.9515295891e-4)
    )
    c = 1.0 - 0.5 * r2 + r2 * r2 * (
        4.166664568298827e-2 + r2 * (-1.388731625493765e-3 + r2 * 2.443315711809948e-5)
    )
    quad = turns.astype(jnp.int32)
    odd = (quad & 1) == 1
    sine = jnp.where(odd, c, s)
    cosine = jnp.where(odd, s, c)
    sine = jnp.where((quad & 2) == 2, -sine, sine)
    cosine = jnp.where(((quad + 1) & 2) == 2, -cosine, cosine)
    return sine, cosine


def lane_mask(shape, which):
    lanes = lax.broadcasted_iota(jnp.int32, shape, 1)
    return (lanes < HEAD) if which == 0 else (lanes >= HEAD)


def row_mask(shape, which):
    rows = lax.broadcasted_iota(jnp.int32, shape, 0)
    return (rows < HEAD) if which == 0 else (rows >= HEAD)


def keep(mask, x):
    return jnp.where(mask, x, jnp.zeros_like(x))


def attn_fwd_kernel(
    groups, which_page, pick, res, tok_ref, box_ref, freq_ref, wq_ref, wk_ref, wv_ref, bq_ref, bv_ref, wbt_ref, wo_ref,
    part_ref, p_ref, q_ref, k_ref, v_ref, ctx_ref, s_ref, c_ref, tok_t_ref, codes, mixed, acc, biases, s_keep, c_keep, t_keep, sems,
):
    step = pl.program_id(0)
    half = s_keep.shape[1]

    def leaving():
        pairs = ((s_keep, s_ref), (c_keep, c_ref), (t_keep, tok_t_ref))
        return [pltpu.make_async_copy(a, b, sems.at[n]) for n, (a, b) in enumerate(pairs)]

    @pl.when(step == 0)
    def _():
        rows = s_keep.shape[0]
        lanes = lax.broadcasted_iota(jnp.int32, (rows, half), 1)
        level = res[pick[which_page]]
        width = (612 + 204 * level).astype(F32)
        height = (792 + 264 * level).astype(F32)
        corners = box_ref[...]
        centre_x = (corners[0:1] + corners[2:3]).astype(F32) * 500.0 / width
        centre_y = (corners[1:2] + corners[3:4]).astype(F32) * 500.0 / height
        both = jnp.concatenate([centre_x, centre_y, jnp.zeros((6, rows), F32)], axis=0).T
        centre = jnp.where(lanes < half // 2, both[:, 0:1], both[:, 1:2])
        sine, cosine = sin_cos(centre * freq_ref[...])
        s_keep[...] = sine
        c_keep[...] = cosine
        codes[:, :half] = cosine.astype(BF16)
        codes[:, half : 2 * half] = sine.astype(BF16)
        acc[...] = jnp.zeros_like(acc)
        biases[0:1] = bq_ref[...].astype(F32).reshape(1, -1)
        biases[1:2] = bv_ref[...].astype(F32).reshape(1, -1)
        tok_t = split_rows(tok_ref[...].T, groups)
        t_keep[0] = tok_t[:half]
        t_keep[1] = tok_t[half:]
        for copy in leaving():
            copy.start()

    tok = tok_ref[...]
    rows = tok.shape[0]
    wide = wq_ref.shape[1]
    span = pl.ds(pl.multiple_of(step * wide, wide), wide)
    qkv = mm(tok, jnp.concatenate([wq_ref[...], wk_ref[...], wv_ref[...]], axis=1))
    q2 = (qkv[:, :wide] + biases[0:1, span]).astype(BF16) * BF16(0.125)
    k2 = qkv[:, wide : 2 * wide].astype(BF16)
    v2 = (qkv[:, 2 * wide :] + biases[1:2, span]).astype(BF16)
    q_ref[...] = q2
    k_ref[...] = k2
    v_ref[...] = v2
    codes[:, 2 * half :] = k2
    sine, cosine = s_keep[...], c_keep[...]
    for which in range(2):
        span = slice(which * rows, (which + 1) * rows)
        qm = keep(lane_mask(q2.shape, which), q2)
        off = mm(qm, wbt_ref[...])
        a, b = off[:, :half], off[:, half:]
        mixed[span, :half] = (a * sine + b * cosine).astype(BF16)
        mixed[span, half : 2 * half] = (b * sine - a * cosine).astype(BF16)
        mixed[span, 2 * half :] = qm
    parts = []
    for which in range(2):
        span = slice(which * rows, (which + 1) * rows)
        scores = mm_nt(mixed[span], codes[...])
        top = jnp.max(scores, axis=1, keepdims=True)
        raised = jnp.exp(scores - top)
        total = jnp.sum(raised, axis=1, keepdims=True)
        prob = (raised * (1.0 / total)).astype(BF16)
        p_ref[which] = prob
        parts.append(mm(prob, v2))
    ctx2 = jnp.where(lane_mask(parts[0].shape, 0), parts[0], parts[1]).astype(BF16)
    ctx_ref[...] = ctx2
    acc[...] += mm(ctx2, wo_ref[...])

    @pl.when(step == pl.num_programs(0) - 1)
    def _():
        part_ref[...] = acc[...].astype(BF16)
        for copy in leaving():
            copy.wait()


def attn_fwd(which_page, pick, res, tokens, boxes, freq, wq, wk, wv, bq, bv, wbt, wo, length, groups):
    dim = tokens.shape[1]
    inner = wq.shape[1]
    heads = inner // HEAD
    pairs = heads // 2
    wide = 2 * HEAD
    page = lambda i, pick, res: (pick[which_page], 0)
    fixed = lambda i, pick, res: (0, 0)
    cols = lambda i, pick, res: (0, i)
    rows = lambda i, pick, res: (i, 0)
    flops = 2 * length * (dim * inner * 4 + heads * (HEAD * dim + length * (dim + 2 * HEAD)))
    return pl.pallas_call(
        partial(attn_fwd_kernel, groups, which_page),
        grid_spec=pltpu.PrefetchScalarGridSpec(
            num_scalar_prefetch=2,
            grid=(pairs,),
            in_specs=[
                pl.BlockSpec((length, dim), page),
                pl.BlockSpec((4, length), lambda i, pick, res: (0, pick[which_page])),
                pl.BlockSpec((1, dim // 2), fixed),
                pl.BlockSpec((dim, wide), cols),
                pl.BlockSpec((dim, wide), cols),
                pl.BlockSpec((dim, wide), cols),
                pl.BlockSpec((inner,), lambda i, pick, res: (0,)),
                pl.BlockSpec((inner,), lambda i, pick, res: (0,)),
                pl.BlockSpec((wide, dim), rows),
                pl.BlockSpec((wide, dim), rows),
            ],
            out_specs=[
                pl.BlockSpec((length, dim), fixed),
                pl.BlockSpec((2, length, length), lambda i, pick, res: (i, 0, 0)),
                pl.BlockSpec((length, wide), cols),
                pl.BlockSpec((length, wide), cols),
                pl.BlockSpec((length, wide), cols),
                pl.BlockSpec((length, wide), cols),
                pl.BlockSpec(memory_space=pl.ANY),
                pl.BlockSpec(memory_space=pl.ANY),
                pl.BlockSpec(memory_space=pl.ANY),
            ],
            scratch_shapes=[
                pltpu.VMEM((length, dim + wide), BF16),
                pltpu.VMEM((2 * length, dim + wide), BF16),
                pltpu.VMEM((length, dim), F32),
                pltpu.VMEM((8, inner), F32),
                pltpu.VMEM((length, dim // 2), F32),
                pltpu.VMEM((length, dim // 2), F32),
                pltpu.VMEM((2, dim // 2, length), BF16),
                pltpu.SemaphoreType.DMA((3,)),
            ],
        ),
        out_shape=[
            hbm((length, dim), BF16),
            hbm((heads, length, length), BF16),
            hbm((length, inner), BF16),
            hbm((length, inner), BF16),
            hbm((length, inner), BF16),
            hbm((length, inner), BF16),
            hbm((length, dim // 2), F32),
            hbm((length, dim // 2), F32),
            hbm((2, dim // 2, length), BF16),
        ],
        compiler_params=params(1),
        cost_estimate=cost(flops, 10e6, heads * length * length),
        name="attn_fwd",
    )(pick, res, tokens, boxes, freq, wq, wk, wv, bq, bv, wbt, wo)


def attn_bwd_kernel(groups, box_groups, first, pick, *refs):
    (df_ref, tok_t_ref, ctx_ref, wo_ref, q_ref, k_ref, v_ref, p_ref, s_ref, c_ref, wbt_ref,
     wq_ref, wk_ref, wv_ref, *refs) = refs
    if first:
        part_ref, small_ref, inp_ref, codes, acc, df_t = refs
    else:
        prev_ref, prev_small_ref, extra_ref, *refs = refs
        sent_ref, kept_ref, small_ref, inp_ref, codes, acc, df_t, grads = refs
    step = pl.program_id(0)
    half = s_ref.shape[1]

    @pl.when(step == 0)
    def _():
        codes[:, :half] = c_ref[...].astype(BF16)
        codes[:, half:] = s_ref[...].astype(BF16)
        acc[...] = jnp.zeros_like(acc)
        turned = split_rows(df_ref[...].T, groups)
        df_t[0] = turned[:half]
        df_t[1] = turned[half:]

    sine, cosine = s_ref[...], c_ref[...]
    q2, k2, v2 = q_ref[...], k_ref[...], v_ref[...]
    dctx = mm_nt(df_ref[...], wo_ref[...]).astype(BF16)
    dctx_t = dctx.T
    q_t = q2.T
    wbt = wbt_ref[...]
    dq = jnp.zeros(q2.shape, F32)
    dk_t, dv_t, dwb = [], [], []
    for which in range(2):
        low, high = which * HEAD, (which + 1) * HEAD
        dm = keep(lane_mask(dctx.shape, which), dctx)
        prob = p_ref[which]
        grad_probs = mm_nt(dm, v2)
        dv_t.append(mm(dctx_t[low:high], prob))
        wide_prob = prob.astype(F32)
        both = wide_prob * grad_probs
        inner = jnp.sum(both, axis=1, keepdims=True)
        ds = (both - wide_prob * inner).astype(BF16)
        dk_t.append(mm(q_t[low:high], ds))
        km = keep(lane_mask(k2.shape, which), k2)
        ga = mm(ds, codes[:, :half]).astype(BF16).astype(F32)
        gb = mm(ds, codes[:, half:]).astype(BF16).astype(F32)
        oa = (ga * sine - gb * cosine).astype(BF16)
        ob = (gb * sine + ga * cosine).astype(BF16)
        wm = keep(row_mask(wbt.shape, which), wbt)
        dq = dq + (mm(ds, km) + mm_nt(oa, wm[:, :half]) + mm_nt(ob, wm[:, half:]))
        dwb.append(jnp.concatenate([mm(q_t[low:high], oa), mm(q_t[low:high], ob)], axis=1))
    dq2 = (dq * 0.125).astype(BF16)
    dk2 = jnp.concatenate(dk_t, axis=0).T.astype(BF16)
    dv2 = jnp.concatenate(dv_t, axis=0).T.astype(BF16)
    sides = jnp.concatenate([dq2, dk2, dv2], axis=1)
    acc[...] += mm_nt(sides, jnp.concatenate([wq_ref[...], wk_ref[...], wv_ref[...]], axis=1))

    box = split_rows(jnp.concatenate(dwb, axis=0).T, box_groups)
    ctx2 = ctx_ref[...]
    zeros = jnp.zeros((1, 3 * q2.shape[1]), F32)
    small = jnp.concatenate(
        [column_sum(dq2.astype(F32)), column_sum(dv2.astype(F32)), zeros], axis=1
    )
    if not first:
        small = small + prev_small_ref[...]
    small_ref[...] = small
    for h in range(2):
        grad = jnp.concatenate(
            [mm(tok_t_ref[h], sides), mm(df_t[h], ctx2), box[h * half : (h + 1) * half]], axis=1
        )
        if first:
            part_ref[h] = grad.astype(BF16)
        else:
            grads[h] = (grad + prev_ref[h].astype(F32)).astype(BF16)
    if not first:
        sent_ref[:half] = grads[pick[3]]
        sent_ref[half:] = wide_tail(small)
        kept_ref[...] = grads[pick[2]]

    @pl.when(step == pl.num_programs(0) - 1)
    def _():
        rows = acc.shape[0]
        inp_ref[:rows] = acc[...].astype(BF16)
        if not first:
            inp_ref[rows:] = extra_ref[...]


def attn_bwd(pick, df, saved, wo, wbt, wq, wk, wv, groups, box_groups, prev=None, extra=None):
    prob, q, k, v, ctx, sine, cosine, tok_t = saved
    length, dim = df.shape
    inner = wq.shape[1]
    heads = inner // HEAD
    pairs = heads // 2
    wide = 2 * HEAD
    first = prev is None
    sent = length if first else 2 * length
    fixed = lambda i, pick: (0, 0)
    cols = lambda i, pick: (0, i)
    rows = lambda i, pick: (i, 0)
    block = lambda i, pick: (0, 0, i)
    flops = 2 * length * (dim * inner * 8 + heads * (3 * HEAD * dim + length * (dim + 4 * HEAD)))
    part = pl.BlockSpec((2, dim // 2, 5 * wide), block)
    small = pl.BlockSpec((1, 5 * wide), cols)
    small_shape = hbm((1, 5 * inner), F32)
    inp = pl.BlockSpec((sent, dim), fixed)
    inp_shape = hbm((sent, dim), BF16)
    scratch = [
        pltpu.VMEM((length, dim), BF16),
        pltpu.VMEM((length, dim), F32),
        pltpu.VMEM((2, dim // 2, length), BF16),
    ]
    if first:
        out_specs = [part, small, inp]
        out_shape = [hbm((2, dim // 2, 5 * inner), BF16), small_shape, inp_shape]
        more_specs, more = [], []
    else:
        out_specs = [
            pl.BlockSpec((dim // 2 + TAIL, 5 * wide), cols), pl.BlockSpec((dim // 2, 5 * wide), cols), small, inp,
        ]
        out_shape = [
            hbm((dim // 2 + TAIL, 5 * inner), BF16), hbm((dim // 2, 5 * inner), BF16), small_shape, inp_shape,
        ]
        more_specs, more = [part, small, pl.BlockSpec((length, dim), fixed)], [*prev, extra]
        scratch.append(pltpu.VMEM((2, dim // 2, 5 * wide), BF16))
    return pl.pallas_call(
        partial(attn_bwd_kernel, groups, box_groups, first),
        grid_spec=pltpu.PrefetchScalarGridSpec(
            num_scalar_prefetch=1,
            grid=(pairs,),
            in_specs=[
                pl.BlockSpec((length, dim), fixed),
                pl.BlockSpec((2, dim // 2, length), lambda i, pick: (0, 0, 0)),
                pl.BlockSpec((length, wide), cols),
                pl.BlockSpec((wide, dim), rows),
                pl.BlockSpec((length, wide), cols),
                pl.BlockSpec((length, wide), cols),
                pl.BlockSpec((length, wide), cols),
                pl.BlockSpec((2, length, length), lambda i, pick: (i, 0, 0)),
                pl.BlockSpec((length, dim // 2), fixed),
                pl.BlockSpec((length, dim // 2), fixed),
                pl.BlockSpec((wide, dim), rows),
                pl.BlockSpec((dim, wide), cols),
                pl.BlockSpec((dim, wide), cols),
                pl.BlockSpec((dim, wide), cols),
            ]
            + more_specs,
            out_specs=out_specs,
            scratch_shapes=scratch,
        ),
        out_shape=out_shape,
        compiler_params=params(1),
        cost_estimate=cost(flops, 14e6),
        name="attn_bwd",
    )(pick, df, tok_t, ctx, wo, q, k, v, prob, sine, cosine, wbt, wq, wk, wv, *more)


def split_rows(x_t, groups):
    return jnp.concatenate([x_t[start : start + count] for start, count in groups], axis=0)


def shard_groups(dim, shards):
    rows = dim // shards
    if not fast_path(dim, shards):
        return [(0, dim)]
    order = [z * 4 + x * 2 + c for c in range(2) for z in range(shards // 4) for x in range(2)]
    return [(block * rows, rows) for block in order]


def fast_path(dim, shards):
    return shards == 16 and (dim // shards) % 16 == 0


def gelu_parts(v):
    e = jnp.exp(v * v * -0.5)
    t = 1.0 / (1.0 + (0.3275911 * math.sqrt(0.5)) * jnp.abs(v))
    poly = t * (
        0.5 * 0.254829592
        + t * (0.5 * -0.284496736 + t * (0.5 * 1.421413741 + t * (0.5 * -1.453152027 + t * (0.5 * 1.061405429))))
    )
    tail = poly * e
    phi = jnp.where(v >= 0, 1.0 - tail, tail)
    return phi, phi + v * (e * (1.0 / math.sqrt(2.0 * math.pi)))


def norm_stats(hidden):
    centred = hidden - jnp.mean(hidden, axis=1, keepdims=True)
    variance = jnp.mean(centred * centred, axis=1, keepdims=True)
    inv = lax.rsqrt(variance + 1e-05)
    return centred * inv, inv


def norm_back(grad, scaled, inv):
    return inv * (
        grad
        - jnp.mean(grad, axis=1, keepdims=True)
        - scaled * jnp.mean(grad * scaled, axis=1, keepdims=True)
    )


def column_sum(x):
    return jnp.sum(x, axis=0, keepdims=True)


def ff_kernel(
    groups, pick, tok_ref, part_ref, got_ref, gout_ref, bo_ref, g1_ref, b1_ref, bb_ref, g2_ref, b2_ref,
    bi_here, bi_there,
    wi_here, wb_here, wi0, wi1, wi2, wi3, wb0, wb1, wb2, wb3,
    out_ref, df_ref, lhs_ref, rhs_ref, small_ref,
    wi, wb, slope, norm_low, grad_low, acc, wide, bi_ref, rhs, sems,
):
    blocks, dim, cols = wi.shape
    here = blocks // 2
    piece = cols // 2
    remote = [(wi0, wb0), (wi1, wb1), (wi2, wb2), (wi3, wb3)]
    for p in range(2 * blocks):
        if p < blocks:
            at = (p % 2) * piece
            span = pl.ds(at, piece)
            source = (wi_here.at[:, pl.ds(p * piece, piece)], wb_here.at[pl.ds(p * piece, piece), :])
        else:
            span = pl.ds(pl.multiple_of(((pick[6] ^ p) & 1) * piece, piece), piece)
            source = remote[p - blocks]
            slot = here + ((((pick[8] ^ p) & 3) >> 1) ^ pick[7])
            span_back = pl.ds(pl.multiple_of(((pick[8] ^ p) & 1) * piece, piece), piece)
        pltpu.make_async_copy(source[0], wi.at[p // 2, :, span], sems.at[0, p]).start()
        if p < blocks:
            pltpu.make_async_copy(source[1], wb.at[p // 2, span, :], sems.at[1, p // 2]).start()
        else:
            pltpu.make_async_copy(source[1], wb.at[slot, span_back, :], sems.at[1, slot]).start()

    def vec(ref):
        return ref[...].astype(F32).reshape(1, -1)

    here_at, there_at = pick[0] * here, pick[1] * here
    bias_here, bias_there = vec(bi_here), vec(bi_there)
    for j in range(here):
        bi_ref[pl.ds(here_at + j, 1), :] = bias_here[:, j * cols : (j + 1) * cols]
        bi_ref[pl.ds(there_at + j, 1), :] = bias_there[:, j * cols : (j + 1) * cols]

    def place(j):
        return jnp.where(j < here, here_at + j, there_at + (pick[7] ^ (j - here)))

    bo, g1, b1, bb, g2, b2 = (vec(r) for r in (bo_ref, g1_ref, b1_ref, bb_ref, g2_ref, b2_ref))
    first_sum = (
        tok_ref[...].astype(F32)
        + (part_ref[...].astype(F32) + got_ref[...].astype(F32))
        + bo
    )
    scaled1, inv1 = norm_stats(first_sum)
    normed = scaled1 * g1 + b1
    low = normed.astype(BF16)
    norm_low[...] = low
    wide[...] = normed + bb
    acc[...] = jnp.zeros_like(acc)
    low_t = split_rows(low.T, groups)
    split = low_t.shape[0] // 2
    lhs_ref[0, 0] = low_t[:split]
    lhs_ref[1, 0] = low_t[split:]

    def leaving(m, j):
        return pltpu.make_async_copy(rhs.at[m, j], rhs_ref.at[m, j], sems.at[2 + m, j])

    def forward(j, _):
        for p in range(2):
            pltpu.make_async_copy(wi0, wi.at[j, :, pl.ds(0, piece)], sems.at[0, 2 * j + p]).wait()
        pltpu.make_async_copy(wb.at[j], wb.at[j], sems.at[1, j]).wait()
        pre = mm(norm_low[...], wi[j]) + bi_ref[pl.ds(place(j), 1), :]
        phi, step = gelu_parts(pre)
        act = (pre * phi).astype(BF16)
        rhs[1, j] = act
        leaving(1, j).start()
        slope[j] = step
        acc[...] += mm(act, wb[j])
        return 0

    lax.fori_loop(0, blocks, forward, 0)
    scaled2, inv2 = norm_stats(wide[...] + acc[...])
    out_ref[...] = (scaled2 * g2 + b2).astype(BF16)
    gout = gout_ref[...].astype(F32)
    small_gain2 = column_sum(gout * scaled2)
    small_bias2 = column_sum(gout)
    grad_second = norm_back(gout * g2, scaled2, inv2)
    small_back = column_sum(grad_second)
    low2 = grad_second.astype(BF16)
    grad_low[...] = low2
    low2_t = split_rows(low2.T, groups)
    lhs_ref[0, 1] = low2_t[:split]
    lhs_ref[1, 1] = low2_t[split:]
    acc[...] = grad_second

    def backward(j, _):
        grad_act = mm_nt(grad_low[...], wb[j]).astype(BF16).astype(F32)
        grad_pre = (grad_act * slope[j]).astype(BF16)
        rhs[0, j] = grad_pre
        leaving(0, j).start()
        bi_ref[pl.ds(place(j), 1), :] = column_sum(grad_pre.astype(F32))
        acc[...] += mm_nt(grad_pre, wi[j])
        return 0

    lax.fori_loop(0, blocks, backward, 0)
    grad_normed = acc[...]
    first_sum = (
        tok_ref[...].astype(F32)
        + (part_ref[...].astype(F32) + got_ref[...].astype(F32))
        + bo
    )
    scaled1, inv1 = norm_stats(first_sum)
    small_gain1 = column_sum(grad_normed * scaled1)
    small_bias1 = column_sum(grad_normed)
    grad_first = norm_back(grad_normed * g1, scaled1, inv1)
    small_out = column_sum(grad_first)
    df_ref[...] = grad_first.astype(BF16)
    for m in range(2):
        for j in range(blocks):
            leaving(m, j).wait()
    small_ref[...] = jnp.concatenate(
        [
            jnp.concatenate([small_gain2, small_bias2], axis=1),
            jnp.concatenate([small_back, small_gain1], axis=1),
            jnp.concatenate([small_bias1, small_out], axis=1),
            jnp.concatenate([bi_ref[j : j + 1] for j in range(here)], axis=1),
            jnp.concatenate([bi_ref[j : j + 1] for j in range(here, blocks)], axis=1),
            jnp.zeros((3, 2 * dim), F32),
        ],
        axis=0,
    )


def feed_forward(pick, tokens, part, got, grad_out, rows, bias_in, bias_there, wi_here, wb_here, wi_pieces, wb_pieces, groups):
    length, dim = part.shape
    cols = 2 * wi_pieces[0].shape[1]
    blocks = 2 * wi_here.shape[1] // cols
    page = lambda i, pick: (pick[0], 0)
    fixed = lambda i, pick: (0, 0)
    row = pl.BlockSpec((dim,), lambda i, pick: (0,))
    bias_row = pl.BlockSpec(bias_in.shape, lambda i, pick: (0,))
    whole = pl.BlockSpec((length, dim), fixed)
    anywhere = pl.BlockSpec(memory_space=pl.ANY)
    hidden = blocks * cols
    return pl.pallas_call(
        partial(ff_kernel, groups),
        grid_spec=pltpu.PrefetchScalarGridSpec(
            num_scalar_prefetch=1,
            grid=(1,),
            in_specs=[
                pl.BlockSpec((length, dim), page),
                whole,
                whole,
                pl.BlockSpec((length, dim), page),
                row, row, row, row, row, row,
                bias_row, bias_row,
            ]
            + [anywhere] * 10,
            out_specs=[
                whole,
                whole,
                pl.BlockSpec((2, 2, dim // 2, length), lambda i, pick: (0, 0, 0, 0)),
                anywhere,
                pl.BlockSpec((8, 2 * dim), fixed),
            ],
            scratch_shapes=[
                pltpu.VMEM((blocks, dim, cols), BF16),
                pltpu.VMEM((blocks, cols, dim), BF16),
                pltpu.VMEM((blocks, length, cols), F32),
                pltpu.VMEM((length, dim), BF16),
                pltpu.VMEM((length, dim), BF16),
                pltpu.VMEM((length, dim), F32),
                pltpu.VMEM((length, dim), F32),
                pltpu.VMEM((blocks, cols), F32),
                pltpu.VMEM((2, blocks, length, cols), BF16),
                pltpu.SemaphoreType.DMA((4, 2 * blocks)),
            ],
        ),
        out_shape=[
            hbm((length, dim), BF16),
            hbm((length, dim), BF16),
            hbm((2, 2, dim // 2, length), BF16),
            hbm((2, blocks, length, cols), BF16),
            hbm((8, 2 * dim), F32),
        ],
        compiler_params=params(1),
        cost_estimate=cost(8 * length * dim * hidden, 4 * dim * hidden + 8 * length * hidden, length * hidden),
        name="feed_forward",
    )(pick, tokens, part, got, grad_out, *rows, bias_in, bias_there, wi_here, wb_here, *wi_pieces, *wb_pieces)


TAIL = 16


def split2(x):
    high = x.astype(BF16)
    return high, (x - high.astype(F32)).astype(BF16)


def rounded(x):
    high, low = split2(x)
    return high.astype(F32) + low.astype(F32)


def tall(x):
    return jnp.concatenate([x, jnp.zeros((TAIL - x.shape[0],) + x.shape[1:], x.dtype)], axis=0)


def ff_send_kernel(pick, lhs_ref, rhs_ref, small_ref, out_ref):
    rows = lhs_ref.shape[2]
    for m in range(2):
        out_ref[m, :rows] = mm(lhs_ref[0, m], rhs_ref[m, 0]).astype(BF16)
    for m, term in enumerate(split2(small_ref[...])):
        out_ref[m, rows:] = tall(term)


def ff_keep_kernel(pick, lhs_ref, rhs_ref, got_ref, small_ref, xs_ref, xk_ref, small_out, acc):
    rows = lhs_ref.shape[2]
    shard = acc.shape[0] // 8
    x_index = pick[4]
    for m in range(2):
        acc[...] = mm(lhs_ref[0, m], rhs_ref[m, 0]) + got_ref[m, :rows].astype(F32)
        for z in range(4):
            away = pl.multiple_of((2 * z + 1 - x_index) * shard, 8)
            mine = pl.multiple_of((2 * z + x_index) * shard, 8)
            xs_ref[m, z * shard : (z + 1) * shard] = acc[pl.ds(away, shard), :].astype(BF16)
            xk_ref[m, z * shard : (z + 1) * shard] = acc[pl.ds(mine, shard), :].astype(BF16)
    small = rounded(small_ref[...]) + (got_ref[0, rows : rows + 8].astype(F32) + got_ref[1, rows : rows + 8].astype(F32))
    small_out[...] = small
    for m, term in enumerate(split2(small)):
        xs_ref[m, 4 * shard :] = tall(term)


def ff_grad(pick, lhs, rhs, small, remote, got=None):
    _, mats, rows, length = lhs.shape
    _, blocks, _, cols = rhs.shape
    half = blocks // 2
    base = half if remote else 0
    which = 2 if got is not None else 3
    dest = (lambda j, pick: j ^ pick[7]) if remote else (lambda j, pick: j)
    column = lambda height: pl.BlockSpec((2, height, cols), lambda j, pick: (0, 0, dest(j, pick)))
    small_spec = pl.BlockSpec((8, cols), lambda j, pick: (0, dest(j, pick)))
    in_specs = [
        pl.BlockSpec((1, mats, rows, length), lambda j, pick: (pick[which], 0, 0, 0)),
        pl.BlockSpec((2, 1, length, cols), lambda j, pick: (0, base + j, 0, 0)),
    ]
    wide = half * cols
    estimate = cost(2 * mats * rows * length * wide, 10e6)
    if got is None:
        return pl.pallas_call(
            ff_send_kernel,
            grid_spec=pltpu.PrefetchScalarGridSpec(
                num_scalar_prefetch=1,
                grid=(half,),
                in_specs=in_specs + [small_spec],
                out_specs=column(rows + TAIL),
            ),
            out_shape=hbm((2, rows + TAIL, wide), BF16),
            compiler_params=params(1),
            cost_estimate=estimate,
            name="ff_grad_send",
        )(pick, lhs, rhs, small)
    return pl.pallas_call(
        ff_keep_kernel,
        grid_spec=pltpu.PrefetchScalarGridSpec(
            num_scalar_prefetch=1,
            grid=(half,),
            in_specs=in_specs + [column(rows + TAIL), small_spec],
            out_specs=[column(rows // 2 + TAIL), column(rows // 2), small_spec],
            scratch_shapes=[pltpu.VMEM((rows, cols), F32)],
        ),
        out_shape=[
            hbm((2, rows // 2 + TAIL, wide), BF16),
            hbm((2, rows // 2, wide), BF16),
            hbm((8, wide), F32),
        ],
        compiler_params=params(1),
        cost_estimate=estimate,
        name="ff_grad_keep",
    )(pick, lhs, rhs, got, small)


def wide_tail(vector):
    high, low = split2(vector)
    return tall(jnp.concatenate([high, low], axis=0))


def attn_split_kernel(pick, kept_ref, got_ref, small_ref, xs_ref, xk_ref, small_out, acc):
    rows = kept_ref.shape[0]
    acc[...] = kept_ref[...].astype(F32) + got_ref[:rows].astype(F32)
    x_index = pick[4]
    shard = rows // 8
    for z in range(4):
        away = pl.multiple_of((2 * z + 1 - x_index) * shard, 8)
        mine = pl.multiple_of((2 * z + x_index) * shard, 8)
        xs_ref[0, z * shard : (z + 1) * shard] = acc[pl.ds(away, shard), :].astype(BF16)
        xk_ref[0, z * shard : (z + 1) * shard] = acc[pl.ds(mine, shard), :].astype(BF16)
    small = rounded(small_ref[...]) + (
        got_ref[rows : rows + 1].astype(F32) + got_ref[rows + 1 : rows + 2].astype(F32)
    )
    small_out[...] = jnp.concatenate([small, jnp.zeros((7, small.shape[1]), F32)], axis=0)
    xs_ref[0, 4 * shard :] = wide_tail(small)


def attn_split(pick, kept, got, small):
    rows, cols = kept.shape
    steps = 3
    column = lambda height: pl.BlockSpec((height, cols // steps), lambda i, pick: (0, i))
    deep = lambda height: pl.BlockSpec((1, height, cols // steps), lambda i, pick: (0, 0, i))
    return pl.pallas_call(
        attn_split_kernel,
        grid_spec=pltpu.PrefetchScalarGridSpec(
            num_scalar_prefetch=1,
            grid=(steps,),
            in_specs=[column(rows), column(rows + TAIL), column(1)],
            out_specs=[deep(rows // 2 + TAIL), deep(rows // 2), column(8)],
            scratch_shapes=[pltpu.VMEM((rows, cols // steps), F32)],
        ),
        out_shape=[
            hbm((1, rows // 2 + TAIL, cols), BF16),
            hbm((1, rows // 2, cols), BF16),
            hbm((8, cols), F32),
        ],
        compiler_params=params(1),
        cost_estimate=cost(kept.size, 6 * kept.size),
        name="attn_split",
    )(pick, kept, got, small)


def tail_sum(ref, at):
    if ref.shape[0] == 2:
        return ref[0, at : at + 8].astype(F32) + ref[1, at : at + 8].astype(F32)
    one = ref[0, at : at + 1].astype(F32) + ref[0, at + 1 : at + 2].astype(F32)
    return jnp.concatenate([one, jnp.zeros((7, one.shape[1]), F32)], axis=0)


def put_tail(ref, at, small):
    if ref.shape[0] == 2:
        for m, term in enumerate(split2(small)):
            ref[m, at:] = tall(term)
    else:
        ref[0, at:] = wide_tail(small[0:1])


def add_x_kernel(tailed, pick, keep_ref, got_ref, small_ref, own, sent, *rest):
    shard = own.shape[1] // 2
    z = pick[5]
    for i, d in enumerate((0, 2, 1, 3)):
        at = pl.multiple_of((z ^ d) * shard, 16)
        ref = own if i < 2 else sent
        ref[:, (i % 2) * shard : (i % 2 + 1) * shard] = (
            keep_ref[:, pl.ds(at, shard), :].astype(F32) + got_ref[:, pl.ds(at, shard), :].astype(F32)
        ).astype(BF16)
    if tailed:
        small = rounded(small_ref[...]) + tail_sum(got_ref, 4 * shard)
        rest[0][...] = small
        put_tail(sent, 2 * shard, small)


def add_x(pick, kept, got, small, tailed):
    mats, rows, cols = kept.shape
    own = hbm((mats, rows // 2, cols), BF16)
    sent = hbm((mats, rows // 2 + (TAIL if tailed else 0), cols), BF16)
    full = lambda s: pl.BlockSpec(s.shape, lambda i, pick: (0,) * len(s.shape))
    extra = [hbm(small.shape, F32)] if tailed else []
    return pl.pallas_call(
        partial(add_x_kernel, tailed),
        grid_spec=pltpu.PrefetchScalarGridSpec(
            num_scalar_prefetch=1,
            grid=(1,),
            in_specs=[full(kept), full(got), full(small)],
            out_specs=[full(s) for s in [own, sent] + extra],
        ),
        out_shape=[own, sent] + extra,
        compiler_params=params(1),
        cost_estimate=cost(kept.size, 6 * kept.size),
        name="add_x",
    )(pick, kept, got, small)


def whole_call(kernel, out_shape, estimate, name, *args):
    full = lambda s: pl.BlockSpec(s.shape, lambda i: (0,) * len(s.shape))
    return pl.pallas_call(
        kernel,
        grid=(1,),
        in_specs=[full(a) for a in args],
        out_specs=[full(s) for s in out_shape],
        out_shape=out_shape,
        compiler_params=params(1),
        cost_estimate=estimate,
        name=name,
    )(*args)


def both(a, b):
    return a.astype(F32) + b.astype(F32)


def add_z_kernel(tailed, keep_ref, got_ref, small_ref, own, sent, *rest):
    shard = own.shape[1]
    own[...] = both(keep_ref[:, :shard], got_ref[:, :shard]).astype(BF16)
    sent[:, :shard] = both(keep_ref[:, shard:], got_ref[:, shard : 2 * shard]).astype(BF16)
    if tailed:
        small = rounded(small_ref[...]) + tail_sum(got_ref, 2 * shard)
        rest[0][...] = small
        put_tail(sent, shard, small)


def add_z(kept, got, small, tailed):
    mats, rows, cols = kept.shape
    shard = rows // 2
    out = [hbm((mats, shard, cols), BF16), hbm((mats, shard + (TAIL if tailed else 0), cols), BF16)]
    if tailed:
        out.append(hbm(small.shape, F32))
    return whole_call(
        partial(add_z_kernel, tailed), out, cost(4e10, 6 * kept.size), "add_z", kept, got, small
    )


def for_head_kernel(own, got, small_ref, out, small_out):
    shard = own.shape[1]
    out[:, :shard] = both(own[...], got[:, :shard]).astype(BF16)
    small = rounded(small_ref[...]) + tail_sum(got, shard)
    small_out[...] = small
    put_tail(out, shard, small)


def for_head(own, got, small):
    out = [hbm(got.shape, BF16), hbm(small.shape, F32)]
    return whole_call(for_head_kernel, out, cost(4e10, 6 * own.size), "for_head", own, got, small)


def ff_last_kernel(pick, own, z_got, got, small_ref, in_out, back_out, *vectors):
    small_out = vectors[-1]
    shard = own.shape[1]
    in_out[...] = both(own[0], z_got[0]) + got[0, :shard].astype(F32)
    back_out[...] = both(own[1], z_got[1]) + got[1, :shard].astype(F32)
    small = rounded(small_ref[...]) + tail_sum(got, shard)
    small_out[...] = small
    dim = small.shape[1] // 2
    for i in range(6):
        vectors[i][...] = small[i // 2 : i // 2 + 1, (i % 2) * dim : (i % 2 + 1) * dim].reshape(dim)
    vectors[6][...] = small_out[pl.ds(3 + pick[0], 1), :].reshape(2 * dim)


def ff_last(pick, own, z_got, got, small):
    _, rows, cols = own.shape
    dim = cols // 2
    full = lambda s: pl.BlockSpec(s.shape, lambda i, pick: (0,) * len(s.shape))
    out_shape = [hbm((rows, cols), F32)] * 2 + [hbm((dim,), F32)] * 6 + [hbm((cols,), F32)]
    return pl.pallas_call(
        ff_last_kernel,
        grid_spec=pltpu.PrefetchScalarGridSpec(
            num_scalar_prefetch=1,
            grid=(1,),
            in_specs=[full(own), full(z_got), full(got), full(small)],
            out_specs=[full(s) for s in out_shape],
            scratch_shapes=[pltpu.VMEM(small.shape, F32)],
        ),
        out_shape=out_shape,
        compiler_params=params(1),
        cost_estimate=cost(10 * got.size, 20 * got.size),
        name="ff_last",
    )(pick, own, z_got, got, small)


def attn_last_kernel(own, got, small_ref, q_out, k_out, v_out, box_out, wo_out, bq_out, bv_out):
    shard = own.shape[1]
    wide = 2 * HEAD
    pairs = q_out.shape[1] // wide
    small = rounded(small_ref[...]) + tail_sum(got, shard)
    for p in range(pairs):
        at = slice(p * wide, (p + 1) * wide)
        for i, ref in enumerate((q_out, k_out, v_out, wo_out, box_out)):
            span = slice((5 * p + i) * wide, (5 * p + i + 1) * wide)
            ref[:, at] = both(own[0, :, span], got[0, :shard, span])
    for i, ref in enumerate((bq_out, bv_out)):
        row = [small[0:1, (5 * p + i) * wide : (5 * p + i + 1) * wide] for p in range(pairs)]
        ref[...] = jnp.concatenate(row, axis=1).reshape(pairs * wide)


def attn_last(own, got, small):
    _, rows, cols = own.shape
    cols = cols // 5
    out = [hbm((rows, cols), F32)] * 5 + [hbm((cols,), F32)] * 2
    return whole_call(attn_last_kernel, out, cost(4 * own.size, 12 * own.size), "attn_last", own, got, small)


def place_grad_kernel(pick, df_ref, a_ref, b_ref, *refs):
    refs[-1][...] = df_ref[...].astype(F32) + (a_ref[...].astype(F32) + b_ref[...].astype(F32))


def place_grad(which, pick, df, mine, got, pages, into=None):
    length, dim = df.shape
    steps = 2
    part = pl.BlockSpec((length // steps, dim), lambda i, pick: (i, 0))
    args = [df, mine, got] + ([] if into is None else [into])
    return pl.pallas_call(
        place_grad_kernel,
        grid_spec=pltpu.PrefetchScalarGridSpec(
            num_scalar_prefetch=1,
            grid=(steps,),
            in_specs=[part] * 3 + ([] if into is None else [pl.BlockSpec(memory_space=pl.ANY)]),
            out_specs=pl.BlockSpec((length // steps, dim), lambda i, pick: (pick[which] * steps + i, 0)),
        ),
        out_shape=hbm((pages * length, dim), F32),
        input_output_aliases={} if into is None else {4: 0},
        compiler_params=params(1),
        cost_estimate=cost(3 * df.size, 10 * df.size),
        name="place_grad",
    )(pick, *args)


def place_output_kernel(pick, a_ref, b_ref, out_ref):
    length = a_ref.shape[0]
    own = pl.multiple_of(pick[0] * length, length)
    other = pl.multiple_of(pick[1] * length, length)
    out_ref[pl.ds(own, length), :] = a_ref[...]
    out_ref[pl.ds(other, length), :] = b_ref[...]


def place_output(pick, mine, got):
    length, dim = mine.shape
    whole = pl.BlockSpec((length, dim), lambda i, pick: (0, 0))
    return pl.pallas_call(
        place_output_kernel,
        grid_spec=pltpu.PrefetchScalarGridSpec(
            num_scalar_prefetch=1,
            grid=(1,),
            in_specs=[whole, pl.BlockSpec((length, dim), lambda i, pick: (1, 0))],
            out_specs=pl.BlockSpec((2 * length, dim), lambda i, pick: (0, 0)),
        ),
        out_shape=hbm((2 * length, dim), BF16),
        compiler_params=params(1),
        cost_estimate=cost(mine.size, 8 * mine.size),
        name="place_output",
    )(pick, mine, got)


def swap_perm(size, flip):
    return [(i, i ^ flip) for i in range(size)]


def encoding_rows(w_box):
    rows, cols = w_box.shape
    quarters = w_box.reshape(4, rows // 4, cols)
    return jnp.concatenate([quarters[i] for i in (0, 2, 1, 3)], axis=0)


def encoding_groups(groups, dim):
    quarter = dim // 4
    place = (0, 2, 1, 3)
    out = []
    for start, count in groups:
        while count:
            size = min(count, quarter - start % quarter)
            out.append((place[start // quarter] * quarter + start % quarter, size))
            start, count = start + size, count - size
    return out


def shards(
    shards_dp,
    tokens,
    boxes,
    resolution,
    w_query,
    bias_query,
    w_key,
    w_value,
    bias_value,
    w_box,
    w_out,
    bias_out,
    norm1_gain,
    norm1_bias,
    w_in,
    bias_in,
    w_back,
    bias_back,
    norm2_gain,
    norm2_bias,
    grad_out,
):
    dim = tokens.shape[1]
    pages = resolution.shape[0]
    length = tokens.shape[0] // pages
    hidden = w_in.shape[1]
    piece = hidden // 4
    here = lax.axis_index("head").astype(jnp.int32)
    spot = lax.axis_index("dp").astype(jnp.int32)
    core, x_index, z_index, corner = spot % 2, (spot // 2) % 2, spot // 4, spot % 4
    corner_z = (z_index % 2) * 2 + core
    pick = jnp.stack([here, 1 - here, core, 1 - core, x_index, z_index, corner, corner // 2, corner_z])
    groups = shard_groups(dim, shards_dp)
    fast = fast_path(dim, shards_dp)

    def over_head(value):
        return lax.ppermute(value, "head", [(0, 1), (1, 0)])

    def over_dp(value, flip):
        return lax.ppermute(value, "dp", swap_perm(shards_dp, flip))

    def after(value, *others):
        return lax.optimization_barrier((value, others))[0]

    in_first = over_head(lax.dynamic_slice_in_dim(w_in, corner * piece, piece, 1))
    back_first = over_head(lax.dynamic_slice_in_dim(w_back, corner_z * piece, piece, 0))
    bias_there = over_head(bias_in)

    quarter = w_box.shape[0] // 4
    freqs = np.exp(np.arange(quarter, dtype=np.float32) * np.float32(-math.log(10000.0) / quarter))
    freqs = jnp.asarray(np.concatenate([freqs, freqs])[None, :])
    box_t = encoding_rows(w_box).T

    def attend(which, tok):
        return attn_fwd(
            which, pick, resolution, tok, boxes, freqs, w_query, w_key, w_value, bias_query, bias_value,
            box_t, w_out, length, groups,
        )

    part_other, *saved_other = attend(1, tokens)
    got = over_head(part_other)
    in_first, back_first = after((in_first, back_first), part_other)
    in_second, back_second = over_dp(in_first, 2), over_dp(back_first, 4)
    in_near, back_near = over_dp(in_first, 1), over_dp(back_first, 1)
    part_own, *saved_own = attend(0, after(tokens, part_other))
    in_second, back_second = after((in_second, back_second), part_own)
    in_pieces = [in_first, in_near, in_second, over_dp(in_second, 1)]
    back_pieces = [back_first, back_near, back_second, over_dp(back_second, 1)]

    out_own, df_own, lhs, rhs, small = feed_forward(
        pick, tokens, part_own, got, grad_out,
        (bias_out, norm1_gain, norm1_bias, bias_back, norm2_gain, norm2_bias),
        bias_in, bias_there, w_in, w_back, in_pieces, back_pieces, groups,
    )
    df_other = over_head(df_own)
    box_groups = encoding_groups(groups, w_box.shape[0])

    def attend_back(df, saved, prev=None, extra=None, pick=pick):
        return attn_bwd(
            pick, df, saved, w_out, box_t, w_query, w_key, w_value, groups, box_groups, prev, extra
        )

    if fast:
        sent_a = ff_grad(pick, lhs, rhs, small, True)
        got_a = over_dp(sent_a, 1)
        sent_b = ff_grad(pick, lhs, after(rhs, sent_a), small, False)
        got_b = over_dp(sent_b, 1)
        xs_a, xk_a, small_1 = ff_grad(pick, lhs, after(rhs, sent_b), small, True, got_a)
        xg_a = over_dp(xs_a, 2)
        got_b = after(got_b, xs_a)
        xs_b, xk_b, small_b = ff_grad(pick, lhs, after(rhs, xs_a), small, False, got_b)
        df_own = after(df_own, xs_b)
    *part_a, inp_own = attend_back(df_own, saved_own)
    if fast:
        xg_a, df_other, xs_b = after((xg_a, df_other, xs_b), inp_own)
        own_a, sent_a, small_2 = add_x(pick, xk_a, after(xg_a, df_other), small_1, True)
        zg_a = over_dp(sent_a, 4)
        inp_send, df_other = after((inp_own, df_other), sent_a)
        xg_b = over_dp(xs_b, 2)
    else:
        inp_send = inp_own
    inp_own_got = over_head(inp_send)

    pick_back = pick if fast else pick.at[2:4].set(jnp.arange(2, dtype=jnp.int32))
    sent, kept, a_small, inp_other = attend_back(df_other, saved_other, part_a, out_own, pick_back)
    inp_other_got = over_head(inp_other)

    if fast:
        xg_b, zg_a, inp_own_got = after((xg_b, zg_a, inp_own_got), inp_other)
        sent, xk_b, zg_a = after((sent, xk_b, zg_a), xg_b, zg_a, inp_own_got)
        sent_got = over_dp(sent, 1)
        own_a, sent_a, small_3 = add_z(own_a, zg_a, small_2, True)
        own_b, sent_b = add_x(pick, after(xk_b, sent_a), xg_b, small_b, False)
        xs, xk, a_small = attn_split(pick, kept, after(sent_got, sent_b), a_small)
        xg = over_dp(xs, 2)
        zg_a, zg_b = over_dp(sent_a, 8), over_dp(sent_b, 4)
        grad_input = place_grad(1, pick, after(df_other, xs), inp_other, inp_own_got, pages)
        zg_a, zg_b = after((zg_a, zg_b), grad_input)
        own_b, sent_b = add_z(own_b, after(zg_b, zg_a), small_b, False)
        own, sent, a_small = add_x(pick, after(xk, sent_b), xg, a_small, True)
        zg = over_dp(sent, 4)
        zg_b = over_dp(sent_b, 8)
        a_sum, small_3 = for_head(own_a, after(zg_a, sent), small_3)
        df_own, inp_other_got = after((df_own, inp_other_got), a_sum)
        a_sum = over_head(a_sum)
        grad_input = place_grad(0, pick, df_own, inp_own, inp_other_got, pages, grad_input)
        own, sent, a_small = add_z(after(own, grad_input), zg, a_small, True)
        zg = over_dp(sent, 8)
        grad_in, grad_back, n2g, n2b, bias_back_sum, n1g, n1b, bias_out_sum, bias_in_sum = ff_last(
            pick, after(own_b, sent), zg_b, a_sum, small_3
        )
        output = place_output(pick, after(out_own, grad_in), inp_other_got)
        own = after(own, output)
        grad_q, grad_k, grad_v, grad_box, grad_wo, bq_sum, bv_sum = attn_last(own, zg, a_small)
        grad_back, grad_wo = grad_back.T, grad_wo.T
    else:
        scatter = lambda value, axis: lax.psum_scatter(
            value.astype(F32), "dp", scatter_dimension=axis, tiled=True
        )
        cores = [pick.at[3].set(c) for c in (0, 1)]
        halves = [
            scatter(
                jnp.concatenate([ff_grad(p, lhs, rhs, small, remote)[:, : dim // 2] for p in cores], axis=1), 1
            )
            for remote in (True, False)
        ]
        total = halves[1] + over_head(halves[0])
        grad_in, grad_back = total[0], total[1].T
        total = scatter(jnp.concatenate([kept, sent[: dim // 2]], axis=0), 0)
        total = total.reshape(total.shape[0], -1, 5, 2 * HEAD).transpose(2, 0, 1, 3)
        grad_q, grad_k, grad_v, grad_wo, grad_box = total.reshape(5, total.shape[1], -1)
        grad_wo = grad_wo.T
        small = lax.psum(small, ("dp", "head"))
        n2g, n2b, bias_back_sum, n1g, n1b, bias_out_sum = small[:3].reshape(6, dim)
        bias_in_sum = lax.dynamic_index_in_dim(small, 3 + here, 0, keepdims=False)
        bq_sum, bv_sum = lax.psum(a_small, "dp").reshape(-1, 5, 2 * HEAD)[:, :2].transpose(1, 0, 2).reshape(2, -1)
        output = place_output(pick, out_own, inp_other_got)
        grad_input = place_grad(1, pick, df_other, inp_other, inp_own_got, pages)
        grad_input = place_grad(0, pick, df_own, inp_own, inp_other_got, pages, grad_input)
    return (
        output,
        grad_input,
        grad_q,
        bq_sum,
        grad_k,
        grad_v,
        bv_sum,
        grad_box,
        grad_wo,
        bias_out_sum,
        n1g,
        n1b,
        grad_in,
        bias_in_sum,
        grad_back,
        bias_back_sum,
        n2g,
        n2b,
    )


def solution(mesh):
    placed = (
        P("dp", None),
        P(None, "dp"),
        P("dp"),
        P(None, "head"),
        P("head"),
        P(None, "head"),
        P(None, "head"),
        P("head"),
        P(None, "head"),
        P("head", None),
        P(),
        P(),
        P(),
        P(None, "head"),
        P("head"),
        P("head", None),
        P(),
        P(),
        P(),
        P("dp", None),
    )
    return jax.shard_map(
        partial(shards, mesh.shape["dp"]),
        mesh=mesh,
        in_specs=placed,
        out_specs=(
            P("dp", None),
            P("dp", None),
            P("dp", "head"),
            P("head"),
            P("dp", "head"),
            P("dp", "head"),
            P("head"),
            P("dp", "head"),
            P("head", "dp"),
            P(),
            P(),
            P(),
            P("dp", "head"),
            P("head"),
            P("head", "dp"),
            P(),
            P(),
            P(),
        ),
        check_vma=False,
    )
```

```python
from functools import partial
import math

import jax
import numpy as np
import jax.numpy as jnp
from jax import lax
from jax.experimental import pallas as pl
from jax.experimental.pallas import tpu as pltpu
from jax.sharding import PartitionSpec as P

HEAD = 64
F32 = jnp.float32
BF16 = jnp.bfloat16
VMEM_LIMIT = 63 * 1024 * 1024


def hbm(shape, dtype):
    return pltpu.HBM(tuple(shape), dtype)


def mm(a, b):
    return jnp.dot(a, b, preferred_element_type=F32)


def mm_nt(a, b):
    return lax.dot_general(a, b, (((1,), (1,)), ((), ())), preferred_element_type=F32)


def params(steps):
    return pltpu.CompilerParams(
        dimension_semantics=("arbitrary",) * steps, vmem_limit_bytes=VMEM_LIMIT
    )


def cost(flops, nbytes, trans=0):
    return pl.CostEstimate(flops=int(flops), bytes_accessed=int(nbytes), transcendentals=int(trans))


def sin_cos(angle):
    turns = jnp.floor(angle * (2.0 / math.pi) + 0.5)
    r = angle - turns * 1.5703125
    r = r - turns * 4.837512969970703125e-4
    r = r - turns * 7.54978995489188216e-8
    r2 = r * r
    s = r + r * r2 * (
        -1.6666654611e-1 + r2 * (8.3321608736e-3 + r2 * -1.9515295891e-4)
    )
    c = 1.0 - 0.5 * r2 + r2 * r2 * (
        4.166664568298827e-2 + r2 * (-1.388731625493765e-3 + r2 * 2.443315711809948e-5)
    )
    quad = turns.astype(jnp.int32)
    odd = (quad & 1) == 1
    sine = jnp.where(odd, c, s)
    cosine = jnp.where(odd, s, c)
    sine = jnp.where((quad & 2) == 2, -sine, sine)
    cosine = jnp.where(((quad + 1) & 2) == 2, -cosine, cosine)
    return sine, cosine


def lane_mask(shape, which):
    lanes = lax.broadcasted_iota(jnp.int32, shape, 1)
    return (lanes < HEAD) if which == 0 else (lanes >= HEAD)


def row_mask(shape, which):
    rows = lax.broadcasted_iota(jnp.int32, shape, 0)
    return (rows < HEAD) if which == 0 else (rows >= HEAD)


def keep(mask, x):
    return jnp.where(mask, x, jnp.zeros_like(x))


def attn_fwd_kernel(
    groups, which_page, pick, res, tok_ref, box_ref, freq_ref, wq_ref, wk_ref, wv_ref, bq_ref, bv_ref, wbt_ref, wo_ref,
    part_ref, p_ref, q_ref, k_ref, v_ref, ctx_ref, s_ref, c_ref, tok_t_ref, codes, mixed, acc, biases, s_keep, c_keep, t_keep, sems,
):
    step = pl.program_id(0)
    half = s_keep.shape[1]

    def leaving():
        pairs = ((s_keep, s_ref), (c_keep, c_ref), (t_keep, tok_t_ref))
        return [pltpu.make_async_copy(a, b, sems.at[n]) for n, (a, b) in enumerate(pairs)]

    @pl.when(step == 0)
    def _():
        rows = s_keep.shape[0]
        lanes = lax.broadcasted_iota(jnp.int32, (rows, half), 1)
        level = res[pick[which_page]]
        width = (612 + 204 * level).astype(F32)
        height = (792 + 264 * level).astype(F32)
        corners = box_ref[...]
        centre_x = (corners[0:1] + corners[2:3]).astype(F32) * 500.0 / width
        centre_y = (corners[1:2] + corners[3:4]).astype(F32) * 500.0 / height
        both = jnp.concatenate([centre_x, centre_y, jnp.zeros((6, rows), F32)], axis=0).T
        centre = jnp.where(lanes < half // 2, both[:, 0:1], both[:, 1:2])
        sine, cosine = sin_cos(centre * freq_ref[...])
        s_keep[...] = sine
        c_keep[...] = cosine
        codes[:, :half] = cosine.astype(BF16)
        codes[:, half : 2 * half] = sine.astype(BF16)
        acc[...] = jnp.zeros_like(acc)
        biases[0:1] = bq_ref[...].astype(F32).reshape(1, -1)
        biases[1:2] = bv_ref[...].astype(F32).reshape(1, -1)
        tok_t = split_rows(tok_ref[...].T, groups)
        t_keep[0] = tok_t[:half]
        t_keep[1] = tok_t[half:]
        for copy in leaving():
            copy.start()

    tok = tok_ref[...]
    rows = tok.shape[0]
    wide = wq_ref.shape[1]
    span = pl.ds(pl.multiple_of(step * wide, wide), wide)
    qkv = mm(tok, jnp.concatenate([wq_ref[...], wk_ref[...], wv_ref[...]], axis=1))
    q2 = (qkv[:, :wide] + biases[0:1, span]).astype(BF16) * BF16(0.125)
    k2 = qkv[:, wide : 2 * wide].astype(BF16)
    v2 = (qkv[:, 2 * wide :] + biases[1:2, span]).astype(BF16)
    q_ref[...] = q2
    k_ref[...] = k2
    v_ref[...] = v2
    codes[:, 2 * half :] = k2
    sine, cosine = s_keep[...], c_keep[...]
    for which in range(2):
        span = slice(which * rows, (which + 1) * rows)
        qm = keep(lane_mask(q2.shape, which), q2)
        off = mm(qm, wbt_ref[...])
        a, b = off[:, :half], off[:, half:]
        mixed[span, :half] = (a * sine + b * cosine).astype(BF16)
        mixed[span, half : 2 * half] = (b * sine - a * cosine).astype(BF16)
        mixed[span, 2 * half :] = qm
    parts = []
    for which in range(2):
        span = slice(which * rows, (which + 1) * rows)
        scores = mm_nt(mixed[span], codes[...])
        top = jnp.max(scores, axis=1, keepdims=True)
        raised = jnp.exp(scores - top)
        total = jnp.sum(raised, axis=1, keepdims=True)
        prob = (raised * (1.0 / total)).astype(BF16)
        p_ref[which] = prob
        parts.append(mm(prob, v2))
    ctx2 = jnp.where(lane_mask(parts[0].shape, 0), parts[0], parts[1]).astype(BF16)
    ctx_ref[...] = ctx2
    acc[...] += mm(ctx2, wo_ref[...])

    @pl.when(step == pl.num_programs(0) - 1)
    def _():
        part_ref[...] = acc[...].astype(BF16)
        for copy in leaving():
            copy.wait()


def attn_fwd(which_page, pick, res, tokens, boxes, freq, wq, wk, wv, bq, bv, wbt, wo, length, groups):
    dim = tokens.shape[1]
    inner = wq.shape[1]
    heads = inner // HEAD
    pairs = heads // 2
    wide = 2 * HEAD
    page = lambda i, pick, res: (pick[which_page], 0)
    fixed = lambda i, pick, res: (0, 0)
    cols = lambda i, pick, res: (0, i)
    rows = lambda i, pick, res: (i, 0)
    flops = 2 * length * (dim * inner * 4 + heads * (HEAD * dim + length * (dim + 2 * HEAD)))
    return pl.pallas_call(
        partial(attn_fwd_kernel, groups, which_page),
        grid_spec=pltpu.PrefetchScalarGridSpec(
            num_scalar_prefetch=2,
            grid=(pairs,),
            in_specs=[
                pl.BlockSpec((length, dim), page),
                pl.BlockSpec((4, length), lambda i, pick, res: (0, pick[which_page])),
                pl.BlockSpec((1, dim // 2), fixed),
                pl.BlockSpec((dim, wide), cols),
                pl.BlockSpec((dim, wide), cols),
                pl.BlockSpec((dim, wide), cols),
                pl.BlockSpec((inner,), lambda i, pick, res: (0,)),
                pl.BlockSpec((inner,), lambda i, pick, res: (0,)),
                pl.BlockSpec((wide, dim), rows),
                pl.BlockSpec((wide, dim), rows),
            ],
            out_specs=[
                pl.BlockSpec((length, dim), fixed),
                pl.BlockSpec((2, length, length), lambda i, pick, res: (i, 0, 0)),
                pl.BlockSpec((length, wide), cols),
                pl.BlockSpec((length, wide), cols),
                pl.BlockSpec((length, wide), cols),
                pl.BlockSpec((length, wide), cols),
                pl.BlockSpec(memory_space=pl.ANY),
                pl.BlockSpec(memory_space=pl.ANY),
                pl.BlockSpec(memory_space=pl.ANY),
            ],
            scratch_shapes=[
                pltpu.VMEM((length, dim + wide), BF16),
                pltpu.VMEM((2 * length, dim + wide), BF16),
                pltpu.VMEM((length, dim), F32),
                pltpu.VMEM((8, inner), F32),
                pltpu.VMEM((length, dim // 2), F32),
                pltpu.VMEM((length, dim // 2), F32),
                pltpu.VMEM((2, dim // 2, length), BF16),
                pltpu.SemaphoreType.DMA((3,)),
            ],
        ),
        out_shape=[
            hbm((length, dim), BF16),
            hbm((heads, length, length), BF16),
            hbm((length, inner), BF16),
            hbm((length, inner), BF16),
            hbm((length, inner), BF16),
            hbm((length, inner), BF16),
            hbm((length, dim // 2), F32),
            hbm((length, dim // 2), F32),
            hbm((2, dim // 2, length), BF16),
        ],
        compiler_params=params(1),
        cost_estimate=cost(flops, 10e6, heads * length * length),
        name="attn_fwd",
    )(pick, res, tokens, boxes, freq, wq, wk, wv, bq, bv, wbt, wo)


def attn_bwd_kernel(groups, box_groups, first, pick, *refs):
    (df_ref, tok_t_ref, ctx_ref, wo_ref, q_ref, k_ref, v_ref, p_ref, s_ref, c_ref, wbt_ref,
     wq_ref, wk_ref, wv_ref, *refs) = refs
    if first:
        part_ref, small_ref, inp_ref, codes, acc, df_t = refs
    else:
        prev_ref, prev_small_ref, extra_ref, *refs = refs
        sent_ref, kept_ref, small_ref, inp_ref, codes, acc, df_t, grads = refs
    step = pl.program_id(0)
    half = s_ref.shape[1]

    @pl.when(step == 0)
    def _():
        codes[:, :half] = c_ref[...].astype(BF16)
        codes[:, half:] = s_ref[...].astype(BF16)
        acc[...] = jnp.zeros_like(acc)
        turned = split_rows(df_ref[...].T, groups)
        df_t[0] = turned[:half]
        df_t[1] = turned[half:]

    sine, cosine = s_ref[...], c_ref[...]
    q2, k2, v2 = q_ref[...], k_ref[...], v_ref[...]
    dctx = mm_nt(df_ref[...], wo_ref[...]).astype(BF16)
    dctx_t = dctx.T
    q_t = q2.T
    wbt = wbt_ref[...]
    dq = jnp.zeros(q2.shape, F32)
    dk_t, dv_t, dwb = [], [], []
    for which in range(2):
        low, high = which * HEAD, (which + 1) * HEAD
        dm = keep(lane_mask(dctx.shape, which), dctx)
        prob = p_ref[which]
        grad_probs = mm_nt(dm, v2)
        dv_t.append(mm(dctx_t[low:high], prob))
        wide_prob = prob.astype(F32)
        both = wide_prob * grad_probs
        inner = jnp.sum(both, axis=1, keepdims=True)
        ds = (both - wide_prob * inner).astype(BF16)
        dk_t.append(mm(q_t[low:high], ds))
        km = keep(lane_mask(k2.shape, which), k2)
        ga = mm(ds, codes[:, :half]).astype(BF16).astype(F32)
        gb = mm(ds, codes[:, half:]).astype(BF16).astype(F32)
        oa = (ga * sine - gb * cosine).astype(BF16)
        ob = (gb * sine + ga * cosine).astype(BF16)
        wm = keep(row_mask(wbt.shape, which), wbt)
        dq = dq + (mm(ds, km) + mm_nt(oa, wm[:, :half]) + mm_nt(ob, wm[:, half:]))
        dwb.append(jnp.concatenate([mm(q_t[low:high], oa), mm(q_t[low:high], ob)], axis=1))
    dq2 = (dq * 0.125).astype(BF16)
    dk2 = jnp.concatenate(dk_t, axis=0).T.astype(BF16)
    dv2 = jnp.concatenate(dv_t, axis=0).T.astype(BF16)
    sides = jnp.concatenate([dq2, dk2, dv2], axis=1)
    acc[...] += mm_nt(sides, jnp.concatenate([wq_ref[...], wk_ref[...], wv_ref[...]], axis=1))

    box = split_rows(jnp.concatenate(dwb, axis=0).T, box_groups)
    ctx2 = ctx_ref[...]
    zeros = jnp.zeros((1, 3 * q2.shape[1]), F32)
    small = jnp.concatenate(
        [column_sum(dq2.astype(F32)), column_sum(dv2.astype(F32)), zeros], axis=1
    )
    if not first:
        small = small + prev_small_ref[...]
    small_ref[...] = small
    for h in range(2):
        grad = jnp.concatenate(
            [mm(tok_t_ref[h], sides), mm(df_t[h], ctx2), box[h * half : (h + 1) * half]], axis=1
        )
        if first:
            part_ref[h] = grad.astype(BF16)
        else:
            grads[h] = (grad + prev_ref[h].astype(F32)).astype(BF16)
    if not first:
        sent_ref[:half] = grads[pick[3]]
        sent_ref[half:] = wide_tail(small)
        kept_ref[...] = grads[pick[2]]

    @pl.when(step == pl.num_programs(0) - 1)
    def _():
        rows = acc.shape[0]
        inp_ref[:rows] = acc[...].astype(BF16)
        if not first:
            inp_ref[rows:] = extra_ref[...]


def attn_bwd(pick, df, saved, wo, wbt, wq, wk, wv, groups, box_groups, prev=None, extra=None):
    prob, q, k, v, ctx, sine, cosine, tok_t = saved
    length, dim = df.shape
    inner = wq.shape[1]
    heads = inner // HEAD
    pairs = heads // 2
    wide = 2 * HEAD
    first = prev is None
    sent = length if first else 2 * length
    fixed = lambda i, pick: (0, 0)
    cols = lambda i, pick: (0, i)
    rows = lambda i, pick: (i, 0)
    block = lambda i, pick: (0, 0, i)
    flops = 2 * length * (dim * inner * 8 + heads * (3 * HEAD * dim + length * (dim + 4 * HEAD)))
    part = pl.BlockSpec((2, dim // 2, 5 * wide), block)
    small = pl.BlockSpec((1, 5 * wide), cols)
    small_shape = hbm((1, 5 * inner), F32)
    inp = pl.BlockSpec((sent, dim), fixed)
    inp_shape = hbm((sent, dim), BF16)
    scratch = [
        pltpu.VMEM((length, dim), BF16),
        pltpu.VMEM((length, dim), F32),
        pltpu.VMEM((2, dim // 2, length), BF16),
    ]
    if first:
        out_specs = [part, small, inp]
        out_shape = [hbm((2, dim // 2, 5 * inner), BF16), small_shape, inp_shape]
        more_specs, more = [], []
    else:
        out_specs = [
            pl.BlockSpec((dim // 2 + TAIL, 5 * wide), cols), pl.BlockSpec((dim // 2, 5 * wide), cols), small, inp,
        ]
        out_shape = [
            hbm((dim // 2 + TAIL, 5 * inner), BF16), hbm((dim // 2, 5 * inner), BF16), small_shape, inp_shape,
        ]
        more_specs, more = [part, small, pl.BlockSpec((length, dim), fixed)], [*prev, extra]
        scratch.append(pltpu.VMEM((2, dim // 2, 5 * wide), BF16))
    return pl.pallas_call(
        partial(attn_bwd_kernel, groups, box_groups, first),
        grid_spec=pltpu.PrefetchScalarGridSpec(
            num_scalar_prefetch=1,
            grid=(pairs,),
            in_specs=[
                pl.BlockSpec((length, dim), fixed),
                pl.BlockSpec((2, dim // 2, length), lambda i, pick: (0, 0, 0)),
                pl.BlockSpec((length, wide), cols),
                pl.BlockSpec((wide, dim), rows),
                pl.BlockSpec((length, wide), cols),
                pl.BlockSpec((length, wide), cols),
                pl.BlockSpec((length, wide), cols),
                pl.BlockSpec((2, length, length), lambda i, pick: (i, 0, 0)),
                pl.BlockSpec((length, dim // 2), fixed),
                pl.BlockSpec((length, dim // 2), fixed),
                pl.BlockSpec((wide, dim), rows),
                pl.BlockSpec((dim, wide), cols),
                pl.BlockSpec((dim, wide), cols),
                pl.BlockSpec((dim, wide), cols),
            ]
            + more_specs,
            out_specs=out_specs,
            scratch_shapes=scratch,
        ),
        out_shape=out_shape,
        compiler_params=params(1),
        cost_estimate=cost(flops, 14e6),
        name="attn_bwd",
    )(pick, df, tok_t, ctx, wo, q, k, v, prob, sine, cosine, wbt, wq, wk, wv, *more)


def split_rows(x_t, groups):
    return jnp.concatenate([x_t[start : start + count] for start, count in groups], axis=0)


def shard_groups(dim, shards):
    rows = dim // shards
    if not fast_path(dim, shards):
        return [(0, dim)]
    order = [z * 4 + x * 2 + c for c in range(2) for z in range(shards // 4) for x in range(2)]
    return [(block * rows, rows) for block in order]


def fast_path(dim, shards):
    return shards == 16 and (dim // shards) % 16 == 0


def gelu_parts(v):
    e = jnp.exp(v * v * -0.5)
    t = 1.0 / (1.0 + (0.3275911 * math.sqrt(0.5)) * jnp.abs(v))
    poly = t * (
        0.5 * 0.254829592
        + t * (0.5 * -0.284496736 + t * (0.5 * 1.421413741 + t * (0.5 * -1.453152027 + t * (0.5 * 1.061405429))))
    )
    tail = poly * e
    phi = jnp.where(v >= 0, 1.0 - tail, tail)
    return phi, phi + v * (e * (1.0 / math.sqrt(2.0 * math.pi)))


def norm_stats(hidden):
    centred = hidden - jnp.mean(hidden, axis=1, keepdims=True)
    variance = jnp.mean(centred * centred, axis=1, keepdims=True)
    inv = lax.rsqrt(variance + 1e-05)
    return centred * inv, inv


def norm_back(grad, scaled, inv):
    return inv * (
        grad
        - jnp.mean(grad, axis=1, keepdims=True)
        - scaled * jnp.mean(grad * scaled, axis=1, keepdims=True)
    )


def column_sum(x):
    return jnp.sum(x, axis=0, keepdims=True)


def ff_kernel(
    groups, pick, tok_ref, part_ref, got_ref, gout_ref, bo_ref, g1_ref, b1_ref, bb_ref, g2_ref, b2_ref,
    bi_here, bi_there,
    wi_here, wb_here, wi0, wi1, wi2, wi3, wb0, wb1, wb2, wb3,
    out_ref, df_ref, lhs_ref, rhs_ref, small_ref,
    wi, wb, slope, norm_low, grad_low, acc, wide, bi_ref, rhs, gout_keep, out_keep, lhs, more_sems, sems,
):
    blocks, dim, cols = wi.shape
    here = blocks // 2
    piece = cols // 2
    remote = [(wi0, wb0), (wi1, wb1), (wi2, wb2), (wi3, wb3)]
    for p in range(2 * blocks):
        if p < blocks:
            at = (p % 2) * piece
            span = pl.ds(at, piece)
            source = (wi_here.at[:, pl.ds(p * piece, piece)], wb_here.at[pl.ds(p * piece, piece), :])
        else:
            span = pl.ds(pl.multiple_of(((pick[6] ^ p) & 1) * piece, piece), piece)
            source = remote[p - blocks]
            slot = here + ((((pick[8] ^ p) & 3) >> 1) ^ pick[7])
            span_back = pl.ds(pl.multiple_of(((pick[8] ^ p) & 1) * piece, piece), piece)
        pltpu.make_async_copy(source[0], wi.at[p // 2, :, span], sems.at[0, p]).start()
        if p < blocks:
            pltpu.make_async_copy(source[1], wb.at[p // 2, span, :], sems.at[1, p // 2]).start()
        else:
            pltpu.make_async_copy(source[1], wb.at[slot, span_back, :], sems.at[1, slot]).start()

    fetch = pltpu.make_async_copy(
        gout_ref.at[pl.ds(pl.multiple_of(pick[0] * gout_keep.shape[0], 8), gout_keep.shape[0]), :], gout_keep, more_sems.at[0]
    )
    fetch.start()
    out_copy = pltpu.make_async_copy(out_keep, out_ref, more_sems.at[1])
    lhs_copies = [pltpu.make_async_copy(lhs.at[m], lhs_ref.at[:, m], more_sems.at[2 + m]) for m in range(2)]

    def vec(ref):
        return ref[...].astype(F32).reshape(1, -1)

    here_at, there_at = pick[0] * here, pick[1] * here
    bias_here, bias_there = vec(bi_here), vec(bi_there)
    for j in range(here):
        bi_ref[pl.ds(here_at + j, 1), :] = bias_here[:, j * cols : (j + 1) * cols]
        bi_ref[pl.ds(there_at + j, 1), :] = bias_there[:, j * cols : (j + 1) * cols]

    def place(j):
        return jnp.where(j < here, here_at + j, there_at + (pick[7] ^ (j - here)))

    bo, g1, b1, bb, g2, b2 = (vec(r) for r in (bo_ref, g1_ref, b1_ref, bb_ref, g2_ref, b2_ref))
    first_sum = (
        tok_ref[...].astype(F32)
        + (part_ref[...].astype(F32) + got_ref[...].astype(F32))
        + bo
    )
    scaled1, inv1 = norm_stats(first_sum)
    normed = scaled1 * g1 + b1
    low = normed.astype(BF16)
    norm_low[...] = low
    wide[...] = normed + bb
    acc[...] = jnp.zeros_like(acc)
    low_t = split_rows(low.T, groups)
    split = low_t.shape[0] // 2
    lhs[0, 0] = low_t[:split]
    lhs[0, 1] = low_t[split:]
    lhs_copies[0].start()

    def leaving(m, j):
        return pltpu.make_async_copy(rhs.at[m, j], rhs_ref.at[m, j], sems.at[2 + m, j])

    def forward(j, _):
        for p in range(2):
            pltpu.make_async_copy(wi0, wi.at[j, :, pl.ds(0, piece)], sems.at[0, 2 * j + p]).wait()
        pltpu.make_async_copy(wb.at[j], wb.at[j], sems.at[1, j]).wait()
        pre = mm(norm_low[...], wi[j]) + bi_ref[pl.ds(place(j), 1), :]
        phi, step = gelu_parts(pre)
        act = (pre * phi).astype(BF16)
        rhs[1, j] = act
        leaving(1, j).start()
        slope[j] = step
        acc[...] += mm(act, wb[j])
        return 0

    lax.fori_loop(0, blocks, forward, 0)
    scaled2, inv2 = norm_stats(wide[...] + acc[...])
    out_keep[...] = (scaled2 * g2 + b2).astype(BF16)
    out_copy.start()
    fetch.wait()
    gout = gout_keep[...].astype(F32)
    small_gain2 = column_sum(gout * scaled2)
    small_bias2 = column_sum(gout)
    grad_second = norm_back(gout * g2, scaled2, inv2)
    small_back = column_sum(grad_second)
    low2 = grad_second.astype(BF16)
    grad_low[...] = low2
    low2_t = split_rows(low2.T, groups)
    lhs[1, 0] = low2_t[:split]
    lhs[1, 1] = low2_t[split:]
    lhs_copies[1].start()
    acc[...] = grad_second

    def backward(j, _):
        grad_act = mm_nt(grad_low[...], wb[j]).astype(BF16).astype(F32)
        grad_pre = (grad_act * slope[j]).astype(BF16)
        rhs[0, j] = grad_pre
        leaving(0, j).start()
        bi_ref[pl.ds(place(j), 1), :] = column_sum(grad_pre.astype(F32))
        acc[...] += mm_nt(grad_pre, wi[j])
        return 0

    lax.fori_loop(0, blocks, backward, 0)
    grad_normed = acc[...]
    first_sum = (
        tok_ref[...].astype(F32)
        + (part_ref[...].astype(F32) + got_ref[...].astype(F32))
        + bo
    )
    scaled1, inv1 = norm_stats(first_sum)
    small_gain1 = column_sum(grad_normed * scaled1)
    small_bias1 = column_sum(grad_normed)
    grad_first = norm_back(grad_normed * g1, scaled1, inv1)
    small_out = column_sum(grad_first)
    df_ref[...] = grad_first.astype(BF16)
    for m in range(2):
        for j in range(blocks):
            leaving(m, j).wait()
    for copy in [out_copy, *lhs_copies]:
        copy.wait()
    small_ref[...] = jnp.concatenate(
        [
            jnp.concatenate([small_gain2, small_bias2], axis=1),
            jnp.concatenate([small_back, small_gain1], axis=1),
            jnp.concatenate([small_bias1, small_out], axis=1),
            jnp.concatenate([bi_ref[j : j + 1] for j in range(here)], axis=1),
            jnp.concatenate([bi_ref[j : j + 1] for j in range(here, blocks)], axis=1),
            jnp.zeros((3, 2 * dim), F32),
        ],
        axis=0,
    )


def feed_forward(pick, tokens, part, got, grad_out, rows, bias_in, bias_there, wi_here, wb_here, wi_pieces, wb_pieces, groups):
    length, dim = part.shape
    cols = 2 * wi_pieces[0].shape[1]
    blocks = 2 * wi_here.shape[1] // cols
    page = lambda i, pick: (pick[0], 0)
    fixed = lambda i, pick: (0, 0)
    row = pl.BlockSpec((dim,), lambda i, pick: (0,))
    bias_row = pl.BlockSpec(bias_in.shape, lambda i, pick: (0,))
    whole = pl.BlockSpec((length, dim), fixed)
    anywhere = pl.BlockSpec(memory_space=pl.ANY)
    hidden = blocks * cols
    return pl.pallas_call(
        partial(ff_kernel, groups),
        grid_spec=pltpu.PrefetchScalarGridSpec(
            num_scalar_prefetch=1,
            grid=(1,),
            in_specs=[
                pl.BlockSpec((length, dim), page),
                whole,
                whole,
                anywhere,
                row, row, row, row, row, row,
                bias_row, bias_row,
            ]
            + [anywhere] * 10,
            out_specs=[
                anywhere,
                whole,
                anywhere,
                anywhere,
                pl.BlockSpec((8, 2 * dim), fixed),
            ],
            scratch_shapes=[
                pltpu.VMEM((blocks, dim, cols), BF16),
                pltpu.VMEM((blocks, cols, dim), BF16),
                pltpu.VMEM((blocks, length, cols), F32),
                pltpu.VMEM((length, dim), BF16),
                pltpu.VMEM((length, dim), BF16),
                pltpu.VMEM((length, dim), F32),
                pltpu.VMEM((length, dim), F32),
                pltpu.VMEM((blocks, cols), F32),
                pltpu.VMEM((2, blocks, length, cols), BF16),
                pltpu.VMEM((length, dim), BF16),
                pltpu.VMEM((length, dim), BF16),
                pltpu.VMEM((2, 2, dim // 2, length), BF16),
                pltpu.SemaphoreType.DMA((4,)),
                pltpu.SemaphoreType.DMA((4, 2 * blocks)),
            ],
        ),
        out_shape=[
            hbm((length, dim), BF16),
            hbm((length, dim), BF16),
            hbm((2, 2, dim // 2, length), BF16),
            hbm((2, blocks, length, cols), BF16),
            hbm((8, 2 * dim), F32),
        ],
        compiler_params=params(1),
        cost_estimate=cost(8 * length * dim * hidden, 4 * dim * hidden + 8 * length * hidden, length * hidden),
        name="feed_forward",
    )(pick, tokens, part, got, grad_out, *rows, bias_in, bias_there, wi_here, wb_here, *wi_pieces, *wb_pieces)


TAIL = 8


def split2(x):
    high = x.astype(BF16)
    return high, (x - high.astype(F32)).astype(BF16)


def rounded(x):
    high, low = split2(x)
    return high.astype(F32) + low.astype(F32)


def tall(x):
    if x.shape[0] == TAIL:
        return x
    return jnp.concatenate([x, jnp.zeros((TAIL - x.shape[0],) + x.shape[1:], x.dtype)], axis=0)


def ff_send_kernel(pick, lhs_ref, rhs_ref, small_ref, out_ref):
    rows = lhs_ref.shape[2]
    for m in range(2):
        out_ref[m, :rows] = mm(lhs_ref[0, m], rhs_ref[m, 0]).astype(BF16)
    for m, term in enumerate(split2(small_ref[...])):
        out_ref[m, rows:] = tall(term)


def ff_keep_kernel(pick, lhs_ref, rhs_ref, got_ref, small_ref, xs_ref, xk_ref, small_out, acc):
    rows = lhs_ref.shape[2]
    shard = acc.shape[0] // 8
    x_index = pick[4]
    for m in range(2):
        acc[...] = mm(lhs_ref[0, m], rhs_ref[m, 0]) + got_ref[m, :rows].astype(F32)
        for z in range(4):
            away = pl.multiple_of((2 * z + 1 - x_index) * shard, 8)
            mine = pl.multiple_of((2 * z + x_index) * shard, 8)
            xs_ref[m, z * shard : (z + 1) * shard] = acc[pl.ds(away, shard), :].astype(BF16)
            xk_ref[m, z * shard : (z + 1) * shard] = acc[pl.ds(mine, shard), :].astype(BF16)
    small = rounded(small_ref[...]) + (got_ref[0, rows : rows + 8].astype(F32) + got_ref[1, rows : rows + 8].astype(F32))
    small_out[...] = small
    for m, term in enumerate(split2(small)):
        xs_ref[m, 4 * shard :] = tall(term)


def ff_grad(pick, lhs, rhs, small, remote, got=None):
    _, mats, rows, length = lhs.shape
    _, blocks, _, cols = rhs.shape
    half = blocks // 2
    base = half if remote else 0
    which = 2 if got is not None else 3
    dest = (lambda j, pick: j ^ pick[7]) if remote else (lambda j, pick: j)
    column = lambda height: pl.BlockSpec((2, height, cols), lambda j, pick: (0, 0, dest(j, pick)))
    small_spec = pl.BlockSpec((8, cols), lambda j, pick: (0, dest(j, pick)))
    in_specs = [
        pl.BlockSpec((1, mats, rows, length), lambda j, pick: (pick[which], 0, 0, 0)),
        pl.BlockSpec((2, 1, length, cols), lambda j, pick: (0, base + j, 0, 0)),
    ]
    wide = half * cols
    estimate = cost(2 * mats * rows * length * wide, 10e6)
    if got is None:
        return pl.pallas_call(
            ff_send_kernel,
            grid_spec=pltpu.PrefetchScalarGridSpec(
                num_scalar_prefetch=1,
                grid=(half,),
                in_specs=in_specs + [small_spec],
                out_specs=column(rows + TAIL),
            ),
            out_shape=hbm((2, rows + TAIL, wide), BF16),
            compiler_params=params(1),
            cost_estimate=estimate,
            name="ff_grad_send",
        )(pick, lhs, rhs, small)
    return pl.pallas_call(
        ff_keep_kernel,
        grid_spec=pltpu.PrefetchScalarGridSpec(
            num_scalar_prefetch=1,
            grid=(half,),
            in_specs=in_specs + [column(rows + TAIL), small_spec],
            out_specs=[column(rows // 2 + TAIL), column(rows // 2), small_spec],
            scratch_shapes=[pltpu.VMEM((rows, cols), F32)],
        ),
        out_shape=[
            hbm((2, rows // 2 + TAIL, wide), BF16),
            hbm((2, rows // 2, wide), BF16),
            hbm((8, wide), F32),
        ],
        compiler_params=params(1),
        cost_estimate=estimate,
        name="ff_grad_keep",
    )(pick, lhs, rhs, got, small)


def wide_tail(vector):
    high, low = split2(vector)
    return tall(jnp.concatenate([high, low], axis=0))


def attn_split_kernel(pick, kept_ref, got_ref, small_ref, xs_ref, xk_ref, small_out, acc):
    rows = kept_ref.shape[0]
    acc[...] = kept_ref[...].astype(F32) + got_ref[:rows].astype(F32)
    x_index = pick[4]
    shard = rows // 8
    for z in range(4):
        away = pl.multiple_of((2 * z + 1 - x_index) * shard, 8)
        mine = pl.multiple_of((2 * z + x_index) * shard, 8)
        xs_ref[0, z * shard : (z + 1) * shard] = acc[pl.ds(away, shard), :].astype(BF16)
        xk_ref[0, z * shard : (z + 1) * shard] = acc[pl.ds(mine, shard), :].astype(BF16)
    small = rounded(small_ref[...]) + (
        got_ref[rows : rows + 1].astype(F32) + got_ref[rows + 1 : rows + 2].astype(F32)
    )
    small_out[...] = jnp.concatenate([small, jnp.zeros((7, small.shape[1]), F32)], axis=0)
    xs_ref[0, 4 * shard :] = wide_tail(small)


def attn_split(pick, kept, got, small):
    rows, cols = kept.shape
    steps = 3
    column = lambda height: pl.BlockSpec((height, cols // steps), lambda i, pick: (0, i))
    deep = lambda height: pl.BlockSpec((1, height, cols // steps), lambda i, pick: (0, 0, i))
    return pl.pallas_call(
        attn_split_kernel,
        grid_spec=pltpu.PrefetchScalarGridSpec(
            num_scalar_prefetch=1,
            grid=(steps,),
            in_specs=[column(rows), column(rows + TAIL), column(1)],
            out_specs=[deep(rows // 2 + TAIL), deep(rows // 2), column(8)],
            scratch_shapes=[pltpu.VMEM((rows, cols // steps), F32)],
        ),
        out_shape=[
            hbm((1, rows // 2 + TAIL, cols), BF16),
            hbm((1, rows // 2, cols), BF16),
            hbm((8, cols), F32),
        ],
        compiler_params=params(1),
        cost_estimate=cost(kept.size, 6 * kept.size),
        name="attn_split",
    )(pick, kept, got, small)


def tail_sum(ref, at):
    if ref.shape[0] == 2:
        return ref[0, at : at + 8].astype(F32) + ref[1, at : at + 8].astype(F32)
    one = ref[0, at : at + 1].astype(F32) + ref[0, at + 1 : at + 2].astype(F32)
    return jnp.concatenate([one, jnp.zeros((7, one.shape[1]), F32)], axis=0)


def put_tail(ref, at, small):
    if ref.shape[0] == 2:
        for m, term in enumerate(split2(small)):
            ref[m, at:] = tall(term)
    else:
        ref[0, at:] = wide_tail(small[0:1])


def add_x_kernel(tailed, pick, keep_ref, got_ref, small_ref, own, sent, *rest):
    shard = own.shape[1] // 2
    z = pick[5]
    for i, d in enumerate((0, 2, 1, 3)):
        at = pl.multiple_of((z ^ d) * shard, 16)
        ref = own if i < 2 else sent
        ref[:, (i % 2) * shard : (i % 2 + 1) * shard] = (
            keep_ref[:, pl.ds(at, shard), :].astype(F32) + got_ref[:, pl.ds(at, shard), :].astype(F32)
        ).astype(BF16)
    if tailed:
        small = rounded(small_ref[...]) + tail_sum(got_ref, 4 * shard)
        rest[0][...] = small
        put_tail(sent, 2 * shard, small)


def add_x(pick, kept, got, small, tailed):
    mats, rows, cols = kept.shape
    own = hbm((mats, rows // 2, cols), BF16)
    sent = hbm((mats, rows // 2 + (TAIL if tailed else 0), cols), BF16)
    full = lambda s: pl.BlockSpec(s.shape, lambda i, pick: (0,) * len(s.shape))
    extra = [hbm(small.shape, F32)] if tailed else []
    return pl.pallas_call(
        partial(add_x_kernel, tailed),
        grid_spec=pltpu.PrefetchScalarGridSpec(
            num_scalar_prefetch=1,
            grid=(1,),
            in_specs=[full(kept), full(got), full(small)],
            out_specs=[full(s) for s in [own, sent] + extra],
        ),
        out_shape=[own, sent] + extra,
        compiler_params=params(1),
        cost_estimate=cost(kept.size, 6 * kept.size),
        name="add_x",
    )(pick, kept, got, small)


def whole_call(kernel, out_shape, estimate, name, *args):
    full = lambda s: pl.BlockSpec(s.shape, lambda i: (0,) * len(s.shape))
    return pl.pallas_call(
        kernel,
        grid=(1,),
        in_specs=[full(a) for a in args],
        out_specs=[full(s) for s in out_shape],
        out_shape=out_shape,
        compiler_params=params(1),
        cost_estimate=estimate,
        name=name,
    )(*args)


def both(a, b):
    return a.astype(F32) + b.astype(F32)


def add_z_kernel(tailed, keep_ref, got_ref, small_ref, own, sent, *rest):
    shard = own.shape[1]
    own[...] = both(keep_ref[:, :shard], got_ref[:, :shard]).astype(BF16)
    sent[:, :shard] = both(keep_ref[:, shard:], got_ref[:, shard : 2 * shard]).astype(BF16)
    if tailed:
        small = rounded(small_ref[...]) + tail_sum(got_ref, 2 * shard)
        rest[0][...] = small
        put_tail(sent, shard, small)


def add_z(kept, got, small, tailed):
    mats, rows, cols = kept.shape
    shard = rows // 2
    out = [hbm((mats, shard, cols), BF16), hbm((mats, shard + (TAIL if tailed else 0), cols), BF16)]
    if tailed:
        out.append(hbm(small.shape, F32))
    return whole_call(
        partial(add_z_kernel, tailed), out, cost(4e10, 6 * kept.size), "add_z", kept, got, small
    )


def for_head_kernel(own, got, small_ref, out, small_out):
    shard = own.shape[1]
    out[:, :shard] = both(own[...], got[:, :shard]).astype(BF16)
    small = rounded(small_ref[...]) + tail_sum(got, shard)
    small_out[...] = small
    put_tail(out, shard, small)


def for_head(own, got, small):
    out = [hbm(got.shape, BF16), hbm(small.shape, F32)]
    return whole_call(for_head_kernel, out, cost(4e10, 6 * own.size), "for_head", own, got, small)


def ff_last_kernel(pick, own, z_got, got, small_ref, in_out, back_out, *vectors):
    small_out = vectors[-1]
    shard = own.shape[1]
    in_out[...] = both(own[0], z_got[0]) + got[0, :shard].astype(F32)
    back_out[...] = both(own[1], z_got[1]) + got[1, :shard].astype(F32)
    small = rounded(small_ref[...]) + tail_sum(got, shard)
    small_out[...] = small
    dim = small.shape[1] // 2
    for i in range(6):
        vectors[i][...] = small[i // 2 : i // 2 + 1, (i % 2) * dim : (i % 2 + 1) * dim].reshape(dim)
    vectors[6][...] = small_out[pl.ds(3 + pick[0], 1), :].reshape(2 * dim)


def ff_last(pick, own, z_got, got, small):
    _, rows, cols = own.shape
    dim = cols // 2
    full = lambda s: pl.BlockSpec(s.shape, lambda i, pick: (0,) * len(s.shape))
    out_shape = [hbm((rows, cols), F32)] * 2 + [hbm((dim,), F32)] * 6 + [hbm((cols,), F32)]
    return pl.pallas_call(
        ff_last_kernel,
        grid_spec=pltpu.PrefetchScalarGridSpec(
            num_scalar_prefetch=1,
            grid=(1,),
            in_specs=[full(own), full(z_got), full(got), full(small)],
            out_specs=[full(s) for s in out_shape],
            scratch_shapes=[pltpu.VMEM(small.shape, F32)],
        ),
        out_shape=out_shape,
        compiler_params=params(1),
        cost_estimate=cost(10 * got.size, 20 * got.size),
        name="ff_last",
    )(pick, own, z_got, got, small)


def attn_last_kernel(own, got, small_ref, q_out, k_out, v_out, box_out, wo_out, bq_out, bv_out):
    shard = own.shape[1]
    wide = 2 * HEAD
    pairs = q_out.shape[1] // wide
    small = rounded(small_ref[...]) + tail_sum(got, shard)
    for p in range(pairs):
        at = slice(p * wide, (p + 1) * wide)
        for i, ref in enumerate((q_out, k_out, v_out, wo_out, box_out)):
            span = slice((5 * p + i) * wide, (5 * p + i + 1) * wide)
            ref[:, at] = both(own[0, :, span], got[0, :shard, span])
    for i, ref in enumerate((bq_out, bv_out)):
        row = [small[0:1, (5 * p + i) * wide : (5 * p + i + 1) * wide] for p in range(pairs)]
        ref[...] = jnp.concatenate(row, axis=1).reshape(pairs * wide)


def attn_last(own, got, small):
    _, rows, cols = own.shape
    cols = cols // 5
    out = [hbm((rows, cols), F32)] * 5 + [hbm((cols,), F32)] * 2
    return whole_call(attn_last_kernel, out, cost(4 * own.size, 12 * own.size), "attn_last", own, got, small)


def place_grad_kernel(pick, df_ref, a_ref, b_ref, *refs):
    refs[-1][...] = df_ref[...].astype(F32) + (a_ref[...].astype(F32) + b_ref[...].astype(F32))


def place_grad(which, pick, df, mine, got, pages, into=None):
    length, dim = df.shape
    steps = 2
    part = pl.BlockSpec((length // steps, dim), lambda i, pick: (i, 0))
    args = [df, mine, got] + ([] if into is None else [into])
    return pl.pallas_call(
        place_grad_kernel,
        grid_spec=pltpu.PrefetchScalarGridSpec(
            num_scalar_prefetch=1,
            grid=(steps,),
            in_specs=[part] * 3 + ([] if into is None else [pl.BlockSpec(memory_space=pl.ANY)]),
            out_specs=pl.BlockSpec((length // steps, dim), lambda i, pick: (pick[which] * steps + i, 0)),
        ),
        out_shape=hbm((pages * length, dim), F32),
        input_output_aliases={} if into is None else {4: 0},
        compiler_params=params(1),
        cost_estimate=cost(3 * df.size, 10 * df.size),
        name="place_grad",
    )(pick, *args)


def place_output_kernel(pick, a_ref, b_ref, out_ref):
    length = a_ref.shape[0]
    own = pl.multiple_of(pick[0] * length, length)
    other = pl.multiple_of(pick[1] * length, length)
    out_ref[pl.ds(own, length), :] = a_ref[...]
    out_ref[pl.ds(other, length), :] = b_ref[...]


def place_output(pick, mine, got):
    length, dim = mine.shape
    whole = pl.BlockSpec((length, dim), lambda i, pick: (0, 0))
    return pl.pallas_call(
        place_output_kernel,
        grid_spec=pltpu.PrefetchScalarGridSpec(
            num_scalar_prefetch=1,
            grid=(1,),
            in_specs=[whole, pl.BlockSpec((length, dim), lambda i, pick: (1, 0))],
            out_specs=pl.BlockSpec((2 * length, dim), lambda i, pick: (0, 0)),
        ),
        out_shape=hbm((2 * length, dim), BF16),
        compiler_params=params(1),
        cost_estimate=cost(mine.size, 8 * mine.size),
        name="place_output",
    )(pick, mine, got)


def swap_perm(size, flip):
    return [(i, i ^ flip) for i in range(size)]


def encoding_rows(w_box):
    rows, cols = w_box.shape
    quarters = w_box.reshape(4, rows // 4, cols)
    return jnp.concatenate([quarters[i] for i in (0, 2, 1, 3)], axis=0)


def encoding_groups(groups, dim):
    quarter = dim // 4
    place = (0, 2, 1, 3)
    out = []
    for start, count in groups:
        while count:
            size = min(count, quarter - start % quarter)
            out.append((place[start // quarter] * quarter + start % quarter, size))
            start, count = start + size, count - size
    return out


def shards(
    shards_dp,
    tokens,
    boxes,
    resolution,
    w_query,
    bias_query,
    w_key,
    w_value,
    bias_value,
    w_box,
    w_out,
    bias_out,
    norm1_gain,
    norm1_bias,
    w_in,
    bias_in,
    w_back,
    bias_back,
    norm2_gain,
    norm2_bias,
    grad_out,
):
    dim = tokens.shape[1]
    pages = resolution.shape[0]
    length = tokens.shape[0] // pages
    hidden = w_in.shape[1]
    piece = hidden // 4
    here = lax.axis_index("head").astype(jnp.int32)
    spot = lax.axis_index("dp").astype(jnp.int32)
    core, x_index, z_index, corner = spot % 2, (spot // 2) % 2, spot // 4, spot % 4
    corner_z = (z_index % 2) * 2 + core
    pick = jnp.stack([here, 1 - here, core, 1 - core, x_index, z_index, corner, corner // 2, corner_z])
    groups = shard_groups(dim, shards_dp)
    fast = fast_path(dim, shards_dp)

    def over_head(value):
        return lax.ppermute(value, "head", [(0, 1), (1, 0)])

    def over_dp(value, flip):
        return lax.ppermute(value, "dp", swap_perm(shards_dp, flip))

    def after(value, *others):
        return lax.optimization_barrier((value, others))[0]

    in_first = over_head(lax.dynamic_slice_in_dim(w_in, corner * piece, piece, 1))
    back_first = over_head(lax.dynamic_slice_in_dim(w_back, corner_z * piece, piece, 0))
    bias_there = over_head(bias_in)

    quarter = w_box.shape[0] // 4
    freqs = np.exp(np.arange(quarter, dtype=np.float32) * np.float32(-math.log(10000.0) / quarter))
    freqs = jnp.asarray(np.concatenate([freqs, freqs])[None, :])
    box_t = encoding_rows(w_box).T

    def attend(which, tok):
        return attn_fwd(
            which, pick, resolution, tok, boxes, freqs, w_query, w_key, w_value, bias_query, bias_value,
            box_t, w_out, length, groups,
        )

    part_other, *saved_other = attend(1, tokens)
    got = over_head(part_other)
    in_first, back_first, bias_there = after((in_first, back_first, bias_there), part_other)
    in_second, back_second = over_dp(in_first, 2), over_dp(back_first, 4)
    in_near, back_near = over_dp(in_first, 1), over_dp(back_first, 1)
    part_own, *saved_own = attend(0, after(tokens, bias_there))
    in_near, back_near = after((in_near, back_near), part_own)
    in_second, back_second = after((in_second, back_second), in_near, back_near)
    in_pieces = [in_first, in_near, in_second, over_dp(in_second, 1)]
    back_pieces = [back_first, back_near, back_second, over_dp(back_second, 1)]

    out_own, df_own, lhs, rhs, small = feed_forward(
        pick, tokens, part_own, got, grad_out,
        (bias_out, norm1_gain, norm1_bias, bias_back, norm2_gain, norm2_bias),
        bias_in, bias_there, w_in, w_back, in_pieces, back_pieces, groups,
    )
    df_other = over_head(df_own)
    box_groups = encoding_groups(groups, w_box.shape[0])

    def attend_back(df, saved, prev=None, extra=None, pick=pick):
        return attn_bwd(
            pick, df, saved, w_out, box_t, w_query, w_key, w_value, groups, box_groups, prev, extra
        )

    if fast:
        sent_a = ff_grad(pick, lhs, rhs, small, True)
        got_a = over_dp(sent_a, 1)
        sent_b = ff_grad(pick, lhs, after(rhs, sent_a), small, False)
        got_b = over_dp(sent_b, 1)
        xs_a, xk_a, small_1 = ff_grad(pick, lhs, after(rhs, sent_b), small, True, got_a)
        xg_a = over_dp(xs_a, 2)
        got_b = after(got_b, xs_a)
        xs_b, xk_b, small_b = ff_grad(pick, lhs, after(rhs, xs_a), small, False, got_b)
        df_own = after(df_own, xs_b)
    *part_a, inp_own = attend_back(df_own, saved_own)
    if fast:
        xg_a, df_other, xs_b = after((xg_a, df_other, xs_b), inp_own)
        own_a, sent_a, small_2 = add_x(pick, xk_a, after(xg_a, df_other), small_1, True)
        zg_a = over_dp(sent_a, 4)
        inp_send, df_other = after((inp_own, df_other), sent_a)
        xg_b = over_dp(xs_b, 2)
    else:
        inp_send = inp_own
    inp_own_got = over_head(inp_send)

    pick_back = pick if fast else pick.at[2:4].set(jnp.arange(2, dtype=jnp.int32))
    sent, kept, a_small, inp_other = attend_back(df_other, saved_other, part_a, out_own, pick_back)
    inp_other_got = over_head(inp_other)

    if fast:
        xg_b, zg_a, inp_own_got = after((xg_b, zg_a, inp_own_got), inp_other)
        sent, xk_b, zg_a = after((sent, xk_b, zg_a), xg_b, zg_a, inp_own_got)
        sent_got = over_dp(sent, 1)
        own_a, sent_a, small_3 = add_z(own_a, zg_a, small_2, True)
        own_b, sent_b = add_x(pick, after(xk_b, sent_a), xg_b, small_b, False)
        xs, xk, a_small = attn_split(pick, kept, after(sent_got, sent_b), a_small)
        xg = over_dp(xs, 2)
        zg_a, zg_b = over_dp(sent_a, 8), over_dp(sent_b, 4)
        grad_input = place_grad(1, pick, after(df_other, xs), inp_other, inp_own_got, pages)
        zg_a, zg_b = after((zg_a, zg_b), grad_input)
        own_b, sent_b = add_z(own_b, after(zg_b, zg_a), small_b, False)
        own, sent, a_small = add_x(pick, after(xk, sent_b), xg, a_small, True)
        zg = over_dp(sent, 4)
        zg_b = over_dp(sent_b, 8)
        a_sum, small_3 = for_head(own_a, after(zg_a, sent), small_3)
        df_own, inp_other_got = after((df_own, inp_other_got), a_sum)
        a_sum = over_head(a_sum)
        grad_input = place_grad(0, pick, df_own, inp_own, inp_other_got, pages, grad_input)
        own, sent, a_small = add_z(after(own, grad_input), zg, a_small, True)
        zg = over_dp(sent, 8)
        grad_in, grad_back, n2g, n2b, bias_back_sum, n1g, n1b, bias_out_sum, bias_in_sum = ff_last(
            pick, after(own_b, sent), zg_b, a_sum, small_3
        )
        output = place_output(pick, after(out_own, grad_in), inp_other_got)
        own = after(own, output)
        grad_q, grad_k, grad_v, grad_box, grad_wo, bq_sum, bv_sum = attn_last(own, zg, a_small)
        grad_back, grad_wo = grad_back.T, grad_wo.T
    else:
        scatter = lambda value, axis: lax.psum_scatter(
            value.astype(F32), "dp", scatter_dimension=axis, tiled=True
        )
        cores = [pick.at[3].set(c) for c in (0, 1)]
        halves = [
            scatter(
                jnp.concatenate([ff_grad(p, lhs, rhs, small, remote)[:, : dim // 2] for p in cores], axis=1), 1
            )
            for remote in (True, False)
        ]
        total = halves[1] + over_head(halves[0])
        grad_in, grad_back = total[0], total[1].T
        total = scatter(jnp.concatenate([kept, sent[: dim // 2]], axis=0), 0)
        total = total.reshape(total.shape[0], -1, 5, 2 * HEAD).transpose(2, 0, 1, 3)
        grad_q, grad_k, grad_v, grad_wo, grad_box = total.reshape(5, total.shape[1], -1)
        grad_wo = grad_wo.T
        small = lax.psum(small, ("dp", "head"))
        n2g, n2b, bias_back_sum, n1g, n1b, bias_out_sum = small[:3].reshape(6, dim)
        bias_in_sum = lax.dynamic_index_in_dim(small, 3 + here, 0, keepdims=False)
        bq_sum, bv_sum = lax.psum(a_small, "dp").reshape(-1, 5, 2 * HEAD)[:, :2].transpose(1, 0, 2).reshape(2, -1)
        output = place_output(pick, out_own, inp_other_got)
        grad_input = place_grad(1, pick, df_other, inp_other, inp_own_got, pages)
        grad_input = place_grad(0, pick, df_own, inp_own, inp_other_got, pages, grad_input)
    return (
        output,
        grad_input,
        grad_q,
        bq_sum,
        grad_k,
        grad_v,
        bv_sum,
        grad_box,
        grad_wo,
        bias_out_sum,
        n1g,
        n1b,
        grad_in,
        bias_in_sum,
        grad_back,
        bias_back_sum,
        n2g,
        n2b,
    )


def solution(mesh):
    placed = (
        P("dp", None),
        P(None, "dp"),
        P("dp"),
        P(None, "head"),
        P("head"),
        P(None, "head"),
        P(None, "head"),
        P("head"),
        P(None, "head"),
        P("head", None),
        P(),
        P(),
        P(),
        P(None, "head"),
        P("head"),
        P("head", None),
        P(),
        P(),
        P(),
        P("dp", None),
    )
    return jax.shard_map(
        partial(shards, mesh.shape["dp"]),
        mesh=mesh,
        in_specs=placed,
        out_specs=(
            P("dp", None),
            P("dp", None),
            P("dp", "head"),
            P("head"),
            P("dp", "head"),
            P("dp", "head"),
            P("head"),
            P("dp", "head"),
            P("head", "dp"),
            P(),
            P(),
            P(),
            P("dp", "head"),
            P("head"),
            P("head", "dp"),
            P(),
            P(),
            P(),
        ),
        check_vma=False,
    )
```

```python
from functools import partial
import math

import jax
import numpy as np
import jax.numpy as jnp
from jax import lax
from jax.experimental import pallas as pl
from jax.experimental.pallas import tpu as pltpu
from jax.sharding import PartitionSpec as P

HEAD = 64
F32 = jnp.float32
BF16 = jnp.bfloat16
VMEM_LIMIT = 63 * 1024 * 1024


def hbm(shape, dtype):
    return pltpu.HBM(tuple(shape), dtype)


def mm(a, b):
    return jnp.dot(a, b, preferred_element_type=F32)


def mm_nt(a, b):
    return lax.dot_general(a, b, (((1,), (1,)), ((), ())), preferred_element_type=F32)


def params(steps):
    return pltpu.CompilerParams(
        dimension_semantics=("arbitrary",) * steps, vmem_limit_bytes=VMEM_LIMIT
    )


def cost(flops, nbytes, trans=0):
    return pl.CostEstimate(flops=int(flops), bytes_accessed=int(nbytes), transcendentals=int(trans))


def sin_cos(angle):
    turns = jnp.floor(angle * (2.0 / math.pi) + 0.5)
    r = angle - turns * 1.5703125
    r = r - turns * 4.837512969970703125e-4
    r = r - turns * 7.54978995489188216e-8
    r2 = r * r
    s = r + r * r2 * (
        -1.6666654611e-1 + r2 * (8.3321608736e-3 + r2 * -1.9515295891e-4)
    )
    c = 1.0 - 0.5 * r2 + r2 * r2 * (
        4.166664568298827e-2 + r2 * (-1.388731625493765e-3 + r2 * 2.443315711809948e-5)
    )
    quad = turns.astype(jnp.int32)
    odd = (quad & 1) == 1
    sine = jnp.where(odd, c, s)
    cosine = jnp.where(odd, s, c)
    sine = jnp.where((quad & 2) == 2, -sine, sine)
    cosine = jnp.where(((quad + 1) & 2) == 2, -cosine, cosine)
    return sine, cosine


def lane_mask(shape, which):
    lanes = lax.broadcasted_iota(jnp.int32, shape, 1)
    return (lanes < HEAD) if which == 0 else (lanes >= HEAD)


def row_mask(shape, which):
    rows = lax.broadcasted_iota(jnp.int32, shape, 0)
    return (rows < HEAD) if which == 0 else (rows >= HEAD)


def keep(mask, x):
    return jnp.where(mask, x, jnp.zeros_like(x))


def attn_fwd_kernel(
    groups, which_page, pick, res, tok_ref, box_ref, freq_ref, wq_ref, wk_ref, wv_ref, bq_ref, bv_ref, wbt_ref, wo_ref,
    part_ref, p_ref, q_ref, k_ref, v_ref, ctx_ref, s_ref, c_ref, tok_t_ref, codes, mixed, acc, biases, s_keep, c_keep, t_keep, sems,
):
    step = pl.program_id(0)
    half = s_keep.shape[1]

    def leaving():
        pairs = ((s_keep, s_ref), (c_keep, c_ref), (t_keep, tok_t_ref))
        return [pltpu.make_async_copy(a, b, sems.at[n]) for n, (a, b) in enumerate(pairs)]

    @pl.when(step == 0)
    def _():
        rows = s_keep.shape[0]
        lanes = lax.broadcasted_iota(jnp.int32, (rows, half), 1)
        level = res[pick[which_page]]
        width = (612 + 204 * level).astype(F32)
        height = (792 + 264 * level).astype(F32)
        corners = box_ref[...]
        centre_x = (corners[0:1] + corners[2:3]).astype(F32) * 500.0 / width
        centre_y = (corners[1:2] + corners[3:4]).astype(F32) * 500.0 / height
        both = jnp.concatenate([centre_x, centre_y, jnp.zeros((6, rows), F32)], axis=0).T
        centre = jnp.where(lanes < half // 2, both[:, 0:1], both[:, 1:2])
        sine, cosine = sin_cos(centre * freq_ref[...])
        s_keep[...] = sine
        c_keep[...] = cosine
        codes[:, :half] = cosine.astype(BF16)
        codes[:, half : 2 * half] = sine.astype(BF16)
        acc[...] = jnp.zeros_like(acc)
        biases[0:1] = bq_ref[...].astype(F32).reshape(1, -1)
        biases[1:2] = bv_ref[...].astype(F32).reshape(1, -1)
        tok_t = split_rows(tok_ref[...].T, groups)
        t_keep[0] = tok_t[:half]
        t_keep[1] = tok_t[half:]
        for copy in leaving():
            copy.start()

    tok = tok_ref[...]
    rows = tok.shape[0]
    wide = wq_ref.shape[1]
    span = pl.ds(pl.multiple_of(step * wide, wide), wide)
    qkv = mm(tok, jnp.concatenate([wq_ref[...], wk_ref[...], wv_ref[...]], axis=1))
    q2 = (qkv[:, :wide] + biases[0:1, span]).astype(BF16) * BF16(0.125)
    k2 = qkv[:, wide : 2 * wide].astype(BF16)
    v2 = (qkv[:, 2 * wide :] + biases[1:2, span]).astype(BF16)
    q_ref[...] = q2
    k_ref[...] = k2
    v_ref[...] = v2
    codes[:, 2 * half :] = k2
    sine, cosine = s_keep[...], c_keep[...]
    for which in range(2):
        span = slice(which * rows, (which + 1) * rows)
        qm = keep(lane_mask(q2.shape, which), q2)
        off = mm(qm, wbt_ref[...])
        a, b = off[:, :half], off[:, half:]
        mixed[span, :half] = (a * sine + b * cosine).astype(BF16)
        mixed[span, half : 2 * half] = (b * sine - a * cosine).astype(BF16)
        mixed[span, 2 * half :] = qm
    parts = []
    for which in range(2):
        span = slice(which * rows, (which + 1) * rows)
        scores = mm_nt(mixed[span], codes[...])
        top = jnp.max(scores, axis=1, keepdims=True)
        raised = jnp.exp(scores - top)
        total = jnp.sum(raised, axis=1, keepdims=True)
        prob = (raised * (1.0 / total)).astype(BF16)
        p_ref[which] = prob
        parts.append(mm(prob, v2))
    ctx2 = jnp.where(lane_mask(parts[0].shape, 0), parts[0], parts[1]).astype(BF16)
    ctx_ref[...] = ctx2
    acc[...] += mm(ctx2, wo_ref[...])

    @pl.when(step == pl.num_programs(0) - 1)
    def _():
        part_ref[...] = acc[...].astype(BF16)
        for copy in leaving():
            copy.wait()


def attn_fwd(which_page, pick, res, tokens, boxes, freq, wq, wk, wv, bq, bv, wbt, wo, length, groups):
    dim = tokens.shape[1]
    inner = wq.shape[1]
    heads = inner // HEAD
    pairs = heads // 2
    wide = 2 * HEAD
    page = lambda i, pick, res: (pick[which_page], 0)
    fixed = lambda i, pick, res: (0, 0)
    cols = lambda i, pick, res: (0, i)
    rows = lambda i, pick, res: (i, 0)
    flops = 2 * length * (dim * inner * 4 + heads * (HEAD * dim + length * (dim + 2 * HEAD)))
    return pl.pallas_call(
        partial(attn_fwd_kernel, groups, which_page),
        grid_spec=pltpu.PrefetchScalarGridSpec(
            num_scalar_prefetch=2,
            grid=(pairs,),
            in_specs=[
                pl.BlockSpec((length, dim), page),
                pl.BlockSpec((4, length), lambda i, pick, res: (0, pick[which_page])),
                pl.BlockSpec((1, dim // 2), fixed),
                pl.BlockSpec((dim, wide), cols),
                pl.BlockSpec((dim, wide), cols),
                pl.BlockSpec((dim, wide), cols),
                pl.BlockSpec((inner,), lambda i, pick, res: (0,)),
                pl.BlockSpec((inner,), lambda i, pick, res: (0,)),
                pl.BlockSpec((wide, dim), rows),
                pl.BlockSpec((wide, dim), rows),
            ],
            out_specs=[
                pl.BlockSpec((length, dim), fixed),
                pl.BlockSpec((2, length, length), lambda i, pick, res: (i, 0, 0)),
                pl.BlockSpec((length, wide), cols),
                pl.BlockSpec((length, wide), cols),
                pl.BlockSpec((length, wide), cols),
                pl.BlockSpec((length, wide), cols),
                pl.BlockSpec(memory_space=pl.ANY),
                pl.BlockSpec(memory_space=pl.ANY),
                pl.BlockSpec(memory_space=pl.ANY),
            ],
            scratch_shapes=[
                pltpu.VMEM((length, dim + wide), BF16),
                pltpu.VMEM((2 * length, dim + wide), BF16),
                pltpu.VMEM((length, dim), F32),
                pltpu.VMEM((8, inner), F32),
                pltpu.VMEM((length, dim // 2), F32),
                pltpu.VMEM((length, dim // 2), F32),
                pltpu.VMEM((2, dim // 2, length), BF16),
                pltpu.SemaphoreType.DMA((3,)),
            ],
        ),
        out_shape=[
            hbm((length, dim), BF16),
            hbm((heads, length, length), BF16),
            hbm((length, inner), BF16),
            hbm((length, inner), BF16),
            hbm((length, inner), BF16),
            hbm((length, inner), BF16),
            hbm((length, dim // 2), F32),
            hbm((length, dim // 2), F32),
            hbm((2, dim // 2, length), BF16),
        ],
        compiler_params=params(1),
        cost_estimate=cost(flops, 10e6, heads * length * length),
        name="attn_fwd",
    )(pick, res, tokens, boxes, freq, wq, wk, wv, bq, bv, wbt, wo)


def attn_bwd_kernel(groups, box_groups, first, pick, *refs):
    (df_ref, tok_t_ref, ctx_ref, wo_ref, q_ref, k_ref, v_ref, p_ref, s_ref, c_ref, wbt_ref,
     wq_ref, wk_ref, wv_ref, *refs) = refs
    if first:
        part_ref, small_ref, inp_ref, codes, acc, df_t = refs
    else:
        prev_ref, prev_small_ref, extra_ref, *refs = refs
        sent_ref, kept_ref, small_ref, inp_ref, codes, acc, df_t, grads = refs
    step = pl.program_id(0)
    half = s_ref.shape[1]

    @pl.when(step == 0)
    def _():
        codes[:, :half] = c_ref[...].astype(BF16)
        codes[:, half:] = s_ref[...].astype(BF16)
        acc[...] = jnp.zeros_like(acc)
        turned = split_rows(df_ref[...].T, groups)
        df_t[0] = turned[:half]
        df_t[1] = turned[half:]

    sine, cosine = s_ref[...], c_ref[...]
    q2, k2, v2 = q_ref[...], k_ref[...], v_ref[...]
    dctx = mm_nt(df_ref[...], wo_ref[...]).astype(BF16)
    dctx_t = dctx.T
    q_t = q2.T
    wbt = wbt_ref[...]
    dq = jnp.zeros(q2.shape, F32)
    dk_t, dv_t, dwb = [], [], []
    for which in range(2):
        low, high = which * HEAD, (which + 1) * HEAD
        dm = keep(lane_mask(dctx.shape, which), dctx)
        prob = p_ref[which]
        grad_probs = mm_nt(dm, v2)
        dv_t.append(mm(dctx_t[low:high], prob))
        wide_prob = prob.astype(F32)
        both = wide_prob * grad_probs
        inner = jnp.sum(both, axis=1, keepdims=True)
        ds = (both - wide_prob * inner).astype(BF16)
        dk_t.append(mm(q_t[low:high], ds))
        km = keep(lane_mask(k2.shape, which), k2)
        ga = mm(ds, codes[:, :half]).astype(BF16).astype(F32)
        gb = mm(ds, codes[:, half:]).astype(BF16).astype(F32)
        oa = (ga * sine - gb * cosine).astype(BF16)
        ob = (gb * sine + ga * cosine).astype(BF16)
        wm = keep(row_mask(wbt.shape, which), wbt)
        dq = dq + (mm(ds, km) + mm_nt(oa, wm[:, :half]) + mm_nt(ob, wm[:, half:]))
        dwb.append(jnp.concatenate([mm(q_t[low:high], oa), mm(q_t[low:high], ob)], axis=1))
    dq2 = (dq * 0.125).astype(BF16)
    dk2 = jnp.concatenate(dk_t, axis=0).T.astype(BF16)
    dv2 = jnp.concatenate(dv_t, axis=0).T.astype(BF16)
    sides = jnp.concatenate([dq2, dk2, dv2], axis=1)
    acc[...] += mm_nt(sides, jnp.concatenate([wq_ref[...], wk_ref[...], wv_ref[...]], axis=1))

    box = split_rows(jnp.concatenate(dwb, axis=0).T, box_groups)
    ctx2 = ctx_ref[...]
    zeros = jnp.zeros((1, 3 * q2.shape[1]), F32)
    small = jnp.concatenate(
        [column_sum(dq2.astype(F32)), column_sum(dv2.astype(F32)), zeros], axis=1
    )
    if not first:
        small = small + prev_small_ref[...]
    small_ref[...] = small
    for h in range(2):
        grad = jnp.concatenate(
            [mm(tok_t_ref[h], sides), mm(df_t[h], ctx2), box[h * half : (h + 1) * half]], axis=1
        )
        if first:
            part_ref[h] = grad.astype(BF16)
        else:
            grads[h] = (grad + prev_ref[h].astype(F32)).astype(BF16)
    if not first:
        sent_ref[:half] = grads[pick[3]]
        sent_ref[half:] = wide_tail(small)
        kept_ref[...] = grads[pick[2]]

    @pl.when(step == pl.num_programs(0) - 1)
    def _():
        rows = acc.shape[0]
        inp_ref[:rows] = acc[...].astype(BF16)
        if not first:
            inp_ref[rows:] = extra_ref[...]


def attn_bwd(pick, df, saved, wo, wbt, wq, wk, wv, groups, box_groups, prev=None, extra=None):
    prob, q, k, v, ctx, sine, cosine, tok_t = saved
    length, dim = df.shape
    inner = wq.shape[1]
    heads = inner // HEAD
    pairs = heads // 2
    wide = 2 * HEAD
    first = prev is None
    sent = length if first else 2 * length
    fixed = lambda i, pick: (0, 0)
    cols = lambda i, pick: (0, i)
    rows = lambda i, pick: (i, 0)
    block = lambda i, pick: (0, 0, i)
    flops = 2 * length * (dim * inner * 8 + heads * (3 * HEAD * dim + length * (dim + 4 * HEAD)))
    part = pl.BlockSpec((2, dim // 2, 5 * wide), block)
    small = pl.BlockSpec((1, 5 * wide), cols)
    small_shape = hbm((1, 5 * inner), F32)
    inp = pl.BlockSpec((sent, dim), fixed)
    inp_shape = hbm((sent, dim), BF16)
    scratch = [
        pltpu.VMEM((length, dim), BF16),
        pltpu.VMEM((length, dim), F32),
        pltpu.VMEM((2, dim // 2, length), BF16),
    ]
    if first:
        out_specs = [part, small, inp]
        out_shape = [hbm((2, dim // 2, 5 * inner), BF16), small_shape, inp_shape]
        more_specs, more = [], []
    else:
        out_specs = [
            pl.BlockSpec((dim // 2 + TAIL, 5 * wide), cols), pl.BlockSpec((dim // 2, 5 * wide), cols), small, inp,
        ]
        out_shape = [
            hbm((dim // 2 + TAIL, 5 * inner), BF16), hbm((dim // 2, 5 * inner), BF16), small_shape, inp_shape,
        ]
        more_specs, more = [part, small, pl.BlockSpec((length, dim), fixed)], [*prev, extra]
        scratch.append(pltpu.VMEM((2, dim // 2, 5 * wide), BF16))
    return pl.pallas_call(
        partial(attn_bwd_kernel, groups, box_groups, first),
        grid_spec=pltpu.PrefetchScalarGridSpec(
            num_scalar_prefetch=1,
            grid=(pairs,),
            in_specs=[
                pl.BlockSpec((length, dim), fixed),
                pl.BlockSpec((2, dim // 2, length), lambda i, pick: (0, 0, 0)),
                pl.BlockSpec((length, wide), cols),
                pl.BlockSpec((wide, dim), rows),
                pl.BlockSpec((length, wide), cols),
                pl.BlockSpec((length, wide), cols),
                pl.BlockSpec((length, wide), cols),
                pl.BlockSpec((2, length, length), lambda i, pick: (i, 0, 0)),
                pl.BlockSpec((length, dim // 2), fixed),
                pl.BlockSpec((length, dim // 2), fixed),
                pl.BlockSpec((wide, dim), rows),
                pl.BlockSpec((dim, wide), cols),
                pl.BlockSpec((dim, wide), cols),
                pl.BlockSpec((dim, wide), cols),
            ]
            + more_specs,
            out_specs=out_specs,
            scratch_shapes=scratch,
        ),
        out_shape=out_shape,
        compiler_params=params(1),
        cost_estimate=cost(flops, 14e6),
        name="attn_bwd",
    )(pick, df, tok_t, ctx, wo, q, k, v, prob, sine, cosine, wbt, wq, wk, wv, *more)


def split_rows(x_t, groups):
    return jnp.concatenate([x_t[start : start + count] for start, count in groups], axis=0)


def shard_groups(dim, shards):
    rows = dim // shards
    if not fast_path(dim, shards):
        return [(0, dim)]
    order = [z * 4 + x * 2 + c for c in range(2) for z in range(shards // 4) for x in range(2)]
    return [(block * rows, rows) for block in order]


def fast_path(dim, shards):
    return shards == 16 and (dim // shards) % 16 == 0


def gelu_parts(v):
    e = jnp.exp(v * v * -0.5)
    t = 1.0 / (1.0 + (0.3275911 * math.sqrt(0.5)) * jnp.abs(v))
    poly = t * (
        0.5 * 0.254829592
        + t * (0.5 * -0.284496736 + t * (0.5 * 1.421413741 + t * (0.5 * -1.453152027 + t * (0.5 * 1.061405429))))
    )
    tail = poly * e
    phi = jnp.where(v >= 0, 1.0 - tail, tail)
    return phi, phi + v * (e * (1.0 / math.sqrt(2.0 * math.pi)))


def norm_stats(hidden):
    centred = hidden - jnp.mean(hidden, axis=1, keepdims=True)
    variance = jnp.mean(centred * centred, axis=1, keepdims=True)
    inv = lax.rsqrt(variance + 1e-05)
    return centred * inv, inv


def norm_back(grad, scaled, inv):
    return inv * (
        grad
        - jnp.mean(grad, axis=1, keepdims=True)
        - scaled * jnp.mean(grad * scaled, axis=1, keepdims=True)
    )


def column_sum(x):
    return jnp.sum(x, axis=0, keepdims=True)


def ff_kernel(
    groups, pick, tok_ref, part_ref, got_ref, gout_ref, bo_ref, g1_ref, b1_ref, bb_ref, g2_ref, b2_ref,
    bi_here, bi_there,
    wi_here, wb_here, wi0, wi1, wi2, wi3, wb0, wb1, wb2, wb3,
    out_ref, df_ref, lhs_ref, rhs_ref, small_ref,
    wi, wb, slope, norm_low, grad_low, acc, wide, bi_ref, rhs, gout_keep, out_keep, lhs, more_sems, sems,
):
    blocks, dim, cols = wi.shape
    here = blocks // 2
    piece = cols // 2
    remote = [(wi0, wb0), (wi1, wb1), (wi2, wb2), (wi3, wb3)]
    for p in range(2 * blocks):
        if p < blocks:
            at = (p % 2) * piece
            span = pl.ds(at, piece)
            source = (wi_here.at[:, pl.ds(p * piece, piece)], wb_here.at[pl.ds(p * piece, piece), :])
        else:
            span = pl.ds(pl.multiple_of(((pick[6] ^ p) & 1) * piece, piece), piece)
            source = remote[p - blocks]
            slot = here + ((((pick[8] ^ p) & 3) >> 1) ^ pick[7])
            span_back = pl.ds(pl.multiple_of(((pick[8] ^ p) & 1) * piece, piece), piece)
        pltpu.make_async_copy(source[0], wi.at[p // 2, :, span], sems.at[0, p]).start()
        if p < blocks:
            pltpu.make_async_copy(source[1], wb.at[p // 2, span, :], sems.at[1, p // 2]).start()
        else:
            pltpu.make_async_copy(source[1], wb.at[slot, span_back, :], sems.at[1, slot]).start()

    fetch = pltpu.make_async_copy(
        gout_ref.at[pl.ds(pl.multiple_of(pick[0] * gout_keep.shape[0], 8), gout_keep.shape[0]), :], gout_keep, more_sems.at[0]
    )
    fetch.start()
    out_copy = pltpu.make_async_copy(out_keep, out_ref, more_sems.at[1])
    lhs_copies = [pltpu.make_async_copy(lhs.at[m], lhs_ref.at[:, m], more_sems.at[2 + m]) for m in range(2)]

    def vec(ref):
        return ref[...].astype(F32).reshape(1, -1)

    here_at, there_at = pick[0] * here, pick[1] * here
    bias_here, bias_there = vec(bi_here), vec(bi_there)
    for j in range(here):
        bi_ref[pl.ds(here_at + j, 1), :] = bias_here[:, j * cols : (j + 1) * cols]
        bi_ref[pl.ds(there_at + j, 1), :] = bias_there[:, j * cols : (j + 1) * cols]

    def place(j):
        return jnp.where(j < here, here_at + j, there_at + (pick[7] ^ (j - here)))

    bo, g1, b1, bb, g2, b2 = (vec(r) for r in (bo_ref, g1_ref, b1_ref, bb_ref, g2_ref, b2_ref))
    first_sum = (
        tok_ref[...].astype(F32)
        + (part_ref[...].astype(F32) + got_ref[...].astype(F32))
        + bo
    )
    scaled1, inv1 = norm_stats(first_sum)
    normed = scaled1 * g1 + b1
    low = normed.astype(BF16)
    norm_low[...] = low
    wide[...] = normed + bb
    acc[...] = jnp.zeros_like(acc)
    low_t = split_rows(low.T, groups)
    split = low_t.shape[0] // 2
    lhs[0, 0] = low_t[:split]
    lhs[0, 1] = low_t[split:]
    lhs_copies[0].start()

    def leaving(m, j):
        return pltpu.make_async_copy(rhs.at[m, j], rhs_ref.at[m, j], sems.at[2 + m, j])

    def forward(j, _):
        for p in range(2):
            pltpu.make_async_copy(wi0, wi.at[j, :, pl.ds(0, piece)], sems.at[0, 2 * j + p]).wait()
        pltpu.make_async_copy(wb.at[j], wb.at[j], sems.at[1, j]).wait()
        pre = mm(norm_low[...], wi[j]) + bi_ref[pl.ds(place(j), 1), :]
        phi, step = gelu_parts(pre)
        act = (pre * phi).astype(BF16)
        rhs[1, j] = act
        leaving(1, j).start()
        slope[j] = step
        acc[...] += mm(act, wb[j])
        return 0

    lax.fori_loop(0, blocks, forward, 0)
    scaled2, inv2 = norm_stats(wide[...] + acc[...])
    out_keep[...] = (scaled2 * g2 + b2).astype(BF16)
    out_copy.start()
    fetch.wait()
    gout = gout_keep[...].astype(F32)
    small_gain2 = column_sum(gout * scaled2)
    small_bias2 = column_sum(gout)
    grad_second = norm_back(gout * g2, scaled2, inv2)
    small_back = column_sum(grad_second)
    low2 = grad_second.astype(BF16)
    grad_low[...] = low2
    low2_t = split_rows(low2.T, groups)
    lhs[1, 0] = low2_t[:split]
    lhs[1, 1] = low2_t[split:]
    lhs_copies[1].start()
    acc[...] = grad_second

    def backward(j, _):
        grad_act = mm_nt(grad_low[...], wb[j]).astype(BF16).astype(F32)
        grad_pre = (grad_act * slope[j]).astype(BF16)
        rhs[0, j] = grad_pre
        leaving(0, j).start()
        bi_ref[pl.ds(place(j), 1), :] = column_sum(grad_pre.astype(F32))
        acc[...] += mm_nt(grad_pre, wi[j])
        return 0

    lax.fori_loop(0, blocks, backward, 0)
    grad_normed = acc[...]
    first_sum = (
        tok_ref[...].astype(F32)
        + (part_ref[...].astype(F32) + got_ref[...].astype(F32))
        + bo
    )
    scaled1, inv1 = norm_stats(first_sum)
    small_gain1 = column_sum(grad_normed * scaled1)
    small_bias1 = column_sum(grad_normed)
    grad_first = norm_back(grad_normed * g1, scaled1, inv1)
    small_out = column_sum(grad_first)
    df_ref[...] = grad_first.astype(BF16)
    for m in range(2):
        for j in range(blocks):
            leaving(m, j).wait()
    for copy in [out_copy, *lhs_copies]:
        copy.wait()
    small_ref[...] = jnp.concatenate(
        [
            jnp.concatenate([small_gain2, small_bias2], axis=1),
            jnp.concatenate([small_back, small_gain1], axis=1),
            jnp.concatenate([small_bias1, small_out], axis=1),
            jnp.concatenate([bi_ref[j : j + 1] for j in range(here)], axis=1),
            jnp.concatenate([bi_ref[j : j + 1] for j in range(here, blocks)], axis=1),
            jnp.zeros((3, 2 * dim), F32),
        ],
        axis=0,
    )


def feed_forward(pick, tokens, part, got, grad_out, rows, bias_in, bias_there, wi_here, wb_here, wi_pieces, wb_pieces, groups):
    length, dim = part.shape
    cols = 2 * wi_pieces[0].shape[1]
    blocks = 2 * wi_here.shape[1] // cols
    page = lambda i, pick: (pick[0], 0)
    fixed = lambda i, pick: (0, 0)
    row = pl.BlockSpec((dim,), lambda i, pick: (0,))
    bias_row = pl.BlockSpec(bias_in.shape, lambda i, pick: (0,))
    whole = pl.BlockSpec((length, dim), fixed)
    anywhere = pl.BlockSpec(memory_space=pl.ANY)
    hidden = blocks * cols
    return pl.pallas_call(
        partial(ff_kernel, groups),
        grid_spec=pltpu.PrefetchScalarGridSpec(
            num_scalar_prefetch=1,
            grid=(1,),
            in_specs=[
                pl.BlockSpec((length, dim), page),
                whole,
                whole,
                anywhere,
                row, row, row, row, row, row,
                bias_row, bias_row,
            ]
            + [anywhere] * 10,
            out_specs=[
                anywhere,
                whole,
                anywhere,
                anywhere,
                pl.BlockSpec((8, 2 * dim), fixed),
            ],
            scratch_shapes=[
                pltpu.VMEM((blocks, dim, cols), BF16),
                pltpu.VMEM((blocks, cols, dim), BF16),
                pltpu.VMEM((blocks, length, cols), F32),
                pltpu.VMEM((length, dim), BF16),
                pltpu.VMEM((length, dim), BF16),
                pltpu.VMEM((length, dim), F32),
                pltpu.VMEM((length, dim), F32),
                pltpu.VMEM((blocks, cols), F32),
                pltpu.VMEM((2, blocks, length, cols), BF16),
                pltpu.VMEM((length, dim), BF16),
                pltpu.VMEM((length, dim), BF16),
                pltpu.VMEM((2, 2, dim // 2, length), BF16),
                pltpu.SemaphoreType.DMA((4,)),
                pltpu.SemaphoreType.DMA((4, 2 * blocks)),
            ],
        ),
        out_shape=[
            hbm((length, dim), BF16),
            hbm((length, dim), BF16),
            hbm((2, 2, dim // 2, length), BF16),
            hbm((2, blocks, length, cols), BF16),
            hbm((8, 2 * dim), F32),
        ],
        compiler_params=params(1),
        cost_estimate=cost(8 * length * dim * hidden, 4 * dim * hidden + 8 * length * hidden, length * hidden),
        name="feed_forward",
    )(pick, tokens, part, got, grad_out, *rows, bias_in, bias_there, wi_here, wb_here, *wi_pieces, *wb_pieces)


TAIL = 8


def split2(x):
    high = x.astype(BF16)
    return high, (x - high.astype(F32)).astype(BF16)


def rounded(x):
    high, low = split2(x)
    return high.astype(F32) + low.astype(F32)


def tall(x):
    if x.shape[0] == TAIL:
        return x
    return jnp.concatenate([x, jnp.zeros((TAIL - x.shape[0],) + x.shape[1:], x.dtype)], axis=0)


def ff_send_kernel(pick, lhs_ref, rhs_ref, small_ref, out_ref):
    rows = lhs_ref.shape[2]
    for m in range(2):
        out_ref[m, :rows] = mm(lhs_ref[0, m], rhs_ref[m, 0]).astype(BF16)
    for m, term in enumerate(split2(small_ref[...])):
        out_ref[m, rows:] = tall(term)


def ff_keep_kernel(pick, lhs_ref, rhs_ref, got_ref, small_ref, xs_ref, xk_ref, small_out, acc):
    rows = lhs_ref.shape[2]
    shard = acc.shape[0] // 8
    x_index = pick[4]
    for m in range(2):
        acc[...] = mm(lhs_ref[0, m], rhs_ref[m, 0]) + got_ref[m, :rows].astype(F32)
        for z in range(4):
            away = pl.multiple_of((2 * z + 1 - x_index) * shard, 8)
            mine = pl.multiple_of((2 * z + x_index) * shard, 8)
            xs_ref[m, z * shard : (z + 1) * shard] = acc[pl.ds(away, shard), :].astype(BF16)
            xk_ref[m, z * shard : (z + 1) * shard] = acc[pl.ds(mine, shard), :].astype(BF16)
    small = rounded(small_ref[...]) + (got_ref[0, rows : rows + 8].astype(F32) + got_ref[1, rows : rows + 8].astype(F32))
    small_out[...] = small
    for m, term in enumerate(split2(small)):
        xs_ref[m, 4 * shard :] = tall(term)


def ff_grad(pick, lhs, rhs, small, remote, got=None):
    _, mats, rows, length = lhs.shape
    _, blocks, _, cols = rhs.shape
    half = blocks // 2
    base = half if remote else 0
    which = 2 if got is not None else 3
    dest = (lambda j, pick: j ^ pick[7]) if remote else (lambda j, pick: j)
    column = lambda height: pl.BlockSpec((2, height, cols), lambda j, pick: (0, 0, dest(j, pick)))
    small_spec = pl.BlockSpec((8, cols), lambda j, pick: (0, dest(j, pick)))
    in_specs = [
        pl.BlockSpec((1, mats, rows, length), lambda j, pick: (pick[which], 0, 0, 0)),
        pl.BlockSpec((2, 1, length, cols), lambda j, pick: (0, base + j, 0, 0)),
    ]
    wide = half * cols
    estimate = cost(2 * mats * rows * length * wide, 10e6)
    if got is None:
        return pl.pallas_call(
            ff_send_kernel,
            grid_spec=pltpu.PrefetchScalarGridSpec(
                num_scalar_prefetch=1,
                grid=(half,),
                in_specs=in_specs + [small_spec],
                out_specs=column(rows + TAIL),
            ),
            out_shape=hbm((2, rows + TAIL, wide), BF16),
            compiler_params=params(1),
            cost_estimate=estimate,
            name="ff_grad_send",
        )(pick, lhs, rhs, small)
    return pl.pallas_call(
        ff_keep_kernel,
        grid_spec=pltpu.PrefetchScalarGridSpec(
            num_scalar_prefetch=1,
            grid=(half,),
            in_specs=in_specs + [column(rows + TAIL), small_spec],
            out_specs=[column(rows // 2 + TAIL), column(rows // 2), small_spec],
            scratch_shapes=[pltpu.VMEM((rows, cols), F32)],
        ),
        out_shape=[
            hbm((2, rows // 2 + TAIL, wide), BF16),
            hbm((2, rows // 2, wide), BF16),
            hbm((8, wide), F32),
        ],
        compiler_params=params(1),
        cost_estimate=estimate,
        name="ff_grad_keep",
    )(pick, lhs, rhs, got, small)


def wide_tail(vector):
    high, low = split2(vector)
    return tall(jnp.concatenate([high, low], axis=0))


def attn_split_kernel(pick, kept_ref, got_ref, small_ref, xs_ref, xk_ref, small_out, acc):
    rows = kept_ref.shape[0]
    acc[...] = kept_ref[...].astype(F32) + got_ref[:rows].astype(F32)
    x_index = pick[4]
    shard = rows // 8
    for z in range(4):
        away = pl.multiple_of((2 * z + 1 - x_index) * shard, 8)
        mine = pl.multiple_of((2 * z + x_index) * shard, 8)
        xs_ref[0, z * shard : (z + 1) * shard] = acc[pl.ds(away, shard), :].astype(BF16)
        xk_ref[0, z * shard : (z + 1) * shard] = acc[pl.ds(mine, shard), :].astype(BF16)
    small = rounded(small_ref[...]) + (
        got_ref[rows : rows + 1].astype(F32) + got_ref[rows + 1 : rows + 2].astype(F32)
    )
    small_out[...] = jnp.concatenate([small, jnp.zeros((7, small.shape[1]), F32)], axis=0)
    xs_ref[0, 4 * shard :] = wide_tail(small)


def attn_split(pick, kept, got, small):
    rows, cols = kept.shape
    steps = 3
    column = lambda height: pl.BlockSpec((height, cols // steps), lambda i, pick: (0, i))
    deep = lambda height: pl.BlockSpec((1, height, cols // steps), lambda i, pick: (0, 0, i))
    return pl.pallas_call(
        attn_split_kernel,
        grid_spec=pltpu.PrefetchScalarGridSpec(
            num_scalar_prefetch=1,
            grid=(steps,),
            in_specs=[column(rows), column(rows + TAIL), column(1)],
            out_specs=[deep(rows // 2 + TAIL), deep(rows // 2), column(8)],
            scratch_shapes=[pltpu.VMEM((rows, cols // steps), F32)],
        ),
        out_shape=[
            hbm((1, rows // 2 + TAIL, cols), BF16),
            hbm((1, rows // 2, cols), BF16),
            hbm((8, cols), F32),
        ],
        compiler_params=params(1),
        cost_estimate=cost(kept.size, 6 * kept.size),
        name="attn_split",
    )(pick, kept, got, small)


def tail_sum(ref, at):
    if ref.shape[0] == 2:
        return ref[0, at : at + 8].astype(F32) + ref[1, at : at + 8].astype(F32)
    one = ref[0, at : at + 1].astype(F32) + ref[0, at + 1 : at + 2].astype(F32)
    return jnp.concatenate([one, jnp.zeros((7, one.shape[1]), F32)], axis=0)


def put_tail(ref, at, small):
    if ref.shape[0] == 2:
        for m, term in enumerate(split2(small)):
            ref[m, at:] = tall(term)
    else:
        ref[0, at:] = wide_tail(small[0:1])


def add_x_kernel(tailed, pick, keep_ref, got_ref, small_ref, own, sent, *rest):
    shard = own.shape[1] // 2
    z = pick[5]
    for i, d in enumerate((0, 2, 1, 3)):
        at = pl.multiple_of((z ^ d) * shard, 16)
        ref = own if i < 2 else sent
        ref[:, (i % 2) * shard : (i % 2 + 1) * shard] = (
            keep_ref[:, pl.ds(at, shard), :].astype(F32) + got_ref[:, pl.ds(at, shard), :].astype(F32)
        ).astype(BF16)
    if tailed:
        small = rounded(small_ref[...]) + tail_sum(got_ref, 4 * shard)
        rest[0][...] = small
        put_tail(sent, 2 * shard, small)


def add_x(pick, kept, got, small, tailed):
    mats, rows, cols = kept.shape
    own = hbm((mats, rows // 2, cols), BF16)
    sent = hbm((mats, rows // 2 + (TAIL if tailed else 0), cols), BF16)
    full = lambda s: pl.BlockSpec(s.shape, lambda i, pick: (0,) * len(s.shape))
    extra = [hbm(small.shape, F32)] if tailed else []
    return pl.pallas_call(
        partial(add_x_kernel, tailed),
        grid_spec=pltpu.PrefetchScalarGridSpec(
            num_scalar_prefetch=1,
            grid=(1,),
            in_specs=[full(kept), full(got), full(small)],
            out_specs=[full(s) for s in [own, sent] + extra],
        ),
        out_shape=[own, sent] + extra,
        compiler_params=params(1),
        cost_estimate=cost(kept.size, 6 * kept.size),
        name="add_x",
    )(pick, kept, got, small)


def whole_call(kernel, out_shape, estimate, name, *args):
    full = lambda s: pl.BlockSpec(s.shape, lambda i: (0,) * len(s.shape))
    return pl.pallas_call(
        kernel,
        grid=(1,),
        in_specs=[full(a) for a in args],
        out_specs=[full(s) for s in out_shape],
        out_shape=out_shape,
        compiler_params=params(1),
        cost_estimate=estimate,
        name=name,
    )(*args)


def both(a, b):
    return a.astype(F32) + b.astype(F32)


def add_z_kernel(tailed, keep_ref, got_ref, small_ref, own, sent, *rest):
    shard = own.shape[1]
    own[...] = both(keep_ref[:, :shard], got_ref[:, :shard]).astype(BF16)
    sent[:, :shard] = both(keep_ref[:, shard:], got_ref[:, shard : 2 * shard]).astype(BF16)
    if tailed:
        small = rounded(small_ref[...]) + tail_sum(got_ref, 2 * shard)
        rest[0][...] = small
        put_tail(sent, shard, small)


def add_z(kept, got, small, tailed):
    mats, rows, cols = kept.shape
    shard = rows // 2
    out = [hbm((mats, shard, cols), BF16), hbm((mats, shard + (TAIL if tailed else 0), cols), BF16)]
    if tailed:
        out.append(hbm(small.shape, F32))
    return whole_call(
        partial(add_z_kernel, tailed), out, cost(4e10, 6 * kept.size), "add_z", kept, got, small
    )


def for_head_kernel(own, got, small_ref, out, small_out):
    shard = own.shape[1]
    out[:, :shard] = both(own[...], got[:, :shard]).astype(BF16)
    small = rounded(small_ref[...]) + tail_sum(got, shard)
    small_out[...] = small
    put_tail(out, shard, small)


def for_head(own, got, small):
    out = [hbm(got.shape, BF16), hbm(small.shape, F32)]
    return whole_call(for_head_kernel, out, cost(4e10, 6 * own.size), "for_head", own, got, small)


def ff_last_kernel(pick, own, z_got, got, small_ref, in_out, back_out, *vectors):
    small_out = vectors[-1]
    shard = own.shape[1]
    in_out[...] = both(own[0], z_got[0]) + got[0, :shard].astype(F32)
    back_out[...] = both(own[1], z_got[1]) + got[1, :shard].astype(F32)
    small = rounded(small_ref[...]) + tail_sum(got, shard)
    small_out[...] = small
    dim = small.shape[1] // 2
    for i in range(6):
        vectors[i][...] = small[i // 2 : i // 2 + 1, (i % 2) * dim : (i % 2 + 1) * dim].reshape(dim)
    vectors[6][...] = small_out[pl.ds(3 + pick[0], 1), :].reshape(2 * dim)


def ff_last(pick, own, z_got, got, small):
    _, rows, cols = own.shape
    dim = cols // 2
    full = lambda s: pl.BlockSpec(s.shape, lambda i, pick: (0,) * len(s.shape))
    out_shape = [hbm((rows, cols), F32)] * 2 + [hbm((dim,), F32)] * 6 + [hbm((cols,), F32)]
    return pl.pallas_call(
        ff_last_kernel,
        grid_spec=pltpu.PrefetchScalarGridSpec(
            num_scalar_prefetch=1,
            grid=(1,),
            in_specs=[full(own), full(z_got), full(got), full(small)],
            out_specs=[full(s) for s in out_shape],
            scratch_shapes=[pltpu.VMEM(small.shape, F32)],
        ),
        out_shape=out_shape,
        compiler_params=params(1),
        cost_estimate=cost(10 * got.size, 20 * got.size),
        name="ff_last",
    )(pick, own, z_got, got, small)


def attn_last_kernel(own, got, small_ref, q_out, k_out, v_out, box_out, wo_out, bq_out, bv_out):
    shard = own.shape[1]
    wide = 2 * HEAD
    pairs = q_out.shape[1] // wide
    small = rounded(small_ref[...]) + tail_sum(got, shard)
    for p in range(pairs):
        at = slice(p * wide, (p + 1) * wide)
        for i, ref in enumerate((q_out, k_out, v_out, wo_out, box_out)):
            span = slice((5 * p + i) * wide, (5 * p + i + 1) * wide)
            ref[:, at] = both(own[0, :, span], got[0, :shard, span])
    for i, ref in enumerate((bq_out, bv_out)):
        row = [small[0:1, (5 * p + i) * wide : (5 * p + i + 1) * wide] for p in range(pairs)]
        ref[...] = jnp.concatenate(row, axis=1).reshape(pairs * wide)


def attn_last(own, got, small):
    _, rows, cols = own.shape
    cols = cols // 5
    out = [hbm((rows, cols), F32)] * 5 + [hbm((cols,), F32)] * 2
    return whole_call(attn_last_kernel, out, cost(4 * own.size, 12 * own.size), "attn_last", own, got, small)


def place_grad_kernel(pick, df_ref, a_ref, b_ref, *refs):
    refs[-1][...] = df_ref[...].astype(F32) + (a_ref[...].astype(F32) + b_ref[...].astype(F32))


def place_grad(which, pick, df, mine, got, pages, into=None):
    length, dim = df.shape
    steps = 2
    part = pl.BlockSpec((length // steps, dim), lambda i, pick: (i, 0))
    args = [df, mine, got] + ([] if into is None else [into])
    return pl.pallas_call(
        place_grad_kernel,
        grid_spec=pltpu.PrefetchScalarGridSpec(
            num_scalar_prefetch=1,
            grid=(steps,),
            in_specs=[part] * 3 + ([] if into is None else [pl.BlockSpec(memory_space=pl.ANY)]),
            out_specs=pl.BlockSpec((length // steps, dim), lambda i, pick: (pick[which] * steps + i, 0)),
        ),
        out_shape=hbm((pages * length, dim), F32),
        input_output_aliases={} if into is None else {4: 0},
        compiler_params=params(1),
        cost_estimate=cost(4e10, 10 * df.size),
        name="place_grad",
    )(pick, *args)


def place_output_kernel(pick, a_ref, b_ref, out_ref):
    length = a_ref.shape[0]
    own = pl.multiple_of(pick[0] * length, length)
    other = pl.multiple_of(pick[1] * length, length)
    out_ref[pl.ds(own, length), :] = a_ref[...]
    out_ref[pl.ds(other, length), :] = b_ref[...]


def place_output(pick, mine, got):
    length, dim = mine.shape
    whole = pl.BlockSpec((length, dim), lambda i, pick: (0, 0))
    return pl.pallas_call(
        place_output_kernel,
        grid_spec=pltpu.PrefetchScalarGridSpec(
            num_scalar_prefetch=1,
            grid=(1,),
            in_specs=[whole, pl.BlockSpec((length, dim), lambda i, pick: (1, 0))],
            out_specs=pl.BlockSpec((2 * length, dim), lambda i, pick: (0, 0)),
        ),
        out_shape=hbm((2 * length, dim), BF16),
        compiler_params=params(1),
        cost_estimate=cost(mine.size, 8 * mine.size),
        name="place_output",
    )(pick, mine, got)


def swap_perm(size, flip):
    return [(i, i ^ flip) for i in range(size)]


def encoding_rows(w_box):
    rows, cols = w_box.shape
    quarters = w_box.reshape(4, rows // 4, cols)
    return jnp.concatenate([quarters[i] for i in (0, 2, 1, 3)], axis=0)


def encoding_groups(groups, dim):
    quarter = dim // 4
    place = (0, 2, 1, 3)
    out = []
    for start, count in groups:
        while count:
            size = min(count, quarter - start % quarter)
            out.append((place[start // quarter] * quarter + start % quarter, size))
            start, count = start + size, count - size
    return out


def shards(
    shards_dp,
    tokens,
    boxes,
    resolution,
    w_query,
    bias_query,
    w_key,
    w_value,
    bias_value,
    w_box,
    w_out,
    bias_out,
    norm1_gain,
    norm1_bias,
    w_in,
    bias_in,
    w_back,
    bias_back,
    norm2_gain,
    norm2_bias,
    grad_out,
):
    dim = tokens.shape[1]
    pages = resolution.shape[0]
    length = tokens.shape[0] // pages
    hidden = w_in.shape[1]
    piece = hidden // 4
    here = lax.axis_index("head").astype(jnp.int32)
    spot = lax.axis_index("dp").astype(jnp.int32)
    core, x_index, z_index, corner = spot % 2, (spot // 2) % 2, spot // 4, spot % 4
    corner_z = (z_index % 2) * 2 + core
    pick = jnp.stack([here, 1 - here, core, 1 - core, x_index, z_index, corner, corner // 2, corner_z])
    groups = shard_groups(dim, shards_dp)
    fast = fast_path(dim, shards_dp)

    def over_head(value):
        return lax.ppermute(value, "head", [(0, 1), (1, 0)])

    def over_dp(value, flip):
        return lax.ppermute(value, "dp", swap_perm(shards_dp, flip))

    def after(value, *others):
        return lax.optimization_barrier((value, others))[0]

    in_first = over_head(lax.dynamic_slice_in_dim(w_in, corner * piece, piece, 1))
    back_first = over_head(lax.dynamic_slice_in_dim(w_back, corner_z * piece, piece, 0))
    bias_there = over_head(bias_in)

    quarter = w_box.shape[0] // 4
    freqs = np.exp(np.arange(quarter, dtype=np.float32) * np.float32(-math.log(10000.0) / quarter))
    freqs = jnp.asarray(np.concatenate([freqs, freqs])[None, :])
    box_t = encoding_rows(w_box).T

    def attend(which, tok):
        return attn_fwd(
            which, pick, resolution, tok, boxes, freqs, w_query, w_key, w_value, bias_query, bias_value,
            box_t, w_out, length, groups,
        )

    part_other, *saved_other = attend(1, tokens)
    got = over_head(part_other)
    in_first, back_first, bias_there = after((in_first, back_first, bias_there), part_other)
    in_second, back_second = over_dp(in_first, 2), over_dp(back_first, 4)
    in_near, back_near = over_dp(in_first, 1), over_dp(back_first, 1)
    part_own, *saved_own = attend(0, after(tokens, bias_there))
    in_near, back_near = after((in_near, back_near), part_own)
    in_second, back_second = after((in_second, back_second), in_near, back_near)
    in_pieces = [in_first, in_near, in_second, over_dp(in_second, 1)]
    back_pieces = [back_first, back_near, back_second, over_dp(back_second, 1)]

    out_own, df_own, lhs, rhs, small = feed_forward(
        pick, tokens, part_own, got, grad_out,
        (bias_out, norm1_gain, norm1_bias, bias_back, norm2_gain, norm2_bias),
        bias_in, bias_there, w_in, w_back, in_pieces, back_pieces, groups,
    )
    df_other = over_head(df_own)
    box_groups = encoding_groups(groups, w_box.shape[0])

    def attend_back(df, saved, prev=None, extra=None, pick=pick):
        return attn_bwd(
            pick, df, saved, w_out, box_t, w_query, w_key, w_value, groups, box_groups, prev, extra
        )

    if fast:
        sent_a = ff_grad(pick, lhs, rhs, small, True)
        got_a = over_dp(sent_a, 1)
        sent_b = ff_grad(pick, lhs, after(rhs, sent_a), small, False)
        got_b = over_dp(sent_b, 1)
        xs_a, xk_a, small_1 = ff_grad(pick, lhs, after(rhs, sent_b), small, True, got_a)
        xg_a = over_dp(xs_a, 2)
        got_b = after(got_b, xs_a)
        xs_b, xk_b, small_b = ff_grad(pick, lhs, after(rhs, xs_a), small, False, got_b)
        df_own = after(df_own, xs_b)
    *part_a, inp_own = attend_back(df_own, saved_own)
    if fast:
        xg_a, df_other, xs_b = after((xg_a, df_other, xs_b), inp_own)
        own_a, sent_a, small_2 = add_x(pick, xk_a, after(xg_a, df_other), small_1, True)
        zg_a = over_dp(sent_a, 4)
        inp_send, df_other = after((inp_own, df_other), sent_a)
        xg_b = over_dp(xs_b, 2)
    else:
        inp_send = inp_own
    inp_own_got = over_head(inp_send)

    pick_back = pick if fast else pick.at[2:4].set(jnp.arange(2, dtype=jnp.int32))
    sent, kept, a_small, inp_other = attend_back(df_other, saved_other, part_a, out_own, pick_back)
    inp_other_got = over_head(inp_other)

    if fast:
        xg_b, zg_a, inp_own_got = after((xg_b, zg_a, inp_own_got), inp_other)
        sent, xk_b, zg_a = after((sent, xk_b, zg_a), xg_b, zg_a, inp_own_got)
        sent_got = over_dp(sent, 1)
        own_a, sent_a, small_3 = add_z(own_a, zg_a, small_2, True)
        own_b, sent_b = add_x(pick, after(xk_b, sent_a), xg_b, small_b, False)
        xs, xk, a_small = attn_split(pick, kept, after(sent_got, sent_b), a_small)
        xg = over_dp(xs, 2)
        zg_a, zg_b = over_dp(sent_a, 8), over_dp(sent_b, 4)
        grad_input = place_grad(1, pick, after(df_other, xs), inp_other, inp_own_got, pages)
        own, sent, a_small = add_x(pick, after(xk, grad_input), xg, a_small, True)
        zg = over_dp(sent, 4)
        zg_a, zg_b = after((zg_a, zg_b), sent)
        own_b, sent_b = add_z(own_b, zg_b, small_b, False)
        zg_b = over_dp(sent_b, 8)
        a_sum, small_3 = for_head(own_a, after(zg_a, sent_b), small_3)
        df_own, inp_other_got = after((df_own, inp_other_got), a_sum)
        a_sum = over_head(a_sum)
        grad_input = place_grad(0, pick, df_own, inp_own, inp_other_got, pages, grad_input)
        own, sent, a_small = add_z(after(own, grad_input), zg, a_small, True)
        zg = over_dp(sent, 8)
        grad_in, grad_back, n2g, n2b, bias_back_sum, n1g, n1b, bias_out_sum, bias_in_sum = ff_last(
            pick, after(own_b, sent), zg_b, a_sum, small_3
        )
        output = place_output(pick, after(out_own, grad_in), inp_other_got)
        own = after(own, output)
        grad_q, grad_k, grad_v, grad_box, grad_wo, bq_sum, bv_sum = attn_last(own, zg, a_small)
        grad_back, grad_wo = grad_back.T, grad_wo.T
    else:
        scatter = lambda value, axis: lax.psum_scatter(
            value.astype(F32), "dp", scatter_dimension=axis, tiled=True
        )
        cores = [pick.at[3].set(c) for c in (0, 1)]
        halves = [
            scatter(
                jnp.concatenate([ff_grad(p, lhs, rhs, small, remote)[:, : dim // 2] for p in cores], axis=1), 1
            )
            for remote in (True, False)
        ]
        total = halves[1] + over_head(halves[0])
        grad_in, grad_back = total[0], total[1].T
        total = scatter(jnp.concatenate([kept, sent[: dim // 2]], axis=0), 0)
        total = total.reshape(total.shape[0], -1, 5, 2 * HEAD).transpose(2, 0, 1, 3)
        grad_q, grad_k, grad_v, grad_wo, grad_box = total.reshape(5, total.shape[1], -1)
        grad_wo = grad_wo.T
        small = lax.psum(small, ("dp", "head"))
        n2g, n2b, bias_back_sum, n1g, n1b, bias_out_sum = small[:3].reshape(6, dim)
        bias_in_sum = lax.dynamic_index_in_dim(small, 3 + here, 0, keepdims=False)
        bq_sum, bv_sum = lax.psum(a_small, "dp").reshape(-1, 5, 2 * HEAD)[:, :2].transpose(1, 0, 2).reshape(2, -1)
        output = place_output(pick, out_own, inp_other_got)
        grad_input = place_grad(1, pick, df_other, inp_other, inp_own_got, pages)
        grad_input = place_grad(0, pick, df_own, inp_own, inp_other_got, pages, grad_input)
    return (
        output,
        grad_input,
        grad_q,
        bq_sum,
        grad_k,
        grad_v,
        bv_sum,
        grad_box,
        grad_wo,
        bias_out_sum,
        n1g,
        n1b,
        grad_in,
        bias_in_sum,
        grad_back,
        bias_back_sum,
        n2g,
        n2b,
    )


def solution(mesh):
    placed = (
        P("dp", None),
        P(None, "dp"),
        P("dp"),
        P(None, "head"),
        P("head"),
        P(None, "head"),
        P(None, "head"),
        P("head"),
        P(None, "head"),
        P("head", None),
        P(),
        P(),
        P(),
        P(None, "head"),
        P("head"),
        P("head", None),
        P(),
        P(),
        P(),
        P("dp", None),
    )
    return jax.shard_map(
        partial(shards, mesh.shape["dp"]),
        mesh=mesh,
        in_specs=placed,
        out_specs=(
            P("dp", None),
            P("dp", None),
            P("dp", "head"),
            P("head"),
            P("dp", "head"),
            P("dp", "head"),
            P("head"),
            P("dp", "head"),
            P("head", "dp"),
            P(),
            P(),
            P(),
            P("dp", "head"),
            P("head"),
            P("head", "dp"),
            P(),
            P(),
            P(),
        ),
        check_vma=False,
    )
```

```python
from functools import partial
import math

import jax
import numpy as np
import jax.numpy as jnp
from jax import lax
from jax.experimental import pallas as pl
from jax.experimental.pallas import tpu as pltpu
from jax.sharding import PartitionSpec as P

HEAD = 64
F32 = jnp.float32
BF16 = jnp.bfloat16
VMEM_LIMIT = 63 * 1024 * 1024


def hbm(shape, dtype):
    return pltpu.HBM(tuple(shape), dtype)


def mm(a, b):
    return jnp.dot(a, b, preferred_element_type=F32)


def mm_nt(a, b):
    return lax.dot_general(a, b, (((1,), (1,)), ((), ())), preferred_element_type=F32)


def params(steps):
    return pltpu.CompilerParams(
        dimension_semantics=("arbitrary",) * steps, vmem_limit_bytes=VMEM_LIMIT
    )


def cost(flops, nbytes, trans=0):
    return pl.CostEstimate(flops=int(flops), bytes_accessed=int(nbytes), transcendentals=int(trans))


def sin_cos(angle):
    turns = jnp.floor(angle * (2.0 / math.pi) + 0.5)
    r = angle - turns * 1.5703125
    r = r - turns * 4.837512969970703125e-4
    r = r - turns * 7.54978995489188216e-8
    r2 = r * r
    s = r + r * r2 * (
        -1.6666654611e-1 + r2 * (8.3321608736e-3 + r2 * -1.9515295891e-4)
    )
    c = 1.0 - 0.5 * r2 + r2 * r2 * (
        4.166664568298827e-2 + r2 * (-1.388731625493765e-3 + r2 * 2.443315711809948e-5)
    )
    quad = turns.astype(jnp.int32)
    odd = (quad & 1) == 1
    sine = jnp.where(odd, c, s)
    cosine = jnp.where(odd, s, c)
    sine = jnp.where((quad & 2) == 2, -sine, sine)
    cosine = jnp.where(((quad + 1) & 2) == 2, -cosine, cosine)
    return sine, cosine


def lane_mask(shape, which):
    lanes = lax.broadcasted_iota(jnp.int32, shape, 1)
    return (lanes < HEAD) if which == 0 else (lanes >= HEAD)


def row_mask(shape, which):
    rows = lax.broadcasted_iota(jnp.int32, shape, 0)
    return (rows < HEAD) if which == 0 else (rows >= HEAD)


def keep(mask, x):
    return jnp.where(mask, x, jnp.zeros_like(x))


def attn_fwd_kernel(
    groups, which_page, pick, res, tok_ref, box_ref, freq_ref, wq_ref, wk_ref, wv_ref, bq_ref, bv_ref, wbt_ref, wo_ref,
    part_ref, p_ref, q_ref, k_ref, v_ref, ctx_ref, s_ref, c_ref, tok_t_ref, codes, mixed, acc, biases, s_keep, c_keep, t_keep, sems,
):
    step = pl.program_id(0)
    half = s_keep.shape[1]

    def leaving():
        pairs = ((s_keep, s_ref), (c_keep, c_ref), (t_keep, tok_t_ref))
        return [pltpu.make_async_copy(a, b, sems.at[n]) for n, (a, b) in enumerate(pairs)]

    @pl.when(step == 0)
    def _():
        rows = s_keep.shape[0]
        lanes = lax.broadcasted_iota(jnp.int32, (rows, half), 1)
        level = res[pick[which_page]]
        width = (612 + 204 * level).astype(F32)
        height = (792 + 264 * level).astype(F32)
        corners = box_ref[...]
        centre_x = (corners[0:1] + corners[2:3]).astype(F32) * 500.0 / width
        centre_y = (corners[1:2] + corners[3:4]).astype(F32) * 500.0 / height
        both = jnp.concatenate([centre_x, centre_y, jnp.zeros((6, rows), F32)], axis=0).T
        centre = jnp.where(lanes < half // 2, both[:, 0:1], both[:, 1:2])
        sine, cosine = sin_cos(centre * freq_ref[...])
        s_keep[...] = sine
        c_keep[...] = cosine
        codes[:, :half] = cosine.astype(BF16)
        codes[:, half : 2 * half] = sine.astype(BF16)
        acc[...] = jnp.zeros_like(acc)
        biases[0:1] = bq_ref[...].astype(F32).reshape(1, -1)
        biases[1:2] = bv_ref[...].astype(F32).reshape(1, -1)
        tok_t = split_rows(tok_ref[...].T, groups)
        t_keep[0] = tok_t[:half]
        t_keep[1] = tok_t[half:]
        for copy in leaving():
            copy.start()

    tok = tok_ref[...]
    rows = tok.shape[0]
    wide = wq_ref.shape[1]
    span = pl.ds(pl.multiple_of(step * wide, wide), wide)
    qkv = mm(tok, jnp.concatenate([wq_ref[...], wk_ref[...], wv_ref[...]], axis=1))
    q2 = (qkv[:, :wide] + biases[0:1, span]).astype(BF16) * BF16(0.125)
    k2 = qkv[:, wide : 2 * wide].astype(BF16)
    v2 = (qkv[:, 2 * wide :] + biases[1:2, span]).astype(BF16)
    q_ref[...] = q2
    k_ref[...] = k2
    v_ref[...] = v2
    codes[:, 2 * half :] = k2
    sine, cosine = s_keep[...], c_keep[...]
    for which in range(2):
        span = slice(which * rows, (which + 1) * rows)
        qm = keep(lane_mask(q2.shape, which), q2)
        off = mm(qm, wbt_ref[...])
        a, b = off[:, :half], off[:, half:]
        mixed[span, :half] = (a * sine + b * cosine).astype(BF16)
        mixed[span, half : 2 * half] = (b * sine - a * cosine).astype(BF16)
        mixed[span, 2 * half :] = qm
    parts = []
    for which in range(2):
        span = slice(which * rows, (which + 1) * rows)
        scores = mm_nt(mixed[span], codes[...])
        top = jnp.max(scores, axis=1, keepdims=True)
        raised = jnp.exp(scores - top)
        total = jnp.sum(raised, axis=1, keepdims=True)
        prob = (raised * (1.0 / total)).astype(BF16)
        p_ref[which] = prob
        parts.append(mm(prob, v2))
    ctx2 = jnp.where(lane_mask(parts[0].shape, 0), parts[0], parts[1]).astype(BF16)
    ctx_ref[...] = ctx2
    acc[...] += mm(ctx2, wo_ref[...])

    @pl.when(step == pl.num_programs(0) - 1)
    def _():
        part_ref[...] = acc[...].astype(BF16)
        for copy in leaving():
            copy.wait()


def attn_fwd(which_page, pick, res, tokens, boxes, freq, wq, wk, wv, bq, bv, wbt, wo, length, groups):
    dim = tokens.shape[1]
    inner = wq.shape[1]
    heads = inner // HEAD
    pairs = heads // 2
    wide = 2 * HEAD
    page = lambda i, pick, res: (pick[which_page], 0)
    fixed = lambda i, pick, res: (0, 0)
    cols = lambda i, pick, res: (0, i)
    rows = lambda i, pick, res: (i, 0)
    flops = 2 * length * (dim * inner * 4 + heads * (HEAD * dim + length * (dim + 2 * HEAD)))
    return pl.pallas_call(
        partial(attn_fwd_kernel, groups, which_page),
        grid_spec=pltpu.PrefetchScalarGridSpec(
            num_scalar_prefetch=2,
            grid=(pairs,),
            in_specs=[
                pl.BlockSpec((length, dim), page),
                pl.BlockSpec((4, length), lambda i, pick, res: (0, pick[which_page])),
                pl.BlockSpec((1, dim // 2), fixed),
                pl.BlockSpec((dim, wide), cols),
                pl.BlockSpec((dim, wide), cols),
                pl.BlockSpec((dim, wide), cols),
                pl.BlockSpec((inner,), lambda i, pick, res: (0,)),
                pl.BlockSpec((inner,), lambda i, pick, res: (0,)),
                pl.BlockSpec((wide, dim), rows),
                pl.BlockSpec((wide, dim), rows),
            ],
            out_specs=[
                pl.BlockSpec((length, dim), fixed),
                pl.BlockSpec((2, length, length), lambda i, pick, res: (i, 0, 0)),
                pl.BlockSpec((length, wide), cols),
                pl.BlockSpec((length, wide), cols),
                pl.BlockSpec((length, wide), cols),
                pl.BlockSpec((length, wide), cols),
                pl.BlockSpec(memory_space=pl.ANY),
                pl.BlockSpec(memory_space=pl.ANY),
                pl.BlockSpec(memory_space=pl.ANY),
            ],
            scratch_shapes=[
                pltpu.VMEM((length, dim + wide), BF16),
                pltpu.VMEM((2 * length, dim + wide), BF16),
                pltpu.VMEM((length, dim), F32),
                pltpu.VMEM((8, inner), F32),
                pltpu.VMEM((length, dim // 2), F32),
                pltpu.VMEM((length, dim // 2), F32),
                pltpu.VMEM((2, dim // 2, length), BF16),
                pltpu.SemaphoreType.DMA((3,)),
            ],
        ),
        out_shape=[
            hbm((length, dim), BF16),
            hbm((heads, length, length), BF16),
            hbm((length, inner), BF16),
            hbm((length, inner), BF16),
            hbm((length, inner), BF16),
            hbm((length, inner), BF16),
            hbm((length, dim // 2), F32),
            hbm((length, dim // 2), F32),
            hbm((2, dim // 2, length), BF16),
        ],
        compiler_params=params(1),
        cost_estimate=cost(flops, 10e6, heads * length * length),
        name="attn_fwd",
    )(pick, res, tokens, boxes, freq, wq, wk, wv, bq, bv, wbt, wo)


def attn_bwd_kernel(groups, box_groups, first, pick, *refs):
    (df_ref, tok_t_ref, ctx_ref, wo_ref, q_ref, k_ref, v_ref, p_ref, s_ref, c_ref, wbt_ref,
     wq_ref, wk_ref, wv_ref, *refs) = refs
    if first:
        part_ref, small_ref, inp_ref, codes, acc, df_t = refs
    else:
        prev_ref, prev_small_ref, extra_ref, *refs = refs
        sent_ref, kept_ref, small_ref, inp_ref, codes, acc, df_t, grads = refs
    step = pl.program_id(0)
    half = s_ref.shape[1]

    @pl.when(step == 0)
    def _():
        codes[:, :half] = c_ref[...].astype(BF16)
        codes[:, half:] = s_ref[...].astype(BF16)
        acc[...] = jnp.zeros_like(acc)
        turned = split_rows(df_ref[...].T, groups)
        df_t[0] = turned[:half]
        df_t[1] = turned[half:]

    sine, cosine = s_ref[...], c_ref[...]
    q2, k2, v2 = q_ref[...], k_ref[...], v_ref[...]
    dctx = mm_nt(df_ref[...], wo_ref[...]).astype(BF16)
    dctx_t = dctx.T
    q_t = q2.T
    wbt = wbt_ref[...]
    dq = jnp.zeros(q2.shape, F32)
    dk_t, dv_t, dwb = [], [], []
    for which in range(2):
        low, high = which * HEAD, (which + 1) * HEAD
        dm = keep(lane_mask(dctx.shape, which), dctx)
        prob = p_ref[which]
        grad_probs = mm_nt(dm, v2)
        dv_t.append(mm(dctx_t[low:high], prob))
        wide_prob = prob.astype(F32)
        both = wide_prob * grad_probs
        inner = jnp.sum(both, axis=1, keepdims=True)
        ds = (both - wide_prob * inner).astype(BF16)
        dk_t.append(mm(q_t[low:high], ds))
        km = keep(lane_mask(k2.shape, which), k2)
        ga = mm(ds, codes[:, :half]).astype(BF16).astype(F32)
        gb = mm(ds, codes[:, half:]).astype(BF16).astype(F32)
        oa = (ga * sine - gb * cosine).astype(BF16)
        ob = (gb * sine + ga * cosine).astype(BF16)
        wm = keep(row_mask(wbt.shape, which), wbt)
        dq = dq + (mm(ds, km) + mm_nt(oa, wm[:, :half]) + mm_nt(ob, wm[:, half:]))
        dwb.append(jnp.concatenate([mm(q_t[low:high], oa), mm(q_t[low:high], ob)], axis=1))
    dq2 = (dq * 0.125).astype(BF16)
    dk2 = jnp.concatenate(dk_t, axis=0).T.astype(BF16)
    dv2 = jnp.concatenate(dv_t, axis=0).T.astype(BF16)
    sides = jnp.concatenate([dq2, dk2, dv2], axis=1)
    acc[...] += mm_nt(sides, jnp.concatenate([wq_ref[...], wk_ref[...], wv_ref[...]], axis=1))

    box = split_rows(jnp.concatenate(dwb, axis=0).T, box_groups)
    ctx2 = ctx_ref[...]
    zeros = jnp.zeros((1, 3 * q2.shape[1]), F32)
    small = jnp.concatenate(
        [column_sum(dq2.astype(F32)), column_sum(dv2.astype(F32)), zeros], axis=1
    )
    if not first:
        small = small + prev_small_ref[...]
    small_ref[...] = small
    for h in range(2):
        grad = jnp.concatenate(
            [mm(tok_t_ref[h], sides), mm(df_t[h], ctx2), box[h * half : (h + 1) * half]], axis=1
        )
        if first:
            part_ref[h] = grad.astype(BF16)
        else:
            grads[h] = (grad + prev_ref[h].astype(F32)).astype(BF16)
    if not first:
        sent_ref[:half] = grads[pick[3]]
        sent_ref[half:] = wide_tail(small)
        kept_ref[...] = grads[pick[2]]

    @pl.when(step == pl.num_programs(0) - 1)
    def _():
        rows = acc.shape[0]
        inp_ref[:rows] = acc[...].astype(BF16)
        if not first:
            inp_ref[rows:] = extra_ref[...]


def attn_bwd(pick, df, saved, wo, wbt, wq, wk, wv, groups, box_groups, prev=None, extra=None):
    prob, q, k, v, ctx, sine, cosine, tok_t = saved
    length, dim = df.shape
    inner = wq.shape[1]
    heads = inner // HEAD
    pairs = heads // 2
    wide = 2 * HEAD
    first = prev is None
    sent = length if first else 2 * length
    fixed = lambda i, pick: (0, 0)
    cols = lambda i, pick: (0, i)
    rows = lambda i, pick: (i, 0)
    block = lambda i, pick: (0, 0, i)
    flops = 2 * length * (dim * inner * 8 + heads * (3 * HEAD * dim + length * (dim + 4 * HEAD)))
    part = pl.BlockSpec((2, dim // 2, 5 * wide), block)
    small = pl.BlockSpec((1, 5 * wide), cols)
    small_shape = hbm((1, 5 * inner), F32)
    inp = pl.BlockSpec((sent, dim), fixed)
    inp_shape = hbm((sent, dim), BF16)
    scratch = [
        pltpu.VMEM((length, dim), BF16),
        pltpu.VMEM((length, dim), F32),
        pltpu.VMEM((2, dim // 2, length), BF16),
    ]
    if first:
        out_specs = [part, small, inp]
        out_shape = [hbm((2, dim // 2, 5 * inner), BF16), small_shape, inp_shape]
        more_specs, more = [], []
    else:
        out_specs = [
            pl.BlockSpec((dim // 2 + TAIL, 5 * wide), cols), pl.BlockSpec((dim // 2, 5 * wide), cols), small, inp,
        ]
        out_shape = [
            hbm((dim // 2 + TAIL, 5 * inner), BF16), hbm((dim // 2, 5 * inner), BF16), small_shape, inp_shape,
        ]
        more_specs, more = [part, small, pl.BlockSpec((length, dim), fixed)], [*prev, extra]
        scratch.append(pltpu.VMEM((2, dim // 2, 5 * wide), BF16))
    return pl.pallas_call(
        partial(attn_bwd_kernel, groups, box_groups, first),
        grid_spec=pltpu.PrefetchScalarGridSpec(
            num_scalar_prefetch=1,
            grid=(pairs,),
            in_specs=[
                pl.BlockSpec((length, dim), fixed),
                pl.BlockSpec((2, dim // 2, length), lambda i, pick: (0, 0, 0)),
                pl.BlockSpec((length, wide), cols),
                pl.BlockSpec((wide, dim), rows),
                pl.BlockSpec((length, wide), cols),
                pl.BlockSpec((length, wide), cols),
                pl.BlockSpec((length, wide), cols),
                pl.BlockSpec((2, length, length), lambda i, pick: (i, 0, 0)),
                pl.BlockSpec((length, dim // 2), fixed),
                pl.BlockSpec((length, dim // 2), fixed),
                pl.BlockSpec((wide, dim), rows),
                pl.BlockSpec((dim, wide), cols),
                pl.BlockSpec((dim, wide), cols),
                pl.BlockSpec((dim, wide), cols),
            ]
            + more_specs,
            out_specs=out_specs,
            scratch_shapes=scratch,
        ),
        out_shape=out_shape,
        compiler_params=params(1),
        cost_estimate=cost(flops, 14e6),
        name="attn_bwd",
    )(pick, df, tok_t, ctx, wo, q, k, v, prob, sine, cosine, wbt, wq, wk, wv, *more)


def split_rows(x_t, groups):
    return jnp.concatenate([x_t[start : start + count] for start, count in groups], axis=0)


def shard_groups(dim, shards):
    rows = dim // shards
    if not fast_path(dim, shards):
        return [(0, dim)]
    order = [z * 4 + x * 2 + c for c in range(2) for z in range(shards // 4) for x in range(2)]
    return [(block * rows, rows) for block in order]


def fast_path(dim, shards):
    return shards == 16 and (dim // shards) % 16 == 0


def gelu_parts(v):
    e = jnp.exp(v * v * -0.5)
    t = 1.0 / (1.0 + (0.3275911 * math.sqrt(0.5)) * jnp.abs(v))
    poly = t * (
        0.5 * 0.254829592
        + t * (0.5 * -0.284496736 + t * (0.5 * 1.421413741 + t * (0.5 * -1.453152027 + t * (0.5 * 1.061405429))))
    )
    tail = poly * e
    phi = jnp.where(v >= 0, 1.0 - tail, tail)
    return phi, phi + v * (e * (1.0 / math.sqrt(2.0 * math.pi)))


def norm_stats(hidden):
    centred = hidden - jnp.mean(hidden, axis=1, keepdims=True)
    variance = jnp.mean(centred * centred, axis=1, keepdims=True)
    inv = lax.rsqrt(variance + 1e-05)
    return centred * inv, inv


def norm_back(grad, scaled, inv):
    return inv * (
        grad
        - jnp.mean(grad, axis=1, keepdims=True)
        - scaled * jnp.mean(grad * scaled, axis=1, keepdims=True)
    )


def column_sum(x):
    return jnp.sum(x, axis=0, keepdims=True)


def ff_kernel(
    groups, pick, tok_ref, part_ref, got_ref, gout_ref, bo_ref, g1_ref, b1_ref, bb_ref, g2_ref, b2_ref,
    bi_here, bi_there,
    wi_here, wb_here, wi0, wi1, wi2, wi3, wb0, wb1, wb2, wb3,
    out_ref, df_ref, lhs_ref, rhs_ref, small_ref,
    wi, wb, slope, norm_low, grad_low, acc, wide, bi_ref, rhs, gout_keep, out_keep, lhs, more_sems, sems,
):
    blocks, dim, cols = wi.shape
    here = blocks // 2
    piece = cols // 2
    remote = [(wi0, wb0), (wi1, wb1), (wi2, wb2), (wi3, wb3)]
    for p in range(2 * blocks):
        if p < blocks:
            at = (p % 2) * piece
            span = pl.ds(at, piece)
            source = (wi_here.at[:, pl.ds(p * piece, piece)], wb_here.at[pl.ds(p * piece, piece), :])
        else:
            span = pl.ds(pl.multiple_of(((pick[6] ^ p) & 1) * piece, piece), piece)
            source = remote[p - blocks]
            slot = here + ((((pick[8] ^ p) & 3) >> 1) ^ pick[7])
            span_back = pl.ds(pl.multiple_of(((pick[8] ^ p) & 1) * piece, piece), piece)
        pltpu.make_async_copy(source[0], wi.at[p // 2, :, span], sems.at[0, p]).start()
        if p < blocks:
            pltpu.make_async_copy(source[1], wb.at[p // 2, span, :], sems.at[1, p // 2]).start()
        else:
            pltpu.make_async_copy(source[1], wb.at[slot, span_back, :], sems.at[1, slot]).start()

    fetch = pltpu.make_async_copy(
        gout_ref.at[pl.ds(pl.multiple_of(pick[0] * gout_keep.shape[0], 8), gout_keep.shape[0]), :], gout_keep, more_sems.at[0]
    )
    fetch.start()
    out_copy = pltpu.make_async_copy(out_keep, out_ref, more_sems.at[1])
    lhs_copies = [pltpu.make_async_copy(lhs.at[m], lhs_ref.at[:, m], more_sems.at[2 + m]) for m in range(2)]

    def vec(ref):
        return ref[...].astype(F32).reshape(1, -1)

    here_at, there_at = pick[0] * here, pick[1] * here
    bias_here, bias_there = vec(bi_here), vec(bi_there)
    for j in range(here):
        bi_ref[pl.ds(here_at + j, 1), :] = bias_here[:, j * cols : (j + 1) * cols]
        bi_ref[pl.ds(there_at + j, 1), :] = bias_there[:, j * cols : (j + 1) * cols]

    def place(j):
        return jnp.where(j < here, here_at + j, there_at + (pick[7] ^ (j - here)))

    bo, g1, b1, bb, g2, b2 = (vec(r) for r in (bo_ref, g1_ref, b1_ref, bb_ref, g2_ref, b2_ref))
    first_sum = (
        tok_ref[...].astype(F32)
        + (part_ref[...].astype(F32) + got_ref[...].astype(F32))
        + bo
    )
    scaled1, inv1 = norm_stats(first_sum)
    normed = scaled1 * g1 + b1
    low = normed.astype(BF16)
    norm_low[...] = low
    wide[...] = normed + bb
    acc[...] = jnp.zeros_like(acc)
    low_t = split_rows(low.T, groups)
    split = low_t.shape[0] // 2
    lhs[0, 0] = low_t[:split]
    lhs[0, 1] = low_t[split:]
    lhs_copies[0].start()

    def leaving(m, j):
        return pltpu.make_async_copy(rhs.at[m, j], rhs_ref.at[m, j], sems.at[2 + m, j])

    def forward(j, _):
        for p in range(2):
            pltpu.make_async_copy(wi0, wi.at[j, :, pl.ds(0, piece)], sems.at[0, 2 * j + p]).wait()
        pltpu.make_async_copy(wb.at[j], wb.at[j], sems.at[1, j]).wait()
        pre = mm(norm_low[...], wi[j]) + bi_ref[pl.ds(place(j), 1), :]
        phi, step = gelu_parts(pre)
        act = (pre * phi).astype(BF16)
        rhs[1, j] = act
        leaving(1, j).start()
        slope[j] = step
        acc[...] += mm(act, wb[j])
        return 0

    lax.fori_loop(0, blocks, forward, 0)
    scaled2, inv2 = norm_stats(wide[...] + acc[...])
    out_keep[...] = (scaled2 * g2 + b2).astype(BF16)
    out_copy.start()
    fetch.wait()
    gout = gout_keep[...].astype(F32)
    small_gain2 = column_sum(gout * scaled2)
    small_bias2 = column_sum(gout)
    grad_second = norm_back(gout * g2, scaled2, inv2)
    small_back = column_sum(grad_second)
    low2 = grad_second.astype(BF16)
    grad_low[...] = low2
    low2_t = split_rows(low2.T, groups)
    lhs[1, 0] = low2_t[:split]
    lhs[1, 1] = low2_t[split:]
    lhs_copies[1].start()
    acc[...] = grad_second

    def backward(j, _):
        grad_act = mm_nt(grad_low[...], wb[j]).astype(BF16).astype(F32)
        grad_pre = (grad_act * slope[j]).astype(BF16)
        rhs[0, j] = grad_pre
        leaving(0, j).start()
        bi_ref[pl.ds(place(j), 1), :] = column_sum(grad_pre.astype(F32))
        acc[...] += mm_nt(grad_pre, wi[j])
        return 0

    lax.fori_loop(0, blocks, backward, 0)
    grad_normed = acc[...]
    first_sum = (
        tok_ref[...].astype(F32)
        + (part_ref[...].astype(F32) + got_ref[...].astype(F32))
        + bo
    )
    scaled1, inv1 = norm_stats(first_sum)
    small_gain1 = column_sum(grad_normed * scaled1)
    small_bias1 = column_sum(grad_normed)
    grad_first = norm_back(grad_normed * g1, scaled1, inv1)
    small_out = column_sum(grad_first)
    df_ref[...] = grad_first.astype(BF16)
    for m in range(2):
        for j in range(blocks):
            leaving(m, j).wait()
    for copy in [out_copy, *lhs_copies]:
        copy.wait()
    small_ref[...] = jnp.concatenate(
        [
            jnp.concatenate([small_gain2, small_bias2], axis=1),
            jnp.concatenate([small_back, small_gain1], axis=1),
            jnp.concatenate([small_bias1, small_out], axis=1),
            jnp.concatenate([bi_ref[j : j + 1] for j in range(here)], axis=1),
            jnp.concatenate([bi_ref[j : j + 1] for j in range(here, blocks)], axis=1),
            jnp.zeros((3, 2 * dim), F32),
        ],
        axis=0,
    )


def feed_forward(pick, tokens, part, got, grad_out, rows, bias_in, bias_there, wi_here, wb_here, wi_pieces, wb_pieces, groups):
    length, dim = part.shape
    cols = 2 * wi_pieces[0].shape[1]
    blocks = 2 * wi_here.shape[1] // cols
    page = lambda i, pick: (pick[0], 0)
    fixed = lambda i, pick: (0, 0)
    row = pl.BlockSpec((dim,), lambda i, pick: (0,))
    bias_row = pl.BlockSpec(bias_in.shape, lambda i, pick: (0,))
    whole = pl.BlockSpec((length, dim), fixed)
    anywhere = pl.BlockSpec(memory_space=pl.ANY)
    hidden = blocks * cols
    return pl.pallas_call(
        partial(ff_kernel, groups),
        grid_spec=pltpu.PrefetchScalarGridSpec(
            num_scalar_prefetch=1,
            grid=(1,),
            in_specs=[
                pl.BlockSpec((length, dim), page),
                whole,
                whole,
                anywhere,
                row, row, row, row, row, row,
                bias_row, bias_row,
            ]
            + [anywhere] * 10,
            out_specs=[
                anywhere,
                whole,
                anywhere,
                anywhere,
                pl.BlockSpec((8, 2 * dim), fixed),
            ],
            scratch_shapes=[
                pltpu.VMEM((blocks, dim, cols), BF16),
                pltpu.VMEM((blocks, cols, dim), BF16),
                pltpu.VMEM((blocks, length, cols), F32),
                pltpu.VMEM((length, dim), BF16),
                pltpu.VMEM((length, dim), BF16),
                pltpu.VMEM((length, dim), F32),
                pltpu.VMEM((length, dim), F32),
                pltpu.VMEM((blocks, cols), F32),
                pltpu.VMEM((2, blocks, length, cols), BF16),
                pltpu.VMEM((length, dim), BF16),
                pltpu.VMEM((length, dim), BF16),
                pltpu.VMEM((2, 2, dim // 2, length), BF16),
                pltpu.SemaphoreType.DMA((4,)),
                pltpu.SemaphoreType.DMA((4, 2 * blocks)),
            ],
        ),
        out_shape=[
            hbm((length, dim), BF16),
            hbm((length, dim), BF16),
            hbm((2, 2, dim // 2, length), BF16),
            hbm((2, blocks, length, cols), BF16),
            hbm((8, 2 * dim), F32),
        ],
        compiler_params=params(1),
        cost_estimate=cost(8 * length * dim * hidden, 4 * dim * hidden + 8 * length * hidden, length * hidden),
        name="feed_forward",
    )(pick, tokens, part, got, grad_out, *rows, bias_in, bias_there, wi_here, wb_here, *wi_pieces, *wb_pieces)


TAIL = 8


def split2(x):
    high = x.astype(BF16)
    return high, (x - high.astype(F32)).astype(BF16)


def rounded(x):
    high, low = split2(x)
    return high.astype(F32) + low.astype(F32)


def tall(x):
    if x.shape[0] == TAIL:
        return x
    return jnp.concatenate([x, jnp.zeros((TAIL - x.shape[0],) + x.shape[1:], x.dtype)], axis=0)


def ff_send_kernel(pick, lhs_ref, rhs_ref, small_ref, out_ref):
    rows = lhs_ref.shape[2]
    for m in range(2):
        out_ref[m, :rows] = mm(lhs_ref[0, m], rhs_ref[m, 0]).astype(BF16)
    for m, term in enumerate(split2(small_ref[...])):
        out_ref[m, rows:] = tall(term)


def ff_keep_kernel(pick, lhs_ref, rhs_ref, got_ref, small_ref, xs_ref, xk_ref, small_out, acc):
    rows = lhs_ref.shape[2]
    shard = acc.shape[0] // 8
    x_index = pick[4]
    for m in range(2):
        acc[...] = mm(lhs_ref[0, m], rhs_ref[m, 0]) + got_ref[m, :rows].astype(F32)
        for z in range(4):
            away = pl.multiple_of((2 * z + 1 - x_index) * shard, 8)
            mine = pl.multiple_of((2 * z + x_index) * shard, 8)
            xs_ref[m, z * shard : (z + 1) * shard] = acc[pl.ds(away, shard), :].astype(BF16)
            xk_ref[m, z * shard : (z + 1) * shard] = acc[pl.ds(mine, shard), :].astype(BF16)
    small = rounded(small_ref[...]) + (got_ref[0, rows : rows + 8].astype(F32) + got_ref[1, rows : rows + 8].astype(F32))
    small_out[...] = small
    for m, term in enumerate(split2(small)):
        xs_ref[m, 4 * shard :] = tall(term)


def ff_grad(pick, lhs, rhs, small, remote, got=None):
    _, mats, rows, length = lhs.shape
    _, blocks, _, cols = rhs.shape
    half = blocks // 2
    base = half if remote else 0
    which = 2 if got is not None else 3
    dest = (lambda j, pick: j ^ pick[7]) if remote else (lambda j, pick: j)
    column = lambda height: pl.BlockSpec((2, height, cols), lambda j, pick: (0, 0, dest(j, pick)))
    small_spec = pl.BlockSpec((8, cols), lambda j, pick: (0, dest(j, pick)))
    in_specs = [
        pl.BlockSpec((1, mats, rows, length), lambda j, pick: (pick[which], 0, 0, 0)),
        pl.BlockSpec((2, 1, length, cols), lambda j, pick: (0, base + j, 0, 0)),
    ]
    wide = half * cols
    estimate = cost(2 * mats * rows * length * wide, 10e6)
    if got is None:
        return pl.pallas_call(
            ff_send_kernel,
            grid_spec=pltpu.PrefetchScalarGridSpec(
                num_scalar_prefetch=1,
                grid=(half,),
                in_specs=in_specs + [small_spec],
                out_specs=column(rows + TAIL),
            ),
            out_shape=hbm((2, rows + TAIL, wide), BF16),
            compiler_params=params(1),
            cost_estimate=estimate,
            name="ff_grad_send",
        )(pick, lhs, rhs, small)
    return pl.pallas_call(
        ff_keep_kernel,
        grid_spec=pltpu.PrefetchScalarGridSpec(
            num_scalar_prefetch=1,
            grid=(half,),
            in_specs=in_specs + [column(rows + TAIL), small_spec],
            out_specs=[column(rows // 2 + TAIL), column(rows // 2), small_spec],
            scratch_shapes=[pltpu.VMEM((rows, cols), F32)],
        ),
        out_shape=[
            hbm((2, rows // 2 + TAIL, wide), BF16),
            hbm((2, rows // 2, wide), BF16),
            hbm((8, wide), F32),
        ],
        compiler_params=params(1),
        cost_estimate=estimate,
        name="ff_grad_keep",
    )(pick, lhs, rhs, got, small)


def wide_tail(vector):
    high, low = split2(vector)
    return tall(jnp.concatenate([high, low], axis=0))


def attn_split_kernel(pick, kept_ref, got_ref, small_ref, xs_ref, xk_ref, small_out, acc):
    rows = kept_ref.shape[0]
    acc[...] = kept_ref[...].astype(F32) + got_ref[:rows].astype(F32)
    x_index = pick[4]
    shard = rows // 8
    for z in range(4):
        away = pl.multiple_of((2 * z + 1 - x_index) * shard, 8)
        mine = pl.multiple_of((2 * z + x_index) * shard, 8)
        xs_ref[0, z * shard : (z + 1) * shard] = acc[pl.ds(away, shard), :].astype(BF16)
        xk_ref[0, z * shard : (z + 1) * shard] = acc[pl.ds(mine, shard), :].astype(BF16)
    small = rounded(small_ref[...]) + (
        got_ref[rows : rows + 1].astype(F32) + got_ref[rows + 1 : rows + 2].astype(F32)
    )
    small_out[...] = jnp.concatenate([small, jnp.zeros((7, small.shape[1]), F32)], axis=0)
    xs_ref[0, 4 * shard :] = wide_tail(small)


def attn_split(pick, kept, got, small):
    rows, cols = kept.shape
    steps = 1
    column = lambda height: pl.BlockSpec((height, cols // steps), lambda i, pick: (0, i))
    deep = lambda height: pl.BlockSpec((1, height, cols // steps), lambda i, pick: (0, 0, i))
    return pl.pallas_call(
        attn_split_kernel,
        grid_spec=pltpu.PrefetchScalarGridSpec(
            num_scalar_prefetch=1,
            grid=(steps,),
            in_specs=[column(rows), column(rows + TAIL), column(1)],
            out_specs=[deep(rows // 2 + TAIL), deep(rows // 2), column(8)],
            scratch_shapes=[pltpu.VMEM((rows, cols // steps), F32)],
        ),
        out_shape=[
            hbm((1, rows // 2 + TAIL, cols), BF16),
            hbm((1, rows // 2, cols), BF16),
            hbm((8, cols), F32),
        ],
        compiler_params=params(1),
        cost_estimate=cost(kept.size, 6 * kept.size),
        name="attn_split",
    )(pick, kept, got, small)


def tail_sum(ref, at):
    if ref.shape[0] == 2:
        return ref[0, at : at + 8].astype(F32) + ref[1, at : at + 8].astype(F32)
    one = ref[0, at : at + 1].astype(F32) + ref[0, at + 1 : at + 2].astype(F32)
    return jnp.concatenate([one, jnp.zeros((7, one.shape[1]), F32)], axis=0)


def put_tail(ref, at, small):
    if ref.shape[0] == 2:
        for m, term in enumerate(split2(small)):
            ref[m, at:] = tall(term)
    else:
        ref[0, at:] = wide_tail(small[0:1])


def add_x_kernel(tailed, pick, keep_ref, got_ref, small_ref, own, sent, *rest):
    shard = own.shape[1] // 2
    z = pick[5]
    for i, d in enumerate((0, 2, 1, 3)):
        at = pl.multiple_of((z ^ d) * shard, 16)
        ref = own if i < 2 else sent
        ref[:, (i % 2) * shard : (i % 2 + 1) * shard] = (
            keep_ref[:, pl.ds(at, shard), :].astype(F32) + got_ref[:, pl.ds(at, shard), :].astype(F32)
        ).astype(BF16)
    if tailed:
        small = rounded(small_ref[...]) + tail_sum(got_ref, 4 * shard)
        rest[0][...] = small
        put_tail(sent, 2 * shard, small)


def add_x(pick, kept, got, small, tailed):
    mats, rows, cols = kept.shape
    own = hbm((mats, rows // 2, cols), BF16)
    sent = hbm((mats, rows // 2 + (TAIL if tailed else 0), cols), BF16)
    full = lambda s: pl.BlockSpec(s.shape, lambda i, pick: (0,) * len(s.shape))
    extra = [hbm(small.shape, F32)] if tailed else []
    return pl.pallas_call(
        partial(add_x_kernel, tailed),
        grid_spec=pltpu.PrefetchScalarGridSpec(
            num_scalar_prefetch=1,
            grid=(1,),
            in_specs=[full(kept), full(got), full(small)],
            out_specs=[full(s) for s in [own, sent] + extra],
        ),
        out_shape=[own, sent] + extra,
        compiler_params=params(1),
        cost_estimate=cost(kept.size, 6 * kept.size),
        name="add_x",
    )(pick, kept, got, small)


def whole_call(kernel, out_shape, estimate, name, *args):
    full = lambda s: pl.BlockSpec(s.shape, lambda i: (0,) * len(s.shape))
    return pl.pallas_call(
        kernel,
        grid=(1,),
        in_specs=[full(a) for a in args],
        out_specs=[full(s) for s in out_shape],
        out_shape=out_shape,
        compiler_params=params(1),
        cost_estimate=estimate,
        name=name,
    )(*args)


def both(a, b):
    return a.astype(F32) + b.astype(F32)


def add_z_kernel(tailed, keep_ref, got_ref, small_ref, own, sent, *rest):
    shard = own.shape[1]
    own[...] = both(keep_ref[:, :shard], got_ref[:, :shard]).astype(BF16)
    sent[:, :shard] = both(keep_ref[:, shard:], got_ref[:, shard : 2 * shard]).astype(BF16)
    if tailed:
        small = rounded(small_ref[...]) + tail_sum(got_ref, 2 * shard)
        rest[0][...] = small
        put_tail(sent, shard, small)


def add_z(kept, got, small, tailed):
    mats, rows, cols = kept.shape
    shard = rows // 2
    out = [hbm((mats, shard, cols), BF16), hbm((mats, shard + (TAIL if tailed else 0), cols), BF16)]
    if tailed:
        out.append(hbm(small.shape, F32))
    return whole_call(
        partial(add_z_kernel, tailed), out, cost(4e10, 6 * kept.size), "add_z", kept, got, small
    )


def for_head_kernel(own, got, small_ref, out, small_out):
    shard = own.shape[1]
    out[:, :shard] = both(own[...], got[:, :shard]).astype(BF16)
    small = rounded(small_ref[...]) + tail_sum(got, shard)
    small_out[...] = small
    put_tail(out, shard, small)


def for_head(own, got, small):
    out = [hbm(got.shape, BF16), hbm(small.shape, F32)]
    return whole_call(for_head_kernel, out, cost(4e10, 6 * own.size), "for_head", own, got, small)


def ff_last_kernel(pick, own, z_got, got, small_ref, in_out, back_out, *vectors):
    small_out = vectors[-1]
    shard = own.shape[1]
    in_out[...] = both(own[0], z_got[0]) + got[0, :shard].astype(F32)
    back_out[...] = both(own[1], z_got[1]) + got[1, :shard].astype(F32)
    small = rounded(small_ref[...]) + tail_sum(got, shard)
    small_out[...] = small
    dim = small.shape[1] // 2
    for i in range(6):
        vectors[i][...] = small[i // 2 : i // 2 + 1, (i % 2) * dim : (i % 2 + 1) * dim].reshape(dim)
    vectors[6][...] = small_out[pl.ds(3 + pick[0], 1), :].reshape(2 * dim)


def ff_last(pick, own, z_got, got, small):
    _, rows, cols = own.shape
    dim = cols // 2
    full = lambda s: pl.BlockSpec(s.shape, lambda i, pick: (0,) * len(s.shape))
    out_shape = [hbm((rows, cols), F32)] * 2 + [hbm((dim,), F32)] * 6 + [hbm((cols,), F32)]
    return pl.pallas_call(
        ff_last_kernel,
        grid_spec=pltpu.PrefetchScalarGridSpec(
            num_scalar_prefetch=1,
            grid=(1,),
            in_specs=[full(own), full(z_got), full(got), full(small)],
            out_specs=[full(s) for s in out_shape],
            scratch_shapes=[pltpu.VMEM(small.shape, F32)],
        ),
        out_shape=out_shape,
        compiler_params=params(1),
        cost_estimate=cost(10 * got.size, 20 * got.size),
        name="ff_last",
    )(pick, own, z_got, got, small)


def attn_last_kernel(own, got, small_ref, q_out, k_out, v_out, box_out, wo_out, bq_out, bv_out):
    shard = own.shape[1]
    wide = 2 * HEAD
    pairs = q_out.shape[1] // wide
    small = rounded(small_ref[...]) + tail_sum(got, shard)
    for p in range(pairs):
        at = slice(p * wide, (p + 1) * wide)
        for i, ref in enumerate((q_out, k_out, v_out, wo_out, box_out)):
            span = slice((5 * p + i) * wide, (5 * p + i + 1) * wide)
            ref[:, at] = both(own[0, :, span], got[0, :shard, span])
    for i, ref in enumerate((bq_out, bv_out)):
        row = [small[0:1, (5 * p + i) * wide : (5 * p + i + 1) * wide] for p in range(pairs)]
        ref[...] = jnp.concatenate(row, axis=1).reshape(pairs * wide)


def attn_last(own, got, small):
    _, rows, cols = own.shape
    cols = cols // 5
    out = [hbm((rows, cols), F32)] * 5 + [hbm((cols,), F32)] * 2
    return whole_call(attn_last_kernel, out, cost(4 * own.size, 12 * own.size), "attn_last", own, got, small)


def place_grad_kernel(pick, df_ref, a_ref, b_ref, *refs):
    refs[-1][...] = df_ref[...].astype(F32) + (a_ref[...].astype(F32) + b_ref[...].astype(F32))


def place_grad(which, pick, df, mine, got, pages, into=None):
    length, dim = df.shape
    steps = 1
    part = pl.BlockSpec((length // steps, dim), lambda i, pick: (i, 0))
    args = [df, mine, got] + ([] if into is None else [into])
    return pl.pallas_call(
        place_grad_kernel,
        grid_spec=pltpu.PrefetchScalarGridSpec(
            num_scalar_prefetch=1,
            grid=(steps,),
            in_specs=[part] * 3 + ([] if into is None else [pl.BlockSpec(memory_space=pl.ANY)]),
            out_specs=pl.BlockSpec((length // steps, dim), lambda i, pick: (pick[which] * steps + i, 0)),
        ),
        out_shape=hbm((pages * length, dim), F32),
        input_output_aliases={} if into is None else {4: 0},
        compiler_params=params(1),
        cost_estimate=cost(4e10, 10 * df.size),
        name="place_grad",
    )(pick, *args)


def place_output_kernel(pick, a_ref, b_ref, out_ref):
    length = a_ref.shape[0]
    own = pl.multiple_of(pick[0] * length, length)
    other = pl.multiple_of(pick[1] * length, length)
    out_ref[pl.ds(own, length), :] = a_ref[...]
    out_ref[pl.ds(other, length), :] = b_ref[...]


def place_output(pick, mine, got):
    length, dim = mine.shape
    whole = pl.BlockSpec((length, dim), lambda i, pick: (0, 0))
    return pl.pallas_call(
        place_output_kernel,
        grid_spec=pltpu.PrefetchScalarGridSpec(
            num_scalar_prefetch=1,
            grid=(1,),
            in_specs=[whole, pl.BlockSpec((length, dim), lambda i, pick: (1, 0))],
            out_specs=pl.BlockSpec((2 * length, dim), lambda i, pick: (0, 0)),
        ),
        out_shape=hbm((2 * length, dim), BF16),
        compiler_params=params(1),
        cost_estimate=cost(mine.size, 8 * mine.size),
        name="place_output",
    )(pick, mine, got)


def swap_perm(size, flip):
    return [(i, i ^ flip) for i in range(size)]


def encoding_rows(w_box):
    rows, cols = w_box.shape
    quarters = w_box.reshape(4, rows // 4, cols)
    return jnp.concatenate([quarters[i] for i in (0, 2, 1, 3)], axis=0)


def encoding_groups(groups, dim):
    quarter = dim // 4
    place = (0, 2, 1, 3)
    out = []
    for start, count in groups:
        while count:
            size = min(count, quarter - start % quarter)
            out.append((place[start // quarter] * quarter + start % quarter, size))
            start, count = start + size, count - size
    return out


def shards(
    shards_dp,
    tokens,
    boxes,
    resolution,
    w_query,
    bias_query,
    w_key,
    w_value,
    bias_value,
    w_box,
    w_out,
    bias_out,
    norm1_gain,
    norm1_bias,
    w_in,
    bias_in,
    w_back,
    bias_back,
    norm2_gain,
    norm2_bias,
    grad_out,
):
    dim = tokens.shape[1]
    pages = resolution.shape[0]
    length = tokens.shape[0] // pages
    hidden = w_in.shape[1]
    piece = hidden // 4
    here = lax.axis_index("head").astype(jnp.int32)
    spot = lax.axis_index("dp").astype(jnp.int32)
    core, x_index, z_index, corner = spot % 2, (spot // 2) % 2, spot // 4, spot % 4
    corner_z = (z_index % 2) * 2 + core
    pick = jnp.stack([here, 1 - here, core, 1 - core, x_index, z_index, corner, corner // 2, corner_z])
    groups = shard_groups(dim, shards_dp)
    fast = fast_path(dim, shards_dp)

    def over_head(value):
        return lax.ppermute(value, "head", [(0, 1), (1, 0)])

    def over_dp(value, flip):
        return lax.ppermute(value, "dp", swap_perm(shards_dp, flip))

    def after(value, *others):
        return lax.optimization_barrier((value, others))[0]

    in_first = over_head(lax.dynamic_slice_in_dim(w_in, corner * piece, piece, 1))
    back_first = over_head(lax.dynamic_slice_in_dim(w_back, corner_z * piece, piece, 0))
    bias_there = over_head(bias_in)

    quarter = w_box.shape[0] // 4
    freqs = np.exp(np.arange(quarter, dtype=np.float32) * np.float32(-math.log(10000.0) / quarter))
    freqs = jnp.asarray(np.concatenate([freqs, freqs])[None, :])
    box_t = encoding_rows(w_box).T

    def attend(which, tok):
        return attn_fwd(
            which, pick, resolution, tok, boxes, freqs, w_query, w_key, w_value, bias_query, bias_value,
            box_t, w_out, length, groups,
        )

    part_other, *saved_other = attend(1, tokens)
    got = over_head(part_other)
    in_first, back_first, bias_there = after((in_first, back_first, bias_there), part_other)
    in_second, back_second = over_dp(in_first, 2), over_dp(back_first, 4)
    in_near, back_near = over_dp(in_first, 1), over_dp(back_first, 1)
    part_own, *saved_own = attend(0, after(tokens, bias_there))
    in_near, back_near = after((in_near, back_near), part_own)
    in_second, back_second = after((in_second, back_second), in_near, back_near)
    in_pieces = [in_first, in_near, in_second, over_dp(in_second, 1)]
    back_pieces = [back_first, back_near, back_second, over_dp(back_second, 1)]

    out_own, df_own, lhs, rhs, small = feed_forward(
        pick, tokens, part_own, got, grad_out,
        (bias_out, norm1_gain, norm1_bias, bias_back, norm2_gain, norm2_bias),
        bias_in, bias_there, w_in, w_back, in_pieces, back_pieces, groups,
    )
    df_other = over_head(df_own)
    box_groups = encoding_groups(groups, w_box.shape[0])

    def attend_back(df, saved, prev=None, extra=None, pick=pick):
        return attn_bwd(
            pick, df, saved, w_out, box_t, w_query, w_key, w_value, groups, box_groups, prev, extra
        )

    if fast:
        sent_a = ff_grad(pick, lhs, rhs, small, True)
        got_a = over_dp(sent_a, 1)
        sent_b = ff_grad(pick, lhs, after(rhs, sent_a), small, False)
        got_b = over_dp(sent_b, 1)
        xs_a, xk_a, small_1 = ff_grad(pick, lhs, after(rhs, sent_b), small, True, got_a)
        xg_a = over_dp(xs_a, 2)
        got_b = after(got_b, xs_a)
        xs_b, xk_b, small_b = ff_grad(pick, lhs, after(rhs, xs_a), small, False, got_b)
        df_own = after(df_own, xs_b)
    *part_a, inp_own = attend_back(df_own, saved_own)
    if fast:
        xg_a, df_other, xs_b = after((xg_a, df_other, xs_b), inp_own)
        own_a, sent_a, small_2 = add_x(pick, xk_a, after(xg_a, df_other), small_1, True)
        zg_a = over_dp(sent_a, 4)
        inp_send, df_other = after((inp_own, df_other), sent_a)
        xg_b = over_dp(xs_b, 2)
    else:
        inp_send = inp_own
    inp_own_got = over_head(inp_send)

    pick_back = pick if fast else pick.at[2:4].set(jnp.arange(2, dtype=jnp.int32))
    sent, kept, a_small, inp_other = attend_back(df_other, saved_other, part_a, out_own, pick_back)
    inp_other_got = over_head(inp_other)

    if fast:
        xg_b, zg_a, inp_own_got = after((xg_b, zg_a, inp_own_got), inp_other)
        sent, xk_b, zg_a = after((sent, xk_b, zg_a), xg_b, zg_a, inp_own_got)
        sent_got = over_dp(sent, 1)
        own_a, sent_a, small_3 = add_z(own_a, zg_a, small_2, True)
        own_b, sent_b = add_x(pick, after(xk_b, sent_a), xg_b, small_b, False)
        xs, xk, a_small = attn_split(pick, kept, after(sent_got, sent_b), a_small)
        xg = over_dp(xs, 2)
        zg_a, zg_b = over_dp(sent_a, 8), over_dp(sent_b, 4)
        grad_input = place_grad(1, pick, after(df_other, xs), inp_other, inp_own_got, pages)
        own, sent, a_small = add_x(pick, after(xk, grad_input), xg, a_small, True)
        zg = over_dp(sent, 4)
        zg_a, zg_b = after((zg_a, zg_b), sent)
        own_b, sent_b = add_z(own_b, zg_b, small_b, False)
        zg_b = over_dp(sent_b, 8)
        a_sum, small_3 = for_head(own_a, after(zg_a, sent_b), small_3)
        df_own, inp_other_got = after((df_own, inp_other_got), a_sum)
        a_sum = over_head(a_sum)
        grad_input = place_grad(0, pick, df_own, inp_own, inp_other_got, pages, grad_input)
        own, sent, a_small = add_z(after(own, grad_input), zg, a_small, True)
        zg = over_dp(sent, 8)
        grad_in, grad_back, n2g, n2b, bias_back_sum, n1g, n1b, bias_out_sum, bias_in_sum = ff_last(
            pick, after(own_b, sent), zg_b, a_sum, small_3
        )
        output = place_output(pick, after(out_own, grad_in), inp_other_got)
        own = after(own, output)
        grad_q, grad_k, grad_v, grad_box, grad_wo, bq_sum, bv_sum = attn_last(own, zg, a_small)
        grad_back, grad_wo = grad_back.T, grad_wo.T
    else:
        scatter = lambda value, axis: lax.psum_scatter(
            value.astype(F32), "dp", scatter_dimension=axis, tiled=True
        )
        cores = [pick.at[3].set(c) for c in (0, 1)]
        halves = [
            scatter(
                jnp.concatenate([ff_grad(p, lhs, rhs, small, remote)[:, : dim // 2] for p in cores], axis=1), 1
            )
            for remote in (True, False)
        ]
        total = halves[1] + over_head(halves[0])
        grad_in, grad_back = total[0], total[1].T
        total = scatter(jnp.concatenate([kept, sent[: dim // 2]], axis=0), 0)
        total = total.reshape(total.shape[0], -1, 5, 2 * HEAD).transpose(2, 0, 1, 3)
        grad_q, grad_k, grad_v, grad_wo, grad_box = total.reshape(5, total.shape[1], -1)
        grad_wo = grad_wo.T
        small = lax.psum(small, ("dp", "head"))
        n2g, n2b, bias_back_sum, n1g, n1b, bias_out_sum = small[:3].reshape(6, dim)
        bias_in_sum = lax.dynamic_index_in_dim(small, 3 + here, 0, keepdims=False)
        bq_sum, bv_sum = lax.psum(a_small, "dp").reshape(-1, 5, 2 * HEAD)[:, :2].transpose(1, 0, 2).reshape(2, -1)
        output = place_output(pick, out_own, inp_other_got)
        grad_input = place_grad(1, pick, df_other, inp_other, inp_own_got, pages)
        grad_input = place_grad(0, pick, df_own, inp_own, inp_other_got, pages, grad_input)
    return (
        output,
        grad_input,
        grad_q,
        bq_sum,
        grad_k,
        grad_v,
        bv_sum,
        grad_box,
        grad_wo,
        bias_out_sum,
        n1g,
        n1b,
        grad_in,
        bias_in_sum,
        grad_back,
        bias_back_sum,
        n2g,
        n2b,
    )


def solution(mesh):
    placed = (
        P("dp", None),
        P(None, "dp"),
        P("dp"),
        P(None, "head"),
        P("head"),
        P(None, "head"),
        P(None, "head"),
        P("head"),
        P(None, "head"),
        P("head", None),
        P(),
        P(),
        P(),
        P(None, "head"),
        P("head"),
        P("head", None),
        P(),
        P(),
        P(),
        P("dp", None),
    )
    return jax.shard_map(
        partial(shards, mesh.shape["dp"]),
        mesh=mesh,
        in_specs=placed,
        out_specs=(
            P("dp", None),
            P("dp", None),
            P("dp", "head"),
            P("head"),
            P("dp", "head"),
            P("dp", "head"),
            P("head"),
            P("dp", "head"),
            P("head", "dp"),
            P(),
            P(),
            P(),
            P("dp", "head"),
            P("head"),
            P("head", "dp"),
            P(),
            P(),
            P(),
        ),
        check_vma=False,
    )
```
